32 devices in a mesh: groups: 2 (over x), pen: 16 (over z, y, core).
Axes of the slice: x: 2, y: 2, z: 4, core: 2. Of those that a mesh axis runs over, the one named last changes fastest.
Arguments:
- point_feat: bfloat16 [64, 65536], P(None, ('groups', 'pen')), parts along dimension 1, may hold values from -6 to 6
- pair_kernel: bfloat16 [2048, 128, 128], P(('groups', 'pen')), parts along dimension 0, may hold values from -0.5 to 0.5
- pair_owner: int32 [2048, 1], P(('groups', 'pen')), parts along dimension 0, may hold values from 0 to 15; in each aligned block of 64 rows (0 to 63, 64 to 127, ...) at most 8 rows name the same one
- pair_block: int32 [2048], P(('groups', 'pen')), parts along dimension 0, may hold values from 0 to 255
- spec_weight: bfloat16 [2, 256, 16, 64, 128], P(None, 'pen'), may hold values from -3 to 3
- mlp_up: bfloat16 [2, 256, 64], replicated, may hold values from -0.75 to 0.75
- mlp_down: bfloat16 [2, 64, 256], replicated, may hold values from -0.375 to 0.375
Outputs:
- point_out: float32 [64, 65536], P(None, ('groups', 'pen')), parts along dimension 1
The draws below stay inside these ranges and needn't reach their ends.
There are 2 independent parts, one for each index of `groups`. The reference program is written for one: setup_inputs(seed, part) draws one part's arguments, and reference() takes and returns one part's arrays. A program takes and returns all parts, laid end to end along the dimension named above; an argument that names none is the same for every part. Nothing has to cross between parts.
Inputs may be any that keep to these rules, and one draw needn't show every extreme that they name: `pair_owner`: among the pairs of one device, no device is named more than 8 times.
All inputs are finite; a program needn't handle non-finite values.
Results may differ from the reference program's by a relative error of at most 0.0055.
Values may be sent and summed in bfloat16 or wider, within the bound.
No kernel may reach another device: no remote copies, remote signals or barrier semaphores. Data moves between devices by JAX's collectives and lax.ppermute only.
A program may use at most 128 MiB of HBM per device.

```python
import math
import jax
import jax.numpy as jnp
import numpy as np
from jax import lax

C = 64
HID = 256
NX = 128
NY = 64
NZ = 64
MX = 16
MY = 16
MZ = 16
LAYERS = 2
BS = 128
NBR = 4
BLK_DEV = 16
CAP = 8
PAIRS = 1024
NPTS = 32768
GB_DEV = 256
N_PEN = 16


def set_ends(values, rng, least, top_value):
    extent = values.shape
    place = [jax.random.randint(jax.random.fold_in(rng, axis), (), 0, extent[axis]) for axis in range(len(extent))]
    values = values.at[tuple(place)].set(least)
    longest = extent.index(max(extent))
    place[longest] = (place[longest] + 1) % extent[longest]
    return values.at[tuple(place)].set(top_value)


def block_levels(stream_key, shape, pieces, low, top_value):
    def one(dim, shards_of):
        steps = jax.random.uniform(jax.random.fold_in(jax.random.fold_in(stream_key, 6), dim), (shards_of,), jnp.float32, low / len(pieces), top_value / len(pieces))
        return jnp.repeat(jnp.exp(steps), shape[dim] // shards_of).reshape((-1,) + (1,) * (len(shape) - dim - 1))

    factor_of = one(*pieces[0])
    for cut in pieces[1:]:
        factor_of = factor_of * one(*cut)
    return factor_of


def assign_block(stream_key, own, number, rows, amount, top, most, lean):
    ranking = jax.random.permutation(stream_key, amount)
    heavy_load, common = shares(amount, rows * top, most, lean, True), shares(amount, rows * top, most, lean, False)
    places = jnp.arange(amount)

    def named(lengths, turn):
        used = int((lengths > 0).sum())
        fixed = max(1, used // 4)
        passed = fixed + (places - fixed + turn * (used - fixed)) % max(1, amount - fixed)
        return jnp.zeros((amount,), jnp.int32).at[ranking[jnp.where(places < fixed, places, passed)]].set(jnp.asarray(lengths, jnp.int32))

    lengths = jnp.where(number % 4 == 0, named(heavy_load, number // 4), named(common, number - number // 4 - 1))
    mixed = jax.random.permutation(jax.random.fold_in(own, 3), amount)
    source_of, receiver = mixed[0:amount // 2 * 2:2], mixed[1:amount // 2 * 2:2]
    room = jnp.minimum(lengths[source_of] - 1, most - lengths[receiver]) // 2
    room = jnp.where((source_of == ranking[0]) | (receiver == ranking[0]) | (lengths[receiver] == 0), 0, jnp.maximum(room, 0))
    passed = jax.random.randint(jax.random.fold_in(own, 4), (amount // 2,), 0, 1 << 20) % (room + 1)
    lengths = lengths.at[source_of].add(-passed).at[receiver].add(passed)
    members = jnp.searchsorted(jnp.cumsum(lengths), jnp.arange(rows * top), side="right").astype(jnp.int32)
    table = members.reshape(top, rows).T
    table = table[jax.random.permutation(jax.random.fold_in(own, 1), rows)]
    turn = jax.random.randint(jax.random.fold_in(own, 2), (rows, 1), 0, top)
    return jnp.take_along_axis(table, (jnp.arange(top)[None, :] + turn) % top, axis=1)


def shares(number_of, total, limit, skew, full):
    portions = [(1 << 20) // math.isqrt(grade ** skew) + 1 for grade in range(1, number_of + 1)]
    largest = limit if full else min(limit, max(-(-total // number_of), total * portions[0] // sum(portions)))
    least = 1 if total - largest >= number_of - 1 else 0
    counts, spare = [largest] + [least] * (number_of - 1), total - largest - least * (number_of - 1)
    while spare > 0:
        movable = [i for i in range(1, number_of) if counts[i] < largest] or [i for i in range(1, number_of) if counts[i] < limit]
        mass, remaining = sum([portions[i] for i in movable]), spare
        for i in movable:
            addition = min(limit - counts[i], max(1, remaining * portions[i] // mass), spare)
            counts[i] = counts[i] + addition
            spare = spare - addition
    return np.array(counts)


def noise(key, dims, scale, most, shards=(), held_as=jnp.bfloat16):
    factor_of = block_levels(key, dims, shards, -0.22, 0.18) if shards else 1.0
    drawn = jax.random.normal(key, dims, jnp.float32) * scale * factor_of
    return jnp.minimum(jnp.maximum(drawn, -most), most).astype(held_as)


def setup_inputs(seed: int = 0, part: int = 0) -> dict:
    arg_keys = jax.random.split(jax.random.key(seed), 8)
    own_keys = jax.random.split(jax.random.fold_in(arg_keys[7], part), 8)
    point_feat = noise(own_keys[0], (C, NPTS), 1.0, 6.0, ((1, 16),))
    pair_kernel = noise(own_keys[1], (PAIRS, BS, BS), BS ** -0.5, 0.5, ((0, 16),))
    pair_owner_keys = jax.random.split(jax.random.fold_in(own_keys[2], 1), PAIRS // (BLK_DEV * NBR))
    pair_owner_turns = jax.random.permutation(jax.random.fold_in(own_keys[2], 3), PAIRS // (BLK_DEV * NBR))
    pair_owner = jax.vmap(lambda own, number: assign_block(jax.random.fold_in(own_keys[2], 2), own, number, BLK_DEV * NBR, N_PEN, 1, CAP, 2))(pair_owner_keys, pair_owner_turns).reshape((PAIRS, 1))
    pair_block = set_ends(jax.random.randint(own_keys[3], (PAIRS,), 0, GB_DEV), jax.random.fold_in(own_keys[3], 1), 0, GB_DEV - 1).astype(jnp.int32)
    spec_weight = noise(arg_keys[4], (LAYERS, MY * MZ, MX, C, 2 * C), (C // 16) ** -0.5, 3.0, ((1, 16),))
    mlp_up = noise(arg_keys[5], (LAYERS, HID, C), C ** -0.5, 0.75)
    mlp_down = noise(arg_keys[6], (LAYERS, C, HID), HID ** -0.5, 0.375)
    return dict(point_feat=point_feat, pair_kernel=pair_kernel, pair_owner=pair_owner, pair_block=pair_block, spec_weight=spec_weight, mlp_up=mlp_up, mlp_down=mlp_down)


HIGHEST = lax.Precision.HIGHEST


def yz_tables():
    mode_index = jnp.arange(MY * MZ, dtype=jnp.int32)
    wave_y = mode_index // MZ - MY // 2
    wave_z = mode_index % MZ
    cell_index = jnp.arange(NY * NZ, dtype=jnp.int32)
    row_y = cell_index // NZ
    row_z = cell_index % NZ
    phase_turns = jnp.mod(row_y[:, None] * wave_y[None, :], NY).astype(jnp.float32) / NY + jnp.mod(row_z[:, None] * wave_z[None, :], NZ).astype(jnp.float32) / NZ
    angle = 2.0 * math.pi * phase_turns
    forward_table = jnp.stack([jnp.cos(angle), -jnp.sin(angle)], axis=2).reshape(NY * NZ, 2 * MY * MZ)
    scaling = jnp.where(wave_z == 0, 1.0, 2.0).astype(jnp.float32) / (NX * NY * NZ)
    inverse_table = forward_table * jnp.repeat(scaling, 2)[None, :]
    return forward_table, inverse_table


def along_tables(positions):
    wave_number = jnp.arange(MX, dtype=jnp.int32) - MX // 2
    angle = 2.0 * math.pi * jnp.mod(wave_number[:, None] * positions[None, :], NX).astype(jnp.float32) / NX
    return jnp.cos(angle), jnp.sin(angle)


def spectral_part(grid_field, weights_now, forward_table, inverse_table):
    modes_all = MY * MZ
    planar = jnp.dot(grid_field.reshape(C * NX, NY * NZ), forward_table, precision=HIGHEST).reshape(C, NX, modes_all, 2)
    cosine_table, sine_table = along_tables(jnp.arange(NX, dtype=jnp.int32))
    part_real = planar[..., 0]
    part_imag = planar[..., 1]
    modes_real = jnp.einsum("jx,cxm->mjc", cosine_table, part_real, precision=HIGHEST) + jnp.einsum("jx,cxm->mjc", sine_table, part_imag, precision=HIGHEST)
    modes_imag = jnp.einsum("jx,cxm->mjc", cosine_table, part_imag, precision=HIGHEST) - jnp.einsum("jx,cxm->mjc", sine_table, part_real, precision=HIGHEST)
    weight_real = weights_now[..., :C].astype(jnp.float32)
    weight_imag = weights_now[..., C:].astype(jnp.float32)
    mixed_real = jnp.einsum("mjc,mjco->mjo", modes_real, weight_real, precision=HIGHEST) - jnp.einsum("mjc,mjco->mjo", modes_imag, weight_imag, precision=HIGHEST)
    mixed_imag = jnp.einsum("mjc,mjco->mjo", modes_real, weight_imag, precision=HIGHEST) + jnp.einsum("mjc,mjco->mjo", modes_imag, weight_real, precision=HIGHEST)
    back_real = jnp.einsum("jx,mjo->oxm", cosine_table, mixed_real, precision=HIGHEST) - jnp.einsum("jx,mjo->oxm", sine_table, mixed_imag, precision=HIGHEST)
    back_imag = jnp.einsum("jx,mjo->oxm", sine_table, mixed_real, precision=HIGHEST) + jnp.einsum("jx,mjo->oxm", cosine_table, mixed_imag, precision=HIGHEST)
    joined = jnp.stack([back_real, back_imag], axis=3).reshape(C * NX, 2 * modes_all)
    return jnp.dot(joined, inverse_table.T, precision=HIGHEST).reshape(C, NX, NY * NZ)


def channel_mlp(summed, weight_up, weight_down):
    def one_plane(values):
        rounded = values.astype(jnp.bfloat16)
        hidden = jnp.dot(weight_up, rounded, preferred_element_type=jnp.float32)
        active = jax.nn.gelu(hidden, approximate=True).astype(jnp.bfloat16)
        return values + jnp.dot(weight_down, active, preferred_element_type=jnp.float32)

    planes_first = jnp.moveaxis(summed, 1, 0)
    return jnp.moveaxis(lax.map(one_plane, planes_first), 0, 1)


def reference(point_feat, pair_kernel, pair_owner, pair_block, spec_weight, mlp_up, mlp_down):
    grid_total = NX * NY * NZ // BS
    target = pair_owner[:, 0] * GB_DEV + pair_block
    feature_blocks = point_feat.reshape(C, PAIRS // NBR, BS).transpose(1, 0, 2)
    pair_features = jnp.repeat(feature_blocks, NBR, axis=0)
    kernels_wide = pair_kernel.astype(jnp.float32)
    contrib = jnp.einsum("pci,pij->pcj", pair_features.astype(jnp.float32), kernels_wide)
    grid_blocks = jax.ops.segment_sum(contrib, target, num_segments=grid_total)
    grid_field = grid_blocks.transpose(1, 0, 2).reshape(C, NX, NY * NZ)
    forward_table, inverse_table = yz_tables()
    for number in range(LAYERS):
        spectral = spectral_part(grid_field, spec_weight[number], forward_table, inverse_table)
        summed = grid_field + spectral
        grid_field = channel_mlp(summed, mlp_up[number], mlp_down[number])
    grid_out = grid_field.astype(jnp.bfloat16).reshape(C, grid_total, BS).transpose(1, 0, 2)
    fetched = grid_out[target]
    back = jnp.einsum("pcj,pij->pci", fetched.astype(jnp.float32), kernels_wide)
    summed_back = back.reshape(PAIRS // NBR, NBR, C, BS).sum(axis=1)
    return summed_back.transpose(1, 0, 2).reshape(C, NPTS)
```

```python
import functools
import math

import jax
import jax.numpy as jnp
import numpy as np
from jax import lax
from jax.experimental import pallas as pl
from jax.experimental.pallas import tpu as pltpu
from jax.sharding import PartitionSpec as P

NX = 128
NY = 64
NZ = 64
MX = 16
MY = 16
MZ = 16
LAYERS = 2
NBR = 4
GELU_K = math.sqrt(2.0 / math.pi)
SCALE = 1.66575

F32 = jnp.float32
BF16 = jnp.bfloat16


def vmem_spec():
    return pl.BlockSpec(memory_space=pltpu.VMEM)


def cost(flops, size, transcendentals=0):
    return pl.CostEstimate(
        flops=int(flops), bytes_accessed=int(size), transcendentals=int(transcendentals)
    )


def dot(left, right):
    return jnp.dot(left, right, preferred_element_type=F32)


def column_waves(devices, modes_here):
    column = np.arange(devices * 2 * MX)
    wave_y = (column // (2 * MX) * modes_here) // MZ - MY // 2
    return wave_y, column // MX % 2, column % MX - MX // 2


def line_tables(devices, modes_here):
    wave_y, part, wave_x = column_waves(devices, modes_here)
    x_angle = 2.0 * np.pi / NX * (np.arange(NX)[:, None] * wave_x % NX)
    y_angle = 2.0 * np.pi / NY * (np.arange(NY)[:, None] * wave_y % NY)
    x_cos, x_sin = SCALE * np.cos(x_angle), SCALE * np.sin(x_angle)
    first = np.where(part == 0, x_cos, -x_sin)
    second = np.where(part == 0, -x_sin, -x_cos)
    return [
        jnp.asarray(each.astype(np.float32))
        for each in (first, second, np.cos(y_angle), np.sin(y_angle))
    ]


def split(values):
    high = values.astype(BF16)
    return high, (values - high.astype(F32)).astype(BF16)


def depth_tables(devices, modes_here):
    local = NZ // devices
    wave_z = np.arange(MZ).reshape(MZ // modes_here, modes_here)
    z_of = np.arange(devices)[None, :] * local + np.arange(local)[:, None]
    angle = 2.0 * np.pi / NZ * (z_of[None, :, :, None] * wave_z[:, None, None, :] % NZ)
    cosine, sine = np.cos(angle), np.sin(angle)
    to_real = np.stack([cosine, sine], axis=-1)
    to_imag = np.stack([-sine, cosine], axis=-1)
    forward = np.stack([to_real, to_imag], axis=-2) / SCALE
    forward = forward.transpose(0, 1, 3, 4, 2, 5).reshape(
        -1, local * modes_here * 2, devices * 2
    )
    scale = np.where(wave_z == 0, 1.0, 2.0)[:, None, None, :] / (NX * NY * NZ * SCALE)
    cosine, sine = cosine * scale, sine * scale
    low = np.stack(
        [np.stack([cosine, -sine], axis=-1), np.stack([sine, cosine], axis=-1)], axis=3
    ).reshape(-1, local * devices * 2, modes_here * 2)
    high = np.stack(
        [np.stack([-sine, -cosine], axis=-1), np.stack([cosine, -sine], axis=-1)], axis=3
    ).reshape(-1, local * devices * 2, modes_here * 2)
    inverse = np.concatenate([low, high], axis=2)
    which = lax.axis_index("pen") * modes_here % MZ // modes_here
    chosen = []
    for table in (forward, inverse):
        table = jnp.asarray(table.astype(np.float32))
        chosen.append(table[0] if table.shape[0] == 1 else table[which])
    forward, inverse = chosen
    return jnp.concatenate(split(forward), axis=1), jnp.concatenate(split(inverse), axis=1)


def table_kernel(first_ref, second_ref, cos_ref, sin_ref, table_ref, flipped_ref):
    pieces = []
    for line in range(first_ref.shape[0]):
        piece = (
            first_ref[line : line + 1, :] * cos_ref[...]
            + second_ref[line : line + 1, :] * sin_ref[...]
        )
        pieces.append(piece.astype(BF16))
    whole = jnp.concatenate(pieces, axis=0)
    table_ref[...] = whole
    flipped_ref[...] = whole.T


def grid_tables(devices, modes_here):
    first, second, y_cos, y_sin = line_tables(devices, modes_here)
    columns = first.shape[1]
    lines = 8
    rows = lines * NY
    const = lambda i: (0, 0)
    return pl.pallas_call(
        table_kernel,
        out_shape=(
            jax.ShapeDtypeStruct((NX * NY, columns), BF16),
            jax.ShapeDtypeStruct((columns, NX * NY), BF16),
        ),
        grid=(NX // lines,),
        in_specs=[
            pl.BlockSpec((lines, columns), lambda i: (i, 0)),
            pl.BlockSpec((lines, columns), lambda i: (i, 0)),
            pl.BlockSpec((NY, columns), const),
            pl.BlockSpec((NY, columns), const),
        ],
        out_specs=(
            pl.BlockSpec((rows, columns), lambda i: (i, 0)),
            pl.BlockSpec((columns, rows), lambda i: (0, i)),
        ),
        cost_estimate=cost(4 * NX * NY * columns, 4 * NX * NY * columns),
        name="tables",
    )(first, second, y_cos, y_sin)


def encode_kernel(feature_ref, weight_ref, spot_ref, out_ref, wide_ref, turned_ref):
    devices = out_ref.shape[0]
    pairs, block = weight_ref.shape[0], weight_ref.shape[1]
    lines = block // NZ
    local = NZ // devices
    tiles = local // 2
    rows = tiles * pairs * lines
    lane = lax.broadcasted_iota(jnp.int32, (lines * devices, 128), 1)

    def one(point, carry):
        features = feature_ref[:, pl.ds(pl.multiple_of(point * block, block), block)]
        features = jnp.concatenate([features, features], axis=0)
        for near in range(NBR):
            pair = point * NBR + near
            turned_ref[near] = lax.dot_general(
                weight_ref[pair], features, (((0,), (1,)), ((), ())), preferred_element_type=F32
            )
            for tile in range(tiles):
                even = turned_ref[near, pl.ds(2 * tile, lines * devices, stride=local), :]
                odd = turned_ref[near, pl.ds(2 * tile + 1, lines * devices, stride=local), :]
                both = jnp.where(lane < 64, even, odd)
                for line in range(lines):
                    wide_ref[
                        pl.ds(tile * pairs * lines + pair * lines + line, devices, stride=rows), :
                    ] = both[line * devices : (line + 1) * devices, :]
        return carry

    lax.fori_loop(0, pairs // NBR, one, 0)
    for device in range(devices):
        out_ref[device, 0:rows, :] = wide_ref[device * rows : (device + 1) * rows, :].astype(BF16)
        out_ref[device, rows : rows + 8, :] = spot_ref[...].astype(BF16)


def encode(features, weights, spots, devices):
    pairs, block = weights.shape[0], weights.shape[1]
    rows = NZ // devices // 2 * pairs * (block // NZ)
    return pl.pallas_call(
        encode_kernel,
        out_shape=jax.ShapeDtypeStruct((devices, rows + 8, 128), BF16),
        in_specs=[vmem_spec()] * 3,
        out_specs=vmem_spec(),
        scratch_shapes=[
            pltpu.VMEM((devices * rows, 128), F32),
            pltpu.VMEM((NBR, block, 128), F32),
        ],
        cost_estimate=cost(4 * pairs * block * block * 64, pairs * block * block * 2),
        name="encode",
    )(features, weights, spots)


def decode_kernel(got_ref, weight_ref, out_ref, wide_ref, turned_ref):
    devices, rows, _ = got_ref.shape
    pairs, block = weight_ref.shape[0], weight_ref.shape[1]
    lines = block // NZ
    local = NZ // devices
    tiles = local // 2
    lane = lax.broadcasted_iota(jnp.int32, (block, 128), 1)
    row = lax.broadcasted_iota(jnp.int32, (block, 128), 0)
    keep = lane // 64 == row % 2
    for device in range(devices):
        wide_ref[device * rows : (device + 1) * rows, :] = got_ref[device].astype(F32)

    def one(point, carry):
        total = None
        for near in range(NBR):
            pair = point * NBR + near
            for tile in range(tiles):
                for line in range(lines):
                    values = wide_ref[
                        pl.ds(tile * pairs * lines + pair * lines + line, devices, stride=rows), :
                    ]
                    for side in range(2):
                        turned_ref[
                            near, pl.ds(line * NZ + tile * 2 + side, devices, stride=local), :
                        ] = values
            left = jnp.where(keep, turned_ref[near], 0.0).astype(BF16)
            part = lax.dot_general(
                left, weight_ref[pair], (((0,), (1,)), ((), ())), preferred_element_type=F32
            )
            total = part if total is None else total + part
        out_ref[:, pl.ds(pl.multiple_of(point * block, block), block)] = (
            total[0:64, :] + total[64:128, :]
        )
        return carry

    lax.fori_loop(0, pairs // NBR, one, 0)


def decode(got, weights, channels):
    devices, rows, _ = got.shape
    pairs, block = weights.shape[0], weights.shape[1]
    return pl.pallas_call(
        decode_kernel,
        out_shape=jax.ShapeDtypeStruct((channels, pairs // NBR * block), F32),
        in_specs=[vmem_spec()] * 2,
        out_specs=vmem_spec(),
        scratch_shapes=[
            pltpu.VMEM((devices * rows, 128), F32),
            pltpu.VMEM((NBR, block, 128), F32),
        ],
        cost_estimate=cost(4 * pairs * block * block * 64, pairs * block * block * 2),
        name="decode",
    )(got, weights)


def pair_spectrum_kernel(modes_here, got_ref, out_ref, phase_ref):
    devices = got_ref.shape[0]
    rows = got_ref.shape[1] - 8
    tiles = out_ref.shape[1] // 128
    lanes = rows // tiles
    wave_x = lax.broadcasted_iota(jnp.int32, (MX, lanes), 0) - MX // 2
    wave_y = lax.broadcasted_iota(jnp.int32, (MY, lanes), 0) - MY // 2
    for source in range(devices):
        spot = got_ref[source, rows : rows + 8, :].astype(F32)
        x_at = spot[0:1, :].astype(jnp.int32)
        y_at = spot[1:2, :].astype(jnp.int32)
        x_angle = (2.0 * math.pi / NX) * ((wave_x * x_at) & (NX - 1)).astype(F32)
        y_angle = (2.0 * math.pi / NY) * ((wave_y * y_at) & (NY - 1)).astype(F32)
        x_cos, x_sin = SCALE * jnp.cos(x_angle), SCALE * jnp.sin(x_angle)
        y_cos, y_sin = jnp.cos(y_angle), jnp.sin(y_angle)
        place = slice(source * lanes, (source + 1) * lanes)
        for device in range(devices):
            row = (device * modes_here) // MZ
            cos_now, sin_now = y_cos[row : row + 1, :], y_sin[row : row + 1, :]
            base = device * 2 * MX
            phase_ref[base : base + MX, place] = (x_cos * cos_now - x_sin * sin_now).astype(BF16)
            phase_ref[base + MX : base + 2 * MX, place] = (
                -x_sin * cos_now - x_cos * sin_now
            ).astype(BF16)
    values = jnp.concatenate(
        [
            jnp.concatenate(
                [
                    got_ref[source, tile * lanes : (tile + 1) * lanes, :]
                    for source in range(devices)
                ],
                axis=0,
            )
            for tile in range(tiles)
        ],
        axis=1,
    )
    out_ref[...] = dot(phase_ref[...], values).astype(BF16)


def pair_spectrum(got, modes_here, lanes):
    devices, rows, _ = got.shape
    count = devices * (rows - 8) // (lanes // 128)
    columns = devices * 2 * MX
    return pl.pallas_call(
        functools.partial(pair_spectrum_kernel, modes_here),
        out_shape=(
            jax.ShapeDtypeStruct((columns, lanes), BF16),
            jax.ShapeDtypeStruct((columns, count), BF16),
        ),
        in_specs=[vmem_spec()],
        out_specs=(vmem_spec(), vmem_spec()),
        cost_estimate=cost(2 * columns * count * lanes, got.size * 2 + columns * count * 2),
        name="pair_spectrum",
    )(got)


def mix_kernel(
    devices, number, got_ref, forward_ref, inverse_ref, all_ref, out_ref, wide_ref, back_ref,
    weight_ref, sem_ref
):
    modes_here, _, channels, _ = weight_ref.shape
    pieces_at = [slice(first, first + 4) for first in range(0, MX, 4)]
    copies = [
        pltpu.make_async_copy(
            all_ref.at[number, :, place], weight_ref.at[:, place], sem_ref.at[index]
        )
        for index, place in enumerate(pieces_at)
    ]
    for copy in copies:
        copy.start()
    local = got_ref.shape[1] // channels
    tiles = got_ref.shape[1] // 128
    group = 8
    for tile in range(tiles):
        wide_ref[tile] = got_ref[:, tile * 128 : (tile + 1) * 128].astype(F32)
    lane = lax.broadcasted_iota(jnp.int32, (2 * modes_here, 128), 1)
    row = lax.broadcasted_iota(jnp.int32, (2 * group, 128), 0)
    lane_small = lax.broadcasted_iota(jnp.int32, (2 * group, 128), 1)
    lane_back = lax.broadcasted_iota(jnp.int32, (2 * devices, 128), 1)
    forward = forward_ref[...]
    inverse = inverse_ref[...]
    spread = []
    for wave in range(MX):
        planes = jnp.concatenate(
            [wide_ref[tile, pl.ds(wave, 2 * devices, stride=MX), :] for tile in range(tiles)],
            axis=1,
        ).astype(BF16)
        turned = dot(forward, jnp.concatenate([planes, planes], axis=0))
        total = None
        for tile in range(tiles):
            part = slice(tile * 128, (tile + 1) * 128)
            size = 2 * modes_here
            even = turned[2 * tile * size : (2 * tile + 1) * size, part]
            odd = turned[(2 * tile + 1) * size : (2 * tile + 2) * size, part]
            both = even + pltpu.roll(odd, 64, 1)
            total = both if total is None else total + both
        spread.append(jnp.where(lane < 64, total, pltpu.roll(total, 64, 1)))
    mixed = []
    for wave in range(MX):
        pieces = []
        if wave % 4 == 0:
            copies[wave // 4].wait()
        for first in range(0, modes_here, group):
            now = spread[wave][2 * first : 2 * (first + group), :]
            left = jnp.concatenate(
                [
                    jnp.where(row // 2 == 2 * step + lane_small // 64, now, 0.0)
                    for step in range(group // 2)
                ],
                axis=1,
            )
            left = jnp.concatenate(split(left), axis=0)
            right = weight_ref[first : first + group, wave, :, :].reshape(
                group * channels, 2 * channels
            )
            both = dot(left, right)
            pieces.append(both[0 : 2 * group] + both[2 * group :])
        mixed.append(pieces[0] if len(pieces) == 1 else jnp.concatenate(pieces, axis=0))
    for wave in range(MX):
        stacked = jnp.concatenate([mixed[wave], pltpu.roll(mixed[wave], 64, 1)], axis=0)
        upper, lower = split(stacked)
        count = upper.shape[0]
        planes = dot(inverse, jnp.concatenate([upper, upper], axis=0)) + dot(
            inverse[:, 0:count], lower
        )
        size = 2 * devices
        for tile in range(tiles):
            even = planes[2 * tile * size : (2 * tile + 1) * size, :]
            odd = planes[(2 * tile + 1) * size : (2 * tile + 2) * size, :]
            back_ref[tile, pl.ds(wave, size, stride=MX), :] = jnp.where(
                lane_back < 64, even, pltpu.roll(odd, 64, 1)
            )
    for tile in range(tiles):
        out_ref[:, tile * 128 : (tile + 1) * 128] = back_ref[tile].astype(BF16)


def mix(got, forward, inverse, weights, number, devices):
    rows, lanes = got.shape
    return pl.pallas_call(
        functools.partial(mix_kernel, devices, number),
        out_shape=jax.ShapeDtypeStruct((rows, lanes), BF16),
        in_specs=[vmem_spec()] * 3 + [pl.BlockSpec(memory_space=pl.ANY)],
        out_specs=vmem_spec(),
        scratch_shapes=[pltpu.VMEM((lanes // 128, rows, 128), F32)] * 2
        + [pltpu.VMEM(weights.shape[1:], BF16), pltpu.SemaphoreType.DMA((4,))],
        cost_estimate=cost(6e8, weights.size + rows * lanes * 4),
        name="mix",
    )(got, forward, inverse, weights)


def spread_weights(up_ref, down_ref, up_wide_ref, down_wide_ref):
    hidden, channels = up_ref.shape[1:]
    up = up_ref[0].T
    down = (down_ref[0].astype(F32) * 0.5).astype(BF16).T
    up_wide_ref[...] = jnp.zeros_like(up_wide_ref)
    down_wide_ref[...] = jnp.zeros_like(down_wide_ref)
    for cell in range(2):
        here = slice(cell * channels, (cell + 1) * channels)
        there = slice(cell * hidden, (cell + 1) * hidden)
        up_wide_ref[here, there] = up
        down_wide_ref[there, here] = down


def mlp(summed, up_ref, down_ref):
    rounded = summed.astype(BF16)
    total = summed
    width = 256
    for first in range(0, up_ref.shape[1], width):
        hidden = dot(rounded, up_ref[:, first : first + width])
        slope = hidden * (GELU_K + (GELU_K * 0.044715) * (hidden * hidden))
        active = (hidden * jnp.tanh(slope) + hidden).astype(BF16)
        total = total + dot(active, down_ref[first : first + width, :])
    return total


def scatter_kernel(spot_ref, got_ref, out_ref, wide_ref):
    devices, rows, _ = got_ref.shape
    rows = rows - 8
    pairs = spot_ref.shape[0] // devices
    size = rows // pairs
    lines = size // TILES(out_ref)
    tiles = TILES(out_ref)
    out_ref[...] = jnp.zeros_like(out_ref)
    for source in range(devices):
        for tile in range(tiles):
            wide_ref[pl.ds(source * rows + tile, pairs * lines, stride=tiles), :] = got_ref[
                source, tile * pairs * lines : (tile + 1) * pairs * lines, :
            ].astype(F32)

    @pl.loop(0, devices)
    def _(source):
        for pair in range(pairs):
            base = pl.multiple_of(spot_ref[source * pairs + pair], size)
            here = pl.multiple_of(source * rows + pair * size, size)
            out_ref[pl.ds(base, size), :] = (
                out_ref[pl.ds(base, size), :] + wide_ref[pl.ds(here, size), :]
            )


def TILES(ref):
    return ref.shape[0] // (NX * NY)


def scatter(spots, got, tiles):
    devices, rows, _ = got.shape
    return pl.pallas_call(
        scatter_kernel,
        out_shape=jax.ShapeDtypeStruct((NX * NY * tiles, 128), F32),
        grid_spec=pltpu.PrefetchScalarGridSpec(
            num_scalar_prefetch=1,
            grid=(1,),
            in_specs=[pl.BlockSpec(got.shape, lambda i, s: (0, 0, 0))],
            out_specs=pl.BlockSpec((NX * NY * tiles, 128), lambda i, s: (0, 0)),
            scratch_shapes=[pltpu.VMEM((devices * (rows - 8), 128), F32)],
        ),
        compiler_params=pltpu.CompilerParams(vmem_limit_bytes=48 * 1024 * 1024),
        cost_estimate=cost(1e6, NX * NY * tiles * 128 * 16),
        name="scatter",
    )(spots, got)


def gather_kernel(size, devices, spot_ref, grid_ref, out_ref):
    pairs = spot_ref.shape[0] // devices

    @pl.loop(0, devices)
    def _(source):
        for pair in range(pairs):
            base = pl.multiple_of(spot_ref[source * pairs + pair], size)
            here = pl.multiple_of(source * (pairs * size) + pair * size, size)
            out_ref[pl.ds(here, size), :] = grid_ref[pl.ds(base, size), :]


def gather(spots, grid, size, devices):
    count = spots.shape[0]
    return pl.pallas_call(
        functools.partial(gather_kernel, size, devices),
        out_shape=jax.ShapeDtypeStruct((count * size, 128), F32),
        grid_spec=pltpu.PrefetchScalarGridSpec(
            num_scalar_prefetch=1,
            grid=(1,),
            in_specs=[pl.BlockSpec(grid.shape, lambda i, s: (0, 0))],
            out_specs=pl.BlockSpec((count * size, 128), lambda i, s: (0, 0)),
        ),
        compiler_params=pltpu.CompilerParams(vmem_limit_bytes=48 * 1024 * 1024),
        cost_estimate=cost(1e6, grid.size * 8),
        name="gather",
    )(spots, grid)


def layer_kernel(
    table_ref, flipped_ref, modes_ref, grid_ref, up_ref, down_ref, out_ref, spec_ref, total_ref,
    up_wide_ref, down_wide_ref
):
    step = pl.program_id(0)
    rows = table_ref.shape[0]
    tiles = modes_ref.shape[1] // 128

    @pl.when(step == 0)
    def _():
        total_ref[...] = jnp.zeros_like(total_ref)
        spread_weights(up_ref, down_ref, up_wide_ref, down_wide_ref)

    spectral = dot(table_ref[...], modes_ref[...])
    results = []
    for tile in range(tiles):
        place = pl.ds(tile, rows, stride=tiles)
        summed = grid_ref[place, :] + spectral[:, tile * 128 : (tile + 1) * 128]
        result = mlp(summed, up_wide_ref, down_wide_ref)
        out_ref[place, :] = result
        results.append(result.astype(BF16))
    total_ref[...] += dot(flipped_ref[...], jnp.concatenate(results, axis=1))

    @pl.when(step == pl.num_programs(0) - 1)
    def _():
        spec_ref[...] = total_ref[...].astype(BF16)


def weight_specs(up, down, number):
    return [
        pl.BlockSpec((1,) + up.shape[1:], lambda i: (number, 0, 0)),
        pl.BlockSpec((1,) + down.shape[1:], lambda i: (number, 0, 0)),
    ]


def wide_weights(up):
    hidden, channels = up.shape[1:]
    return [
        pltpu.VMEM((2 * channels, 2 * hidden), BF16),
        pltpu.VMEM((2 * hidden, 2 * channels), BF16),
    ]


def layer(table, flipped, modes, grid, up, down, number):
    cells, columns = table.shape
    lanes = modes.shape[1]
    tiles = lanes // 128
    rows = 512
    const = lambda i: (0, 0)
    return pl.pallas_call(
        layer_kernel,
        out_shape=(
            jax.ShapeDtypeStruct((cells * tiles, 128), F32),
            jax.ShapeDtypeStruct((columns, lanes), BF16),
        ),
        grid=(cells // rows,),
        in_specs=[
            pl.BlockSpec((rows, columns), lambda i: (i, 0)),
            pl.BlockSpec((columns, rows), lambda i: (0, i)),
            pl.BlockSpec((columns, lanes), const),
            pl.BlockSpec((rows * tiles, 128), lambda i: (i, 0)),
        ]
        + weight_specs(up, down, number),
        out_specs=(
            pl.BlockSpec((rows * tiles, 128), lambda i: (i, 0)),
            pl.BlockSpec((columns, lanes), const),
        ),
        scratch_shapes=[pltpu.VMEM((columns, lanes), F32)] + wide_weights(up),
        cost_estimate=cost(
            4 * cells * columns * lanes + 16 * cells * lanes * up.shape[1],
            cells * (columns * 4 + lanes * 8),
        ),
        name="layer",
    )(table, flipped, modes, grid, up, down)


def last_kernel(phase_ref, modes_ref, grid_ref, up_ref, down_ref, out_ref, up_wide_ref, down_wide_ref):
    group, rows, _ = out_ref.shape
    tiles = modes_ref.shape[1] // 128
    rows = rows // tiles

    @pl.when(pl.program_id(0) == 0)
    def _():
        spread_weights(up_ref, down_ref, up_wide_ref, down_wide_ref)

    spectral = lax.dot_general(
        phase_ref[...], modes_ref[...], (((0,), (0,)), ((), ())), preferred_element_type=F32
    )
    for tile in range(tiles):
        summed = (
            grid_ref[pl.ds(tile, group * rows, stride=tiles), :]
            + spectral[:, tile * 128 : (tile + 1) * 128]
        )
        result = mlp(summed, up_wide_ref, down_wide_ref).astype(BF16)
        for source in range(group):
            out_ref[source, tile * rows : (tile + 1) * rows, :] = result[
                source * rows : (source + 1) * rows, :
            ]


def last_layer(phases, modes, grid, up, down, number, devices):
    columns, count = phases.shape
    lanes = modes.shape[1]
    tiles = lanes // 128
    group = 4
    rows = count // devices
    return pl.pallas_call(
        last_kernel,
        out_shape=jax.ShapeDtypeStruct((devices, rows * tiles, 128), BF16),
        grid=(devices // group,),
        in_specs=[
            pl.BlockSpec((columns, group * rows), lambda i: (0, i)),
            pl.BlockSpec((columns, lanes), lambda i: (0, 0)),
            pl.BlockSpec((group * rows * tiles, 128), lambda i: (i, 0)),
        ]
        + weight_specs(up, down, number),
        out_specs=pl.BlockSpec((group, rows * tiles, 128), lambda i: (i, 0, 0)),
        scratch_shapes=wide_weights(up),
        cost_estimate=cost(
            2 * count * columns * lanes + 16 * count * lanes * up.shape[1],
            count * (columns * 2 + lanes * 6),
        ),
        name="last_layer",
    )(phases, modes, grid, up, down)


def exchange(values):
    return lax.all_to_all(values, "pen", split_axis=0, concat_axis=0, tiled=True)


def per_device(point_feat, pair_kernel, pair_owner, pair_block, spec_weight, mlp_up, mlp_down):
    devices = lax.axis_size("pen")
    pairs, block = pair_kernel.shape[0], pair_kernel.shape[1]
    channels = point_feat.shape[0]
    modes_here = spec_weight.shape[1]
    lines = block // NZ
    lanes = NZ // devices * channels
    tiles = lanes // 128
    columns = devices * 2 * MX

    target = pair_owner[:, 0] * (NX * NY // lines // devices) + pair_block
    x_at = jnp.repeat(target // (NY // lines), lines)
    y_at = (target % (NY // lines))[:, None] * lines + jnp.arange(lines, dtype=jnp.int32)
    spots = jnp.stack([x_at, y_at.reshape(-1)] + [jnp.zeros_like(x_at)] * 6).astype(F32)

    got = exchange(encode(point_feat, pair_kernel, spots, devices))

    table, flipped = grid_tables(devices, modes_here)
    forward, inverse = depth_tables(devices, modes_here)
    here = got[:, -8:-6, 0 : pairs * lines : lines].astype(jnp.int32)
    rows = ((here[:, 0, :] * NY + here[:, 1, :]) * tiles).reshape(devices * pairs)

    spectrum, phases = pair_spectrum(got, modes_here, lanes)
    grid = scatter(rows, got, tiles)
    modes = exchange(spectrum.reshape(devices, 2 * MX, lanes)).reshape(columns, lanes)
    modes = mix(modes, forward, inverse, spec_weight, 0, devices)
    modes = exchange(modes.reshape(devices, 2 * MX, lanes)).reshape(columns, lanes)
    grid, spectrum = layer(table, flipped, modes, grid, mlp_up, mlp_down, 0)
    listed = gather(rows, grid, lines * tiles, devices)
    modes = exchange(spectrum.reshape(devices, 2 * MX, lanes)).reshape(columns, lanes)
    modes = mix(modes, forward, inverse, spec_weight, 1, devices)
    modes = exchange(modes.reshape(devices, 2 * MX, lanes)).reshape(columns, lanes)
    result = last_layer(phases, modes, listed, mlp_up, mlp_down, 1, devices)
    return decode(exchange(result), pair_kernel, channels)


def solution(mesh):
    in_specs = (
        P(None, ("groups", "pen")),
        P(("groups", "pen"), None, None),
        P(("groups", "pen"), None),
        P(("groups", "pen")),
        P(None, "pen", None, None, None),
        P(),
        P(),
    )
    out_specs = P(None, ("groups", "pen"))
    return jax.shard_map(
        per_device, mesh=mesh, in_specs=in_specs, out_specs=out_specs, check_vma=False
    )
```

```python
import functools
import math

import jax
import jax.numpy as jnp
import numpy as np
from jax import lax
from jax.experimental import pallas as pl
from jax.experimental.pallas import tpu as pltpu
from jax.sharding import PartitionSpec as P

NX = 128
NY = 64
NZ = 64
MX = 16
MY = 16
MZ = 16
LAYERS = 2
NBR = 4
GELU_K = math.sqrt(2.0 / math.pi)
SCALE = 1.66575
PAD = 8

F32 = jnp.float32
BF16 = jnp.bfloat16


def vmem_spec():
    return pl.BlockSpec(memory_space=pltpu.VMEM)


def cost(flops, size, transcendentals=0):
    return pl.CostEstimate(
        flops=int(flops), bytes_accessed=int(size), transcendentals=int(transcendentals)
    )


def dot(left, right):
    return jnp.dot(left, right, preferred_element_type=F32)


def x_waves():
    wave = np.arange(MX) - MX // 2
    return np.concatenate([wave[wave % 2 == 0], wave[wave % 2 == 1]])


def y_waves(devices, modes_here):
    return (np.arange(devices) * modes_here) // MZ - MY // 2


def turn(wave, count):
    return 2.0 * np.pi / count * (np.arange(count)[:, None] * wave[None, :] % count)


def line_tables(devices, modes_here):
    size = 2 * MX * devices
    column = np.arange(size)
    half = MX // 2
    wave_x = x_waves()[column // (size // 2) * half + column % half]
    wave_y = y_waves(devices, modes_here)[column // MX % devices]
    part = column // half % 2
    x_angle = turn(wave_x, NX)[: NX // 2]
    y_angle = turn(wave_y, NY)
    x_cos, x_sin = SCALE * np.cos(x_angle), SCALE * np.sin(x_angle)
    first = np.where(part == 0, x_cos, -x_sin)
    second = np.where(part == 0, -x_sin, -x_cos)
    return [
        jnp.asarray(each.astype(np.float32))
        for each in (first, second, np.cos(y_angle), np.sin(y_angle))
    ]


def lookup_tables():
    result = []
    for wave, count, scale in ((x_waves(), NX, SCALE), (np.arange(MY) - MY // 2, NY, 1.0)):
        angle = turn(wave, count).T
        values = scale * np.concatenate([np.cos(angle), -np.sin(angle)])
        result.append(jnp.concatenate(split(jnp.asarray(values.astype(np.float32))), axis=0))
    return result


def split(values):
    high = values.astype(BF16)
    return high, (values - high.astype(F32)).astype(BF16)


def depth_tables(devices, modes_here):
    local = NZ // devices
    wave_z = np.arange(MZ).reshape(MZ // modes_here, modes_here)
    z_of = np.arange(devices)[None, :] + devices * np.arange(local)[:, None]
    angle = 2.0 * np.pi / NZ * (z_of[None, :, :, None] * wave_z[:, None, None, :] % NZ)
    cosine, sine = np.cos(angle), np.sin(angle)
    to_real = np.stack([cosine, sine], axis=-1)
    to_imag = np.stack([-sine, cosine], axis=-1)
    forward = np.stack([to_real, to_imag], axis=-2) / SCALE
    forward = forward.transpose(0, 1, 3, 4, 5, 2).reshape(
        -1, local * modes_here * 2, devices * 2
    )
    scale = np.where(wave_z == 0, 1.0, 2.0)[:, None, None, :] / (NX * NY * NZ * SCALE)
    cosine, sine = cosine * scale, sine * scale
    low = np.stack(
        [np.stack([cosine, -sine], axis=-1), np.stack([sine, cosine], axis=-1)], axis=2
    ).reshape(-1, local * devices * 2, modes_here * 2)
    high = np.stack(
        [np.stack([-sine, -cosine], axis=-1), np.stack([cosine, -sine], axis=-1)], axis=2
    ).reshape(-1, local * devices * 2, modes_here * 2)
    inverse = np.concatenate([low, high], axis=2)
    which = lax.axis_index("pen") * modes_here % MZ // modes_here
    chosen = []
    for table in (forward, inverse):
        table = jnp.asarray(table.astype(np.float32))
        chosen.append(table[0] if table.shape[0] == 1 else table[which])
    forward, inverse = chosen
    return jnp.concatenate(split(forward), axis=1), jnp.concatenate(split(inverse), axis=1)


def table_kernel(first_ref, second_ref, cos_ref, sin_ref, table_ref, flipped_ref):
    pieces = []
    for line in range(first_ref.shape[0]):
        piece = (
            first_ref[line : line + 1, :] * cos_ref[...]
            + second_ref[line : line + 1, :] * sin_ref[...]
        )
        pieces.append(piece.astype(BF16))
    whole = jnp.concatenate(pieces, axis=0)
    table_ref[...] = whole
    flipped_ref[...] = whole.T


def grid_tables(devices, modes_here):
    first, second, y_cos, y_sin = line_tables(devices, modes_here)
    columns = first.shape[1]
    lines = 8
    rows = lines * NY
    const = lambda i: (0, 0)
    return pl.pallas_call(
        table_kernel,
        out_shape=(
            jax.ShapeDtypeStruct((NX // 2 * NY, columns), BF16),
            jax.ShapeDtypeStruct((columns, NX // 2 * NY), BF16),
        ),
        grid=(NX // 2 // lines,),
        in_specs=[
            pl.BlockSpec((lines, columns), lambda i: (i, 0)),
            pl.BlockSpec((lines, columns), lambda i: (i, 0)),
            pl.BlockSpec((NY, columns), const),
            pl.BlockSpec((NY, columns), const),
        ],
        out_specs=(
            pl.BlockSpec((rows, columns), lambda i: (i, 0)),
            pl.BlockSpec((columns, rows), lambda i: (0, i)),
        ),
        cost_estimate=cost(4 * NX // 2 * NY * columns, 4 * NX // 2 * NY * columns),
        name="tables",
    )(first, second, y_cos, y_sin)


def encode_kernel(feature_ref, weight_ref, spot_ref, out_ref, wide_ref):
    devices = out_ref.shape[0]
    pairs, block = weight_ref.shape[0], weight_ref.shape[1]
    lines = block // NZ
    tiles = NZ // devices // 2
    rows = tiles * pairs * lines
    lane = lax.broadcasted_iota(jnp.int32, (devices, 128), 1)

    def one(point, carry):
        features = feature_ref[:, pl.ds(pl.multiple_of(point * block, block), block)]
        features = jnp.concatenate([features, features], axis=0)
        for near in range(NBR):
            pair = point * NBR + near
            turned = lax.dot_general(
                weight_ref[pair], features, (((0,), (1,)), ((), ())), preferred_element_type=F32
            )
            for line in range(lines):
                for tile in range(tiles):
                    first = line * NZ + 2 * tile * devices
                    wide_ref[
                        pl.ds((tile * pairs + pair) * lines + line, devices, stride=rows + PAD), :
                    ] = jnp.where(
                        lane < 64,
                        turned[first : first + devices],
                        turned[first + devices : first + 2 * devices],
                    )
        return carry

    lax.fori_loop(0, pairs // NBR, one, 0)
    for device in range(devices):
        base = device * (rows + PAD)
        out_ref[device, 0:rows, :] = wide_ref[base : base + rows, :].astype(BF16)
        out_ref[device, rows : rows + 8, :] = spot_ref[...].astype(BF16)


def encode(features, weights, spots, devices):
    pairs, block = weights.shape[0], weights.shape[1]
    rows = NZ // devices // 2 * pairs * (block // NZ)
    return pl.pallas_call(
        encode_kernel,
        out_shape=jax.ShapeDtypeStruct((devices, rows + 8, 128), BF16),
        in_specs=[vmem_spec()] * 3,
        out_specs=vmem_spec(),
        scratch_shapes=[pltpu.VMEM((devices * (rows + PAD), 128), F32)],
        cost_estimate=cost(4 * pairs * block * block * 64, pairs * block * block * 2),
        name="encode",
    )(features, weights, spots)


def decode_kernel(got_ref, weight_ref, out_ref, wide_ref):
    devices, rows, _ = got_ref.shape
    pairs, block = weight_ref.shape[0], weight_ref.shape[1]
    lines = block // NZ
    tiles = NZ // devices // 2
    lane = lax.broadcasted_iota(jnp.int32, (devices, 128), 1)
    for device in range(devices):
        base = device * (rows + PAD)
        wide_ref[base : base + rows, :] = got_ref[device].astype(F32)

    def one(point, carry):
        total = None
        for near in range(NBR):
            pair = point * NBR + near
            pieces = []
            for line in range(lines):
                for tile in range(tiles):
                    values = wide_ref[
                        pl.ds((tile * pairs + pair) * lines + line, devices, stride=rows + PAD), :
                    ]
                    pieces.append(jnp.where(lane < 64, values, 0.0))
                    pieces.append(jnp.where(lane < 64, 0.0, values))
            part = lax.dot_general(
                jnp.concatenate(pieces, axis=0).astype(BF16),
                weight_ref[pair],
                (((0,), (1,)), ((), ())),
                preferred_element_type=F32,
            )
            total = part if total is None else total + part
        out_ref[:, pl.ds(pl.multiple_of(point * block, block), block)] = (
            total[0:64, :] + total[64:128, :]
        )
        return carry

    lax.fori_loop(0, pairs // NBR, one, 0)


def decode(got, weights, channels):
    devices, rows, _ = got.shape
    pairs, block = weights.shape[0], weights.shape[1]
    return pl.pallas_call(
        decode_kernel,
        out_shape=jax.ShapeDtypeStruct((channels, pairs // NBR * block), F32),
        in_specs=[vmem_spec()] * 2,
        out_specs=vmem_spec(),
        scratch_shapes=[pltpu.VMEM((devices * (rows + PAD), 128), F32)],
        cost_estimate=cost(4 * pairs * block * block * 64, pairs * block * block * 2),
        name="decode",
    )(got, weights)


def pair_spectrum_kernel(modes_here, got_ref, x_ref, y_ref, out_ref, phase_ref):
    devices = got_ref.shape[0]
    rows = got_ref.shape[1] - 8
    tiles = out_ref.shape[1] // 128
    lanes = rows // tiles
    half = MX // 2
    x_all = lax.broadcasted_iota(jnp.int32, (NX, lanes), 0)
    y_all = lax.broadcasted_iota(jnp.int32, (NY, lanes), 0)

    def look_up(table_ref, chosen):
        values = dot(table_ref[...], chosen.astype(F32).astype(BF16))
        count = values.shape[0] // 2
        return values[0:count] + values[count:]

    for source in range(devices):
        spot = got_ref[source, rows : rows + 8, :].astype(F32)
        x_turn = look_up(x_ref, x_all == spot[0:1, :].astype(jnp.int32))
        y_turn = look_up(y_ref, y_all == spot[1:2, :].astype(jnp.int32))
        place = slice(source * lanes, (source + 1) * lanes)
        for device in range(devices):
            row = (device * modes_here) // MZ
            y_cos, y_less = y_turn[row : row + 1, :], y_turn[MY + row : MY + row + 1, :]
            for parity in range(2):
                first = parity * half
                x_cos, x_less = x_turn[first : first + half], x_turn[MX + first : MX + first + half]
                both = jnp.concatenate(
                    [x_cos * y_cos - x_less * y_less, x_less * y_cos + x_cos * y_less], axis=0
                )
                base = (2 * device + parity) * MX
                phase_ref[base : base + MX, place] = both.astype(BF16)
    values = jnp.concatenate(
        [
            jnp.concatenate(
                [
                    got_ref[source, tile * lanes : (tile + 1) * lanes, :]
                    for source in range(devices)
                ],
                axis=0,
            )
            for tile in range(tiles)
        ],
        axis=1,
    )
    out_ref[...] = dot(phase_ref[...], values).astype(BF16)


def pair_spectrum(got, modes_here, lanes):
    devices, rows, _ = got.shape
    count = devices * (rows - 8) // (lanes // 128)
    columns = devices * 2 * MX
    return pl.pallas_call(
        functools.partial(pair_spectrum_kernel, modes_here),
        out_shape=(
            jax.ShapeDtypeStruct((columns, lanes), BF16),
            jax.ShapeDtypeStruct((columns, count), BF16),
        ),
        in_specs=[vmem_spec()] * 3,
        out_specs=(vmem_spec(), vmem_spec()),
        cost_estimate=cost(2 * columns * count * lanes, got.size * 2 + columns * count * 2),
        name="pair_spectrum",
    )(got, *lookup_tables())


def row_of(wave, part):
    half = MX // 2
    order = list(x_waves() + half).index(wave)
    return order // half * MX + part * half + order % half


def mix_kernel(
    devices, number, got_ref, forward_ref, inverse_ref, all_ref, out_ref, wide_ref, back_ref,
    weight_ref, sem_ref
):
    modes_here, _, channels, _ = weight_ref.shape
    pieces_at = [slice(first, first + 4) for first in range(0, MX, 4)]
    copies = [
        pltpu.make_async_copy(
            all_ref.at[number, :, place], weight_ref.at[:, place], sem_ref.at[index]
        )
        for index, place in enumerate(pieces_at)
    ]
    for copy in copies:
        copy.start()
    local = got_ref.shape[1] // channels
    tiles = got_ref.shape[1] // 128
    group = 8
    for tile in range(tiles):
        wide_ref[tile] = got_ref[:, tile * 128 : (tile + 1) * 128].astype(F32)
    lane = lax.broadcasted_iota(jnp.int32, (2 * modes_here, 128), 1)
    row = lax.broadcasted_iota(jnp.int32, (2 * group, 128), 0)
    lane_small = lax.broadcasted_iota(jnp.int32, (2 * group, 128), 1)
    lane_back = lax.broadcasted_iota(jnp.int32, (2 * devices, 128), 1)
    forward = forward_ref[...]
    inverse = inverse_ref[...]
    spread = []
    for wave in range(MX):
        planes = jnp.concatenate(
            [
                jnp.concatenate(
                    [
                        wide_ref[tile, pl.ds(row_of(wave, part), devices, stride=2 * MX), :]
                        for part in range(2)
                    ],
                    axis=0,
                )
                for tile in range(tiles)
            ],
            axis=1,
        ).astype(BF16)
        turned = dot(forward, jnp.concatenate([planes, planes], axis=0))
        total = None
        for tile in range(tiles):
            part = slice(tile * 128, (tile + 1) * 128)
            size = 2 * modes_here
            even = turned[2 * tile * size : (2 * tile + 1) * size, part]
            odd = turned[(2 * tile + 1) * size : (2 * tile + 2) * size, part]
            both = even + pltpu.roll(odd, 64, 1)
            total = both if total is None else total + both
        spread.append(jnp.where(lane < 64, total, pltpu.roll(total, 64, 1)))
    mixed = []
    for wave in range(MX):
        pieces = []
        if wave % 4 == 0:
            copies[wave // 4].wait()
        for first in range(0, modes_here, group):
            now = spread[wave][2 * first : 2 * (first + group), :]
            left = jnp.concatenate(
                [
                    jnp.where(row // 2 == 2 * step + lane_small // 64, now, 0.0)
                    for step in range(group // 2)
                ],
                axis=1,
            )
            left = jnp.concatenate(split(left), axis=0)
            right = weight_ref[first : first + group, wave, :, :].reshape(
                group * channels, 2 * channels
            )
            both = dot(left, right)
            pieces.append(both[0 : 2 * group] + both[2 * group :])
        mixed.append(pieces[0] if len(pieces) == 1 else jnp.concatenate(pieces, axis=0))
    for wave in range(MX):
        stacked = jnp.concatenate([mixed[wave], pltpu.roll(mixed[wave], 64, 1)], axis=0)
        upper, lower = split(stacked)
        count = upper.shape[0]
        planes = dot(inverse, jnp.concatenate([upper, upper], axis=0)) + dot(
            inverse[:, 0:count], lower
        )
        size = 2 * devices
        for tile in range(tiles):
            even = planes[2 * tile * size : (2 * tile + 1) * size, :]
            odd = planes[(2 * tile + 1) * size : (2 * tile + 2) * size, :]
            both = jnp.where(lane_back < 64, even, pltpu.roll(odd, 64, 1))
            for part in range(2):
                back_ref[tile, pl.ds(row_of(wave, part), devices, stride=2 * MX), :] = both[
                    part * devices : (part + 1) * devices
                ]
    for tile in range(tiles):
        out_ref[:, tile * 128 : (tile + 1) * 128] = back_ref[tile].astype(BF16)


def mix(got, forward, inverse, weights, number, devices):
    rows, lanes = got.shape
    return pl.pallas_call(
        functools.partial(mix_kernel, devices, number),
        out_shape=jax.ShapeDtypeStruct((rows, lanes), BF16),
        in_specs=[vmem_spec()] * 3 + [pl.BlockSpec(memory_space=pl.ANY)],
        out_specs=vmem_spec(),
        scratch_shapes=[pltpu.VMEM((lanes // 128, rows, 128), F32)] * 2
        + [pltpu.VMEM(weights.shape[1:], BF16), pltpu.SemaphoreType.DMA((4,))],
        cost_estimate=cost(6e8, weights.size + rows * lanes * 4),
        name="mix",
    )(got, forward, inverse, weights)


def spread_weights(up_ref, down_ref, up_wide_ref, down_wide_ref):
    hidden, channels = up_ref.shape[1:]
    up = up_ref[0].T
    down = (down_ref[0].astype(F32) * 0.5).astype(BF16).T
    up_wide_ref[...] = jnp.zeros_like(up_wide_ref)
    down_wide_ref[...] = jnp.zeros_like(down_wide_ref)
    for cell in range(2):
        here = slice(cell * channels, (cell + 1) * channels)
        there = slice(cell * hidden, (cell + 1) * hidden)
        up_wide_ref[here, there] = up
        down_wide_ref[there, here] = down


def gelu_twice(hidden):
    hidden = hidden.astype(BF16)
    first = jnp.asarray(GELU_K, BF16)
    third = jnp.asarray(GELU_K * 0.044715, BF16)
    return hidden * jnp.tanh(hidden * (first + third * (hidden * hidden))) + hidden


def mlp(summed, up_ref, down_ref):
    width = 256
    rounded = [each.astype(BF16) for each in summed]
    totals = list(summed)
    for first in range(0, up_ref.shape[1], width):
        hidden = [dot(each, up_ref[:, first : first + width]) for each in rounded]
        active = [gelu_twice(each) for each in hidden]
        for n, each in enumerate(active):
            totals[n] = totals[n] + dot(each, down_ref[first : first + width, :])
    return totals


def scatter_kernel(spot_ref, got_ref, out_ref, wide_ref):
    devices, rows, _ = got_ref.shape
    rows = rows - 8
    pairs = spot_ref.shape[0] // devices
    size = rows // pairs
    lines = size // TILES(out_ref)
    tiles = TILES(out_ref)
    out_ref[...] = jnp.zeros_like(out_ref)
    for source in range(devices):
        for tile in range(tiles):
            wide_ref[pl.ds(source * rows + tile, pairs * lines, stride=tiles), :] = got_ref[
                source, tile * pairs * lines : (tile + 1) * pairs * lines, :
            ].astype(F32)

    @pl.loop(0, devices)
    def _(source):
        for pair in range(pairs):
            base = pl.multiple_of(spot_ref[source * pairs + pair], size)
            here = pl.multiple_of(source * rows + pair * size, size)
            out_ref[pl.ds(base, size), :] = (
                out_ref[pl.ds(base, size), :] + wide_ref[pl.ds(here, size), :]
            )


def TILES(ref):
    return ref.shape[0] // (NX * NY)


def scatter(spots, got, tiles):
    devices, rows, _ = got.shape
    return pl.pallas_call(
        scatter_kernel,
        out_shape=jax.ShapeDtypeStruct((NX * NY * tiles, 128), F32),
        grid_spec=pltpu.PrefetchScalarGridSpec(
            num_scalar_prefetch=1,
            grid=(1,),
            in_specs=[pl.BlockSpec(got.shape, lambda i, s: (0, 0, 0))],
            out_specs=pl.BlockSpec((NX * NY * tiles, 128), lambda i, s: (0, 0)),
            scratch_shapes=[pltpu.VMEM((devices * (rows - 8), 128), F32)],
        ),
        compiler_params=pltpu.CompilerParams(vmem_limit_bytes=48 * 1024 * 1024),
        cost_estimate=cost(1e6, NX * NY * tiles * 128 * 16),
        name="scatter",
    )(spots, got)


def gather_kernel(size, devices, spot_ref, grid_ref, out_ref):
    pairs = spot_ref.shape[0] // devices

    @pl.loop(0, devices)
    def _(source):
        for pair in range(pairs):
            base = pl.multiple_of(spot_ref[source * pairs + pair], size)
            here = pl.multiple_of(source * (pairs * size) + pair * size, size)
            out_ref[pl.ds(here, size), :] = grid_ref[pl.ds(base, size), :]


def gather(spots, grid, size, devices):
    count = spots.shape[0]
    return pl.pallas_call(
        functools.partial(gather_kernel, size, devices),
        out_shape=jax.ShapeDtypeStruct((count * size, 128), F32),
        grid_spec=pltpu.PrefetchScalarGridSpec(
            num_scalar_prefetch=1,
            grid=(1,),
            in_specs=[pl.BlockSpec(grid.shape, lambda i, s: (0, 0))],
            out_specs=pl.BlockSpec((count * size, 128), lambda i, s: (0, 0)),
        ),
        compiler_params=pltpu.CompilerParams(vmem_limit_bytes=48 * 1024 * 1024),
        cost_estimate=cost(1e6, grid.size * 8),
        name="gather",
    )(spots, grid)


def layer_kernel(
    table_ref, flipped_ref, modes_ref, grid_ref, up_ref, down_ref, out_ref, spec_ref, total_ref,
    up_wide_ref, down_wide_ref, folded_ref
):
    step = pl.program_id(0)
    rows = table_ref.shape[0]
    tiles = modes_ref.shape[1] // 128
    count = table_ref.shape[1] // 2
    blocks = count // MX

    @pl.when(step == 0)
    def _():
        total_ref[...] = jnp.zeros_like(total_ref)
        spread_weights(up_ref, down_ref, up_wide_ref, down_wide_ref)
        for parity in range(2):
            for block in range(blocks):
                base = (2 * block + parity) * MX
                folded_ref[parity, block * MX : (block + 1) * MX, :] = modes_ref[base : base + MX]

    even = dot(table_ref[:, 0:count], folded_ref[0])
    odd = dot(table_ref[:, count:], folded_ref[1])
    halves = (even + odd, even - odd)
    places = [(side, tile) for side in range(2) for tile in range(tiles)]
    summed = [
        grid_ref[side, pl.ds(tile, rows, stride=tiles), :]
        + halves[side][:, tile * 128 : (tile + 1) * 128]
        for side, tile in places
    ]
    results = mlp(summed, up_wide_ref, down_wide_ref)
    for (side, tile), result in zip(places, results):
        out_ref[side, pl.ds(tile, rows, stride=tiles), :] = result
    low, high = results[0:tiles], results[tiles:]
    plus = jnp.concatenate([(a + b).astype(BF16) for a, b in zip(low, high)], axis=1)
    minus = jnp.concatenate([(a - b).astype(BF16) for a, b in zip(low, high)], axis=1)
    total_ref[0] += dot(flipped_ref[0:count, :], plus)
    total_ref[1] += dot(flipped_ref[count:, :], minus)

    @pl.when(step == pl.num_programs(0) - 1)
    def _():
        for parity in range(2):
            for block in range(blocks):
                base = (2 * block + parity) * MX
                spec_ref[base : base + MX, :] = total_ref[
                    parity, block * MX : (block + 1) * MX, :
                ].astype(BF16)


def weight_specs(up, down, number):
    return [
        pl.BlockSpec((1,) + up.shape[1:], lambda i: (number, 0, 0)),
        pl.BlockSpec((1,) + down.shape[1:], lambda i: (number, 0, 0)),
    ]


def wide_weights(up):
    hidden, channels = up.shape[1:]
    return [
        pltpu.VMEM((2 * channels, 2 * hidden), BF16),
        pltpu.VMEM((2 * hidden, 2 * channels), BF16),
    ]


def layer(table, flipped, modes, grid, up, down, number):
    cells, columns = table.shape
    lanes = modes.shape[1]
    tiles = lanes // 128
    rows = 512
    const = lambda i: (0, 0)
    return pl.pallas_call(
        layer_kernel,
        out_shape=(
            jax.ShapeDtypeStruct((2, cells * tiles, 128), F32),
            jax.ShapeDtypeStruct((columns, lanes), BF16),
        ),
        grid=(cells // rows,),
        in_specs=[
            pl.BlockSpec((rows, columns), lambda i: (i, 0)),
            pl.BlockSpec((columns, rows), lambda i: (0, i)),
            pl.BlockSpec((columns, lanes), const),
            pl.BlockSpec((2, rows * tiles, 128), lambda i: (0, i, 0)),
        ]
        + weight_specs(up, down, number),
        out_specs=(
            pl.BlockSpec((2, rows * tiles, 128), lambda i: (0, i, 0)),
            pl.BlockSpec((columns, lanes), const),
        ),
        scratch_shapes=[pltpu.VMEM((2, columns // 2, lanes), F32)]
        + wide_weights(up)
        + [pltpu.VMEM((2, columns // 2, lanes), BF16)],
        cost_estimate=cost(
            4 * cells * columns * lanes + 16 * cells * lanes * up.shape[1],
            cells * (columns * 4 + lanes * 8),
        ),
        name="layer",
    )(table, flipped, modes, grid.reshape(2, cells * tiles, 128), up, down)


def last_kernel(phase_ref, modes_ref, grid_ref, up_ref, down_ref, out_ref, up_wide_ref, down_wide_ref):
    group, rows, _ = out_ref.shape
    tiles = modes_ref.shape[1] // 128
    rows = rows // tiles

    @pl.when(pl.program_id(0) == 0)
    def _():
        spread_weights(up_ref, down_ref, up_wide_ref, down_wide_ref)

    spectral = lax.dot_general(
        phase_ref[...], modes_ref[...], (((0,), (0,)), ((), ())), preferred_element_type=F32
    )
    summed = [
        grid_ref[pl.ds(tile, group * rows, stride=tiles), :]
        + spectral[:, tile * 128 : (tile + 1) * 128]
        for tile in range(tiles)
    ]
    results = mlp(summed, up_wide_ref, down_wide_ref)
    for tile, result in enumerate(results):
        result = result.astype(BF16)
        for source in range(group):
            out_ref[source, tile * rows : (tile + 1) * rows, :] = result[
                source * rows : (source + 1) * rows, :
            ]


def last_layer(phases, modes, grid, up, down, number, devices):
    columns, count = phases.shape
    lanes = modes.shape[1]
    tiles = lanes // 128
    group = 8
    rows = count // devices
    return pl.pallas_call(
        last_kernel,
        out_shape=jax.ShapeDtypeStruct((devices, rows * tiles, 128), BF16),
        grid=(devices // group,),
        in_specs=[
            pl.BlockSpec((columns, group * rows), lambda i: (0, i)),
            pl.BlockSpec((columns, lanes), lambda i: (0, 0)),
            pl.BlockSpec((group * rows * tiles, 128), lambda i: (i, 0)),
        ]
        + weight_specs(up, down, number),
        out_specs=pl.BlockSpec((group, rows * tiles, 128), lambda i: (i, 0, 0)),
        scratch_shapes=wide_weights(up),
        cost_estimate=cost(
            2 * count * columns * lanes + 16 * count * lanes * up.shape[1],
            count * (columns * 2 + lanes * 6),
        ),
        name="last_layer",
    )(phases, modes, grid, up, down)


def exchange(values):
    return lax.all_to_all(values, "pen", split_axis=0, concat_axis=0, tiled=True)


def per_device(point_feat, pair_kernel, pair_owner, pair_block, spec_weight, mlp_up, mlp_down):
    devices = lax.axis_size("pen")
    pairs, block = pair_kernel.shape[0], pair_kernel.shape[1]
    channels = point_feat.shape[0]
    modes_here = spec_weight.shape[1]
    lines = block // NZ
    lanes = NZ // devices * channels
    tiles = lanes // 128
    columns = devices * 2 * MX

    target = pair_owner[:, 0] * (NX * NY // lines // devices) + pair_block
    x_at = jnp.repeat(target // (NY // lines), lines)
    y_at = (target % (NY // lines))[:, None] * lines + jnp.arange(lines, dtype=jnp.int32)
    spots = jnp.stack([x_at, y_at.reshape(-1)] + [jnp.zeros_like(x_at)] * 6).astype(F32)

    got = exchange(encode(point_feat, pair_kernel, spots, devices))

    table, flipped = grid_tables(devices, modes_here)
    forward, inverse = depth_tables(devices, modes_here)
    got, table, flipped = lax.optimization_barrier((got, table, flipped))
    here = got[:, -8:-6, 0 : pairs * lines : lines].astype(jnp.int32)
    rows = ((here[:, 0, :] * NY + here[:, 1, :]) * tiles).reshape(devices * pairs)

    spectrum, phases = pair_spectrum(got, modes_here, lanes)
    grid = scatter(rows, got, tiles)
    modes = exchange(spectrum.reshape(devices, 2 * MX, lanes)).reshape(columns, lanes)
    modes = mix(modes, forward, inverse, spec_weight, 0, devices)
    modes = exchange(modes.reshape(devices, 2 * MX, lanes)).reshape(columns, lanes)
    grid, spectrum = layer(table, flipped, modes, grid, mlp_up, mlp_down, 0)
    listed = gather(rows, grid.reshape(-1, 128), lines * tiles, devices)
    modes = exchange(spectrum.reshape(devices, 2 * MX, lanes)).reshape(columns, lanes)
    modes = mix(modes, forward, inverse, spec_weight, 1, devices)
    modes = exchange(modes.reshape(devices, 2 * MX, lanes)).reshape(columns, lanes)
    result = last_layer(phases, modes, listed, mlp_up, mlp_down, 1, devices)
    return decode(exchange(result), pair_kernel, channels)


def solution(mesh):
    in_specs = (
        P(None, ("groups", "pen")),
        P(("groups", "pen"), None, None),
        P(("groups", "pen"), None),
        P(("groups", "pen")),
        P(None, "pen", None, None, None),
        P(),
        P(),
    )
    out_specs = P(None, ("groups", "pen"))
    return jax.shard_map(
        per_device, mesh=mesh, in_specs=in_specs, out_specs=out_specs, check_vma=False
    )
```

```python
import functools
import math

import jax
import jax.numpy as jnp
import numpy as np
from jax import lax
from jax.experimental import pallas as pl
from jax.experimental.pallas import tpu as pltpu
from jax.sharding import PartitionSpec as P

NX = 128
NY = 64
NZ = 64
MX = 16
MY = 16
MZ = 16
LAYERS = 2
NBR = 4
GELU_K = math.sqrt(2.0 / math.pi)
SCALE = 1.66575
PAD = 8
PARTS = 4

F32 = jnp.float32
BF16 = jnp.bfloat16


def vmem_spec():
    return pl.BlockSpec(memory_space=pltpu.VMEM)


def in_vmem(values):
    return pltpu.with_memory_space_constraint(values, pltpu.VMEM)


def in_hbm(values):
    return pltpu.with_memory_space_constraint(values, pltpu.HBM)


def any_spec():
    return pl.BlockSpec(memory_space=pl.ANY)


def limit(mebibytes):
    return pltpu.CompilerParams(vmem_limit_bytes=mebibytes << 20)


def cost(flops, size, transcendentals=0):
    return pl.CostEstimate(
        flops=int(flops), bytes_accessed=int(size), transcendentals=int(transcendentals)
    )


def dot(left, right):
    return jnp.dot(left, right, preferred_element_type=F32)


def x_waves():
    wave = np.arange(MX) - MX // 2
    return np.concatenate([wave[wave % 2 == 0], wave[wave % 2 == 1]])


def y_waves(devices, modes_here):
    return (np.arange(devices) * modes_here) // MZ - MY // 2


def turn(wave, count):
    return 2.0 * np.pi / count * (np.arange(count)[:, None] * wave[None, :] % count)


def line_tables(devices, modes_here):
    size = 2 * MX * devices
    column = np.arange(size)
    half = MX // 2
    wave_x = x_waves()[column // (size // 2) * half + column % half]
    wave_y = y_waves(devices, modes_here)[column // MX % devices]
    part = column // half % 2
    x_angle = turn(wave_x, NX)[: NX // 2]
    y_angle = turn(wave_y, NY)
    x_cos, x_sin = SCALE * np.cos(x_angle), SCALE * np.sin(x_angle)
    first = np.where(part == 0, x_cos, -x_sin)
    second = np.where(part == 0, -x_sin, -x_cos)
    return [
        jnp.asarray(each.astype(np.float32))
        for each in (first, second, np.cos(y_angle), np.sin(y_angle))
    ]


def lookup_tables():
    result = []
    for wave, count, scale in ((x_waves(), NX, SCALE), (np.arange(MY) - MY // 2, NY, 1.0)):
        angle = turn(wave, count).T
        values = scale * np.concatenate([np.cos(angle), -np.sin(angle)])
        result.append(jnp.concatenate(split(jnp.asarray(values.astype(np.float32))), axis=0))
    return result


def split(values):
    high = values.astype(BF16)
    return high, (values - high.astype(F32)).astype(BF16)


def depth_tables(devices, modes_here):
    local = NZ // devices
    wave_z = np.arange(MZ).reshape(MZ // modes_here, modes_here)
    z_of = np.arange(devices)[None, :] + devices * np.arange(local)[:, None]
    angle = 2.0 * np.pi / NZ * (z_of[None, :, :, None] * wave_z[:, None, None, :] % NZ)
    cosine, sine = np.cos(angle), np.sin(angle)
    to_real = np.stack([cosine, sine], axis=-1)
    to_imag = np.stack([-sine, cosine], axis=-1)
    forward = np.stack([to_real, to_imag], axis=-2) / SCALE
    forward = forward.transpose(0, 1, 3, 4, 5, 2).reshape(
        -1, local * modes_here * 2, devices * 2
    )
    scale = np.where(wave_z == 0, 1.0, 2.0)[:, None, None, :] / (NX * NY * NZ * SCALE)
    cosine, sine = cosine * scale, sine * scale
    low = np.stack(
        [np.stack([cosine, -sine], axis=-1), np.stack([sine, cosine], axis=-1)], axis=2
    ).reshape(-1, local * devices * 2, modes_here * 2)
    high = np.stack(
        [np.stack([-sine, -cosine], axis=-1), np.stack([cosine, -sine], axis=-1)], axis=2
    ).reshape(-1, local * devices * 2, modes_here * 2)
    inverse = np.concatenate([low, high], axis=2)
    which = lax.axis_index("pen") * modes_here % MZ // modes_here
    chosen = []
    for table in (forward, inverse):
        table = jnp.asarray(table.astype(np.float32))
        chosen.append(table[0] if table.shape[0] == 1 else table[which])
    forward, inverse = chosen
    return jnp.concatenate(split(forward), axis=1), jnp.concatenate(split(inverse), axis=1)


def table_kernel(first_ref, second_ref, cos_ref, sin_ref, table_ref, flipped_ref):
    pieces = []
    for line in range(first_ref.shape[0]):
        piece = (
            first_ref[line : line + 1, :] * cos_ref[...]
            + second_ref[line : line + 1, :] * sin_ref[...]
        )
        pieces.append(piece.astype(BF16))
    whole = jnp.concatenate(pieces, axis=0)
    table_ref[...] = whole
    flipped_ref[...] = whole.T


def grid_tables(devices, modes_here):
    first, second, y_cos, y_sin = line_tables(devices, modes_here)
    columns = first.shape[1]
    lines = 8
    rows = lines * NY
    const = lambda i: (0, 0)
    return pl.pallas_call(
        table_kernel,
        out_shape=(
            pltpu.HBM((NX // 2 * NY, columns), BF16),
            pltpu.HBM((columns, NX // 2 * NY), BF16),
        ),
        grid=(NX // 2 // lines,),
        in_specs=[
            pl.BlockSpec((lines, columns), lambda i: (i, 0)),
            pl.BlockSpec((lines, columns), lambda i: (i, 0)),
            pl.BlockSpec((NY, columns), const),
            pl.BlockSpec((NY, columns), const),
        ],
        out_specs=(
            pl.BlockSpec((rows, columns), lambda i: (i, 0)),
            pl.BlockSpec((columns, rows), lambda i: (0, i)),
        ),
        cost_estimate=cost(4 * NX // 2 * NY * columns, 4 * NX // 2 * NY * columns),
        compiler_params=limit(8),
        name="tables",
    )(first, second, y_cos, y_sin)


def copies_of(from_ref, to_ref, sem_ref):
    step = from_ref.shape[0] // PARTS
    return [
        pltpu.make_async_copy(
            from_ref.at[pl.ds(part * step, step)],
            to_ref.at[pl.ds(part * step, step)],
            sem_ref.at[part],
        )
        for part in range(PARTS)
    ]


def encode_kernel(
    feature_hbm_ref, weight_hbm_ref, owner_ref, number_ref, out_ref, wide_ref, feature_ref,
    weight_ref, sem_ref
):
    devices = out_ref.shape[0]
    pairs, block = weight_ref.shape[0], weight_ref.shape[1]
    points = pairs // NBR
    lines = block // NZ
    tiles = NZ // devices // 2
    rows = tiles * pairs * lines
    copies = copies_of(weight_hbm_ref, weight_ref, sem_ref)
    first_copy = pltpu.make_async_copy(feature_hbm_ref, feature_ref, sem_ref.at[PARTS])
    for copy in [first_copy] + copies:
        copy.start()
    lane = lax.broadcasted_iota(jnp.int32, (devices, 128), 1)
    strip = NY // lines
    target = owner_ref[...] * (NX * strip // devices) + number_ref[...]
    y_at = (target % strip) * lines
    spots = jnp.concatenate(
        [
            jnp.concatenate([target // strip] * lines, axis=1),
            jnp.concatenate([y_at + line for line in range(lines)], axis=1),
            jnp.zeros((6, 128), jnp.int32),
        ],
        axis=0,
    )
    spots = spots.astype(F32).astype(BF16)
    for device in range(devices):
        out_ref[device, rows : rows + 8, :] = spots
    first_copy.wait()

    def one(point, carry):
        features = feature_ref[:, pl.ds(pl.multiple_of(point * block, block), block)]
        features = jnp.concatenate([features, features], axis=0)
        for near in range(NBR):
            pair = point * NBR + near
            turned = lax.dot_general(
                weight_ref[pair], features, (((0,), (1,)), ((), ())), preferred_element_type=F32
            )
            for line in range(lines):
                for tile in range(tiles):
                    first = line * NZ + 2 * tile * devices
                    wide_ref[
                        pl.ds((tile * lines + line) * pairs + pair, devices, stride=rows + PAD), :
                    ] = jnp.where(
                        lane < 64,
                        turned[first : first + devices],
                        turned[first + devices : first + 2 * devices],
                    )
        return carry

    for part, copy in enumerate(copies):
        copy.wait()
        lax.fori_loop(
            part * points // PARTS, (part + 1) * points // PARTS, one, 0, unroll=2
        )
    for device in range(devices):
        base = device * (rows + PAD)
        out_ref[device, 0:rows, :] = wide_ref[base : base + rows, :].astype(BF16)


def encode(features, weights, owners, numbers, devices):
    pairs, block = weights.shape[0], weights.shape[1]
    rows = NZ // devices // 2 * pairs * (block // NZ)
    return pl.pallas_call(
        encode_kernel,
        out_shape=jax.ShapeDtypeStruct((devices, rows + 8, 128), BF16),
        in_specs=[any_spec()] * 2 + [vmem_spec()] * 2,
        out_specs=vmem_spec(),
        scratch_shapes=[
            pltpu.VMEM((devices * (rows + PAD), 128), F32),
            pltpu.VMEM(features.shape, BF16),
            pltpu.VMEM(weights.shape, BF16),
            pltpu.SemaphoreType.DMA((PARTS + 1,)),
        ],
        compiler_params=limit(10),
        cost_estimate=cost(4 * pairs * block * block * 64, pairs * block * block * 2),
        name="encode",
    )(in_hbm(features), in_hbm(weights), owners, numbers)


def decode_kernel(got_ref, weight_hbm_ref, out_ref, wide_ref, weight_ref, sem_ref):
    copies = copies_of(weight_hbm_ref, weight_ref, sem_ref)
    for copy in copies:
        copy.start()
    devices, rows, _ = got_ref.shape
    pairs, block = weight_ref.shape[0], weight_ref.shape[1]
    lines = block // NZ
    tiles = NZ // devices // 2
    lane = lax.broadcasted_iota(jnp.int32, (devices, 128), 1)
    for device in range(devices):
        base = device * (rows + PAD)
        wide_ref[base : base + rows, :] = got_ref[device].astype(F32)

    def one(point, carry):
        total = None
        for near in range(NBR):
            pair = point * NBR + near
            pieces = []
            for line in range(lines):
                for tile in range(tiles):
                    values = wide_ref[
                        pl.ds((tile * lines + line) * pairs + pair, devices, stride=rows + PAD), :
                    ]
                    pieces.append(jnp.where(lane < 64, values, 0.0))
                    pieces.append(jnp.where(lane < 64, 0.0, values))
            part = lax.dot_general(
                jnp.concatenate(pieces, axis=0).astype(BF16),
                weight_ref[pair],
                (((0,), (1,)), ((), ())),
                preferred_element_type=F32,
            )
            total = part if total is None else total + part
        out_ref[:, pl.ds(pl.multiple_of(point * block, block), block)] = (
            total[0:64, :] + total[64:128, :]
        )
        return carry

    points = pairs // NBR
    for part, copy in enumerate(copies):
        copy.wait()
        lax.fori_loop(
            part * points // PARTS, (part + 1) * points // PARTS, one, 0, unroll=2
        )


def decode(got, weights, channels):
    devices, rows, _ = got.shape
    pairs, block = weights.shape[0], weights.shape[1]
    return pl.pallas_call(
        decode_kernel,
        out_shape=jax.ShapeDtypeStruct((channels, pairs // NBR * block), F32),
        in_specs=[vmem_spec(), any_spec()],
        out_specs=vmem_spec(),
        scratch_shapes=[
            pltpu.VMEM((devices * (rows + PAD), 128), F32),
            pltpu.VMEM(weights.shape, BF16),
            pltpu.SemaphoreType.DMA((PARTS,)),
        ],
        cost_estimate=cost(4 * pairs * block * block * 64, pairs * block * block * 2),
        compiler_params=limit(12),
        name="decode",
    )(got, in_hbm(weights))


def look_up(table_ref, count, spot):
    every = lax.broadcasted_iota(jnp.int32, (count, spot.shape[1]), 0)
    values = dot(table_ref[...], (every == spot).astype(F32).astype(BF16))
    half = values.shape[0] // 2
    return values[0:half] + values[half:]


def fill_phases(modes_here, devices, spots, x_ref, y_ref, phase_ref):
    half = MX // 2
    for source, spot in enumerate(spots):
        spot = spot.astype(F32)
        x_turn = look_up(x_ref, NX, spot[0:1, :].astype(jnp.int32))
        y_turn = look_up(y_ref, NY, spot[1:2, :].astype(jnp.int32))
        lanes = spot.shape[1]
        place = slice(source * lanes, (source + 1) * lanes)
        for device in range(devices):
            row = (device * modes_here) // MZ
            y_cos, y_less = y_turn[row : row + 1, :], y_turn[MY + row : MY + row + 1, :]
            for parity in range(2):
                first = parity * half
                x_cos, x_less = x_turn[first : first + half], x_turn[MX + first : MX + first + half]
                both = jnp.concatenate(
                    [x_cos * y_cos - x_less * y_less, x_less * y_cos + x_cos * y_less], axis=0
                )
                base = (2 * device + parity) * MX
                phase_ref[base : base + MX, place] = both.astype(BF16)


def pair_spectrum_kernel(
    modes_here, got_ref, x_ref, y_ref, out_ref, phase_hbm_ref, phase_ref, sem_ref
):
    devices = got_ref.shape[0]
    rows = got_ref.shape[1] - 8
    tiles = out_ref.shape[1] // 128
    lanes = rows // tiles
    spots = [got_ref[source, rows : rows + 8, :] for source in range(devices)]
    fill_phases(modes_here, devices, spots, x_ref, y_ref, phase_ref)
    copy = pltpu.make_async_copy(phase_ref, phase_hbm_ref, sem_ref)
    copy.start()
    values = jnp.concatenate(
        [
            jnp.concatenate(
                [
                    got_ref[source, tile * lanes : (tile + 1) * lanes, :]
                    for source in range(devices)
                ],
                axis=0,
            )
            for tile in range(tiles)
        ],
        axis=1,
    )
    out_ref[...] = dot(phase_ref[...], values).astype(BF16)
    copy.wait()


def pair_spectrum(got, tables, modes_here, lanes):
    devices, rows, _ = got.shape
    count = devices * (rows - 8) // (lanes // 128)
    columns = devices * 2 * MX
    return pl.pallas_call(
        functools.partial(pair_spectrum_kernel, modes_here),
        out_shape=(
            jax.ShapeDtypeStruct((columns, lanes), BF16),
            pltpu.HBM((columns, count), BF16),
        ),
        in_specs=[vmem_spec()] * 3,
        out_specs=(vmem_spec(), any_spec()),
        scratch_shapes=[pltpu.VMEM((columns, count), BF16), pltpu.SemaphoreType.DMA],
        compiler_params=limit(10),
        cost_estimate=cost(2 * columns * count * lanes, got.size * 2 + columns * count * 2),
        name="pair_spectrum",
    )(got, *tables)


def row_of(wave, part):
    half = MX // 2
    order = list(x_waves() + half).index(wave)
    return order // half * MX + part * half + order % half


def mix_kernel(
    devices, number, got_ref, forward_ref, inverse_ref, weight_hbm_ref, out_ref, wide_ref,
    back_ref, weight_ref, sem_ref
):
    modes_here, _, channels, _ = weight_ref.shape
    each = MX // PARTS
    copies = [
        pltpu.make_async_copy(
            weight_hbm_ref.at[number, :, pl.ds(part * each, each)],
            weight_ref.at[:, pl.ds(part * each, each)],
            sem_ref.at[part],
        )
        for part in range(PARTS)
    ]
    for copy in copies:
        copy.start()
    local = got_ref.shape[1] // channels
    tiles = got_ref.shape[1] // 128
    group = 8
    for tile in range(tiles):
        wide_ref[tile] = got_ref[:, tile * 128 : (tile + 1) * 128].astype(F32)
    lane = lax.broadcasted_iota(jnp.int32, (2 * modes_here, 128), 1)
    row = lax.broadcasted_iota(jnp.int32, (2 * group, 128), 0)
    lane_small = lax.broadcasted_iota(jnp.int32, (2 * group, 128), 1)
    lane_back = lax.broadcasted_iota(jnp.int32, (2 * devices, 128), 1)
    forward = forward_ref[...]
    inverse = inverse_ref[...]
    spread = []
    for wave in range(MX):
        planes = jnp.concatenate(
            [
                jnp.concatenate(
                    [
                        wide_ref[tile, pl.ds(row_of(wave, part), devices, stride=2 * MX), :]
                        for part in range(2)
                    ],
                    axis=0,
                )
                for tile in range(tiles)
            ],
            axis=1,
        ).astype(BF16)
        turned = dot(forward, jnp.concatenate([planes, planes], axis=0))
        total = None
        for tile in range(tiles):
            part = slice(tile * 128, (tile + 1) * 128)
            size = 2 * modes_here
            even = turned[2 * tile * size : (2 * tile + 1) * size, part]
            odd = turned[(2 * tile + 1) * size : (2 * tile + 2) * size, part]
            both = even + pltpu.roll(odd, 64, 1)
            total = both if total is None else total + both
        spread.append(jnp.where(lane < 64, total, pltpu.roll(total, 64, 1)))
    mixed = []
    for wave in range(MX):
        pieces = []
        if wave % each == 0:
            copies[wave // each].wait()
        for first in range(0, modes_here, group):
            now = spread[wave][2 * first : 2 * (first + group), :]
            left = jnp.concatenate(
                [
                    jnp.where(row // 2 == 2 * step + lane_small // 64, now, 0.0)
                    for step in range(group // 2)
                ],
                axis=1,
            )
            left = jnp.concatenate(split(left), axis=0)
            right = weight_ref[first : first + group, wave, :, :].reshape(
                group * channels, 2 * channels
            )
            both = dot(left, right)
            pieces.append(both[0 : 2 * group] + both[2 * group :])
        mixed.append(pieces[0] if len(pieces) == 1 else jnp.concatenate(pieces, axis=0))
    for wave in range(MX):
        stacked = jnp.concatenate([mixed[wave], pltpu.roll(mixed[wave], 64, 1)], axis=0)
        upper, lower = split(stacked)
        count = upper.shape[0]
        planes = dot(inverse, jnp.concatenate([upper, upper], axis=0)) + dot(
            inverse[:, 0:count], lower
        )
        size = 2 * devices
        for tile in range(tiles):
            even = planes[2 * tile * size : (2 * tile + 1) * size, :]
            odd = planes[(2 * tile + 1) * size : (2 * tile + 2) * size, :]
            both = jnp.where(lane_back < 64, even, pltpu.roll(odd, 64, 1))
            for part in range(2):
                back_ref[tile, pl.ds(row_of(wave, part), devices, stride=2 * MX), :] = both[
                    part * devices : (part + 1) * devices
                ]
    for tile in range(tiles):
        out_ref[:, tile * 128 : (tile + 1) * 128] = back_ref[tile].astype(BF16)


def mix(got, forward, inverse, weights, number, devices):
    rows, lanes = got.shape
    return pl.pallas_call(
        functools.partial(mix_kernel, devices, number),
        out_shape=jax.ShapeDtypeStruct((rows, lanes), BF16),
        in_specs=[vmem_spec()] * 3 + [any_spec()],
        out_specs=vmem_spec(),
        scratch_shapes=[pltpu.VMEM((lanes // 128, rows, 128), F32)] * 2
        + [pltpu.VMEM(weights.shape[1:], BF16), pltpu.SemaphoreType.DMA((PARTS,))],
        compiler_params=limit(12),
        cost_estimate=cost(6e8, weights.size + rows * lanes * 4),
        name="mix",
    )(got, forward, inverse, in_hbm(weights))


def spread_weights(up_ref, down_ref, up_wide_ref, down_wide_ref):
    channels, hidden = up_ref.shape[1:]
    up = up_ref[0]
    down = (down_ref[0].astype(F32) * 0.5).astype(BF16).T
    up_wide_ref[...] = jnp.zeros_like(up_wide_ref)
    down_wide_ref[...] = jnp.zeros_like(down_wide_ref)
    for cell in range(2):
        here = slice(cell * channels, (cell + 1) * channels)
        there = slice(cell * hidden, (cell + 1) * hidden)
        up_wide_ref[here, there] = up
        down_wide_ref[there, here] = down


def gelu_twice(hidden):
    hidden = hidden.astype(BF16)
    first = jnp.asarray(GELU_K, BF16)
    third = jnp.asarray(GELU_K * 0.044715, BF16)
    return hidden * jnp.tanh(hidden * (first + third * (hidden * hidden))) + hidden


def mlp(summed, up_ref, down_ref):
    width = 256
    rounded = [each.astype(BF16) for each in summed]
    totals = list(summed)
    for first in range(0, up_ref.shape[1], width):
        hidden = [dot(each, up_ref[:, first : first + width]) for each in rounded]
        active = [gelu_twice(each) for each in hidden]
        for n, each in enumerate(active):
            totals[n] = totals[n] + dot(each, down_ref[first : first + width, :])
    return totals


def scatter_kernel(spot_ref, got_ref, out_hbm_ref, wide_ref, out_ref, sem_ref):
    devices, rows, _ = got_ref.shape
    rows = rows - 8
    pairs = spot_ref.shape[0] // devices
    size = rows // pairs
    tiles = TILES(out_ref)
    lines = size // tiles
    out_ref[...] = jnp.zeros_like(out_ref)
    for source in range(devices):
        for tile in range(tiles):
            for line in range(lines):
                first = (tile * lines + line) * pairs
                wide_ref[pl.ds(source * rows + line * tiles + tile, pairs, stride=size), :] = (
                    got_ref[source, first : first + pairs, :].astype(F32)
                )

    @pl.loop(0, devices)
    def _(source):
        for pair in range(pairs):
            base = pl.multiple_of(spot_ref[source * pairs + pair], size)
            here = pl.multiple_of(source * rows + pair * size, size)
            out_ref[pl.ds(base, size), :] = (
                out_ref[pl.ds(base, size), :] + wide_ref[pl.ds(here, size), :]
            )

    copy = pltpu.make_async_copy(out_ref, out_hbm_ref, sem_ref)
    copy.start()
    copy.wait()


def TILES(ref):
    return ref.shape[0] // (NX * NY)


def smem_spec():
    return pl.BlockSpec(memory_space=pltpu.SMEM)


def scatter(spots, got, tiles):
    devices, rows, _ = got.shape
    return pl.pallas_call(
        scatter_kernel,
        out_shape=pltpu.HBM((NX * NY * tiles, 128), F32),
        in_specs=[smem_spec(), vmem_spec()],
        out_specs=any_spec(),
        scratch_shapes=[
            pltpu.VMEM((devices * (rows - 8), 128), F32),
            pltpu.VMEM((NX * NY * tiles, 128), F32),
            pltpu.SemaphoreType.DMA,
        ],
        compiler_params=limit(14),
        cost_estimate=cost(1e6, NX * NY * tiles * 128 * 16),
        name="scatter",
    )(spots, got)


def gather_kernel(size, devices, spot_ref, grid_hbm_ref, out_ref, grid_ref, sem_ref):
    copy = pltpu.make_async_copy(grid_hbm_ref, grid_ref, sem_ref)
    copy.start()
    copy.wait()
    pairs = spot_ref.shape[0] // devices

    @pl.loop(0, devices)
    def _(source):
        for pair in range(pairs):
            base = pl.multiple_of(spot_ref[source * pairs + pair], size)
            here = pl.multiple_of(source * (pairs * size) + pair * size, size)
            out_ref[pl.ds(here, size), :] = grid_ref[pl.ds(base, size), :]


def gather(spots, grid, size, devices):
    count = spots.shape[0]
    return pl.pallas_call(
        functools.partial(gather_kernel, size, devices),
        out_shape=pltpu.VMEM((count * size, 128), F32),
        in_specs=[smem_spec(), any_spec()],
        out_specs=vmem_spec(),
        scratch_shapes=[pltpu.VMEM(grid.shape, F32), pltpu.SemaphoreType.DMA],
        compiler_params=limit(12),
        cost_estimate=cost(1e6, grid.size * 8),
        name="gather",
    )(spots, in_hbm(grid))


def layer_kernel(
    table_ref, flipped_ref, modes_ref, grid_ref, up_ref, down_ref, out_ref, spec_ref, total_ref,
    up_wide_ref, down_wide_ref, folded_ref
):
    step = pl.program_id(0)
    rows = table_ref.shape[0]
    tiles = modes_ref.shape[1] // 128
    count = table_ref.shape[1] // 2
    blocks = count // MX

    @pl.when(step == 0)
    def _():
        total_ref[...] = jnp.zeros_like(total_ref)
        spread_weights(up_ref, down_ref, up_wide_ref, down_wide_ref)
        for parity in range(2):
            for block in range(blocks):
                base = (2 * block + parity) * MX
                folded_ref[parity, block * MX : (block + 1) * MX, :] = modes_ref[base : base + MX]

    even = dot(table_ref[:, 0:count], folded_ref[0])
    odd = dot(table_ref[:, count:], folded_ref[1])
    halves = (even + odd, even - odd)
    places = [(side, tile) for side in range(2) for tile in range(tiles)]
    summed = [
        grid_ref[side, pl.ds(tile, rows, stride=tiles), :]
        + halves[side][:, tile * 128 : (tile + 1) * 128]
        for side, tile in places
    ]
    results = mlp(summed, up_wide_ref, down_wide_ref)
    for (side, tile), result in zip(places, results):
        out_ref[side, pl.ds(tile, rows, stride=tiles), :] = result
    low, high = results[0:tiles], results[tiles:]
    plus = jnp.concatenate([(a + b).astype(BF16) for a, b in zip(low, high)], axis=1)
    minus = jnp.concatenate([(a - b).astype(BF16) for a, b in zip(low, high)], axis=1)
    total_ref[0] += dot(flipped_ref[0:count, :], plus)
    total_ref[1] += dot(flipped_ref[count:, :], minus)

    @pl.when(step == pl.num_programs(0) - 1)
    def _():
        for parity in range(2):
            for block in range(blocks):
                base = (2 * block + parity) * MX
                spec_ref[base : base + MX, :] = total_ref[
                    parity, block * MX : (block + 1) * MX, :
                ].astype(BF16)


def weight_specs(up, down, number):
    return [
        pl.BlockSpec((1,) + up.shape[1:], lambda i: (number, 0, 0)),
        pl.BlockSpec((1,) + down.shape[1:], lambda i: (number, 0, 0)),
    ]


def wide_weights(up):
    channels, hidden = up.shape[1:]
    return [
        pltpu.VMEM((2 * channels, 2 * hidden), BF16),
        pltpu.VMEM((2 * hidden, 2 * channels), BF16),
    ]


def layer(table, flipped, modes, grid, up, down, number):
    cells, columns = table.shape
    lanes = modes.shape[1]
    tiles = lanes // 128
    rows = 512
    const = lambda i: (0, 0)
    return pl.pallas_call(
        layer_kernel,
        out_shape=(
            pltpu.HBM((2, cells * tiles, 128), F32),
            jax.ShapeDtypeStruct((columns, lanes), BF16),
        ),
        grid=(cells // rows,),
        in_specs=[
            pl.BlockSpec((rows, columns), lambda i: (i, 0)),
            pl.BlockSpec((columns, rows), lambda i: (0, i)),
            pl.BlockSpec((columns, lanes), const),
            pl.BlockSpec((2, rows * tiles, 128), lambda i: (0, i, 0)),
        ]
        + weight_specs(up, down, number),
        out_specs=(
            pl.BlockSpec((2, rows * tiles, 128), lambda i: (0, i, 0)),
            pl.BlockSpec((columns, lanes), const),
        ),
        scratch_shapes=[pltpu.VMEM((2, columns // 2, lanes), F32)]
        + wide_weights(up)
        + [pltpu.VMEM((2, columns // 2, lanes), BF16)],
        cost_estimate=cost(
            4 * cells * columns * lanes + 16 * cells * lanes * up.shape[2],
            cells * (columns * 4 + lanes * 8),
        ),
        compiler_params=limit(22),
        name="layer",
    )(
        in_hbm(table), in_hbm(flipped), modes, in_hbm(grid.reshape(2, cells * tiles, 128)),
        up, down,
    )


def last_kernel(lines, phase_ref, modes_ref, grid_ref, up_ref, down_ref, out_ref, up_wide_ref, down_wide_ref):
    group, rows, _ = out_ref.shape
    tiles = modes_ref.shape[1] // 128
    rows = rows // tiles

    @pl.when(pl.program_id(0) == 0)
    def _():
        spread_weights(up_ref, down_ref, up_wide_ref, down_wide_ref)

    spectral = lax.dot_general(
        phase_ref[...], modes_ref[...], (((0,), (0,)), ((), ())), preferred_element_type=F32
    )
    size = tiles * lines
    pairs = rows // lines
    summed = [
        jnp.concatenate(
            [
                grid_ref[
                    pl.ds(source * pairs * size + line * tiles + tile, pairs, stride=size), :
                ]
                for source in range(group)
                for line in range(lines)
            ],
            axis=0,
        )
        + spectral[:, tile * 128 : (tile + 1) * 128]
        for tile in range(tiles)
    ]
    results = mlp(summed, up_wide_ref, down_wide_ref)
    for tile, result in enumerate(results):
        result = result.astype(BF16)
        for source in range(group):
            out_ref[source, tile * rows : (tile + 1) * rows, :] = result[
                source * rows : (source + 1) * rows, :
            ]


def last_layer(phases, modes, grid, up, down, number, devices, lines):
    columns, count = phases.shape
    lanes = modes.shape[1]
    tiles = lanes // 128
    group = 8
    rows = count // devices
    return pl.pallas_call(
        functools.partial(last_kernel, lines),
        out_shape=jax.ShapeDtypeStruct((devices, rows * tiles, 128), BF16),
        grid=(devices // group,),
        in_specs=[
            pl.BlockSpec((columns, group * rows), lambda i: (0, i)),
            pl.BlockSpec((columns, lanes), lambda i: (0, 0)),
            pl.BlockSpec((group * rows * tiles, 128), lambda i: (i, 0)),
        ]
        + weight_specs(up, down, number),
        out_specs=pl.BlockSpec((group, rows * tiles, 128), lambda i: (i, 0, 0)),
        scratch_shapes=wide_weights(up),
        cost_estimate=cost(
            2 * count * columns * lanes + 16 * count * lanes * up.shape[2],
            count * (columns * 2 + lanes * 6),
        ),
        compiler_params=limit(24),
        name="last_layer",
    )(in_hbm(phases), modes, in_vmem(grid), up, down)


def exchange(values):
    return lax.all_to_all(values, "pen", split_axis=0, concat_axis=0, tiled=True)


def per_device(point_feat, pair_kernel, pair_owner, pair_block, spec_weight, mlp_up, mlp_down):
    devices = lax.axis_size("pen")
    pairs, block = pair_kernel.shape[0], pair_kernel.shape[1]
    channels = point_feat.shape[0]
    modes_here = spec_weight.shape[1]
    lines = block // NZ
    lanes = NZ // devices * channels
    tiles = lanes // 128
    columns = devices * 2 * MX

    up = mlp_up.transpose(0, 2, 1)
    send = encode(
        point_feat, pair_kernel, pair_owner.reshape(1, pairs), pair_block.reshape(1, pairs), devices
    )
    got = exchange(send)

    table, flipped = grid_tables(devices, modes_here)
    got, table, flipped = lax.optimization_barrier((got, table, flipped))
    forward, inverse = depth_tables(devices, modes_here)
    lookups = lookup_tables()
    here = got[:, -8:-6, 0:pairs].astype(jnp.int32)
    rows = ((here[:, 0, :] * NY + here[:, 1, :]) * tiles).reshape(devices * pairs)

    spectrum, phases = pair_spectrum(got, lookups, modes_here, lanes)
    grid = scatter(rows, got, tiles)
    modes = exchange(spectrum.reshape(devices, 2 * MX, lanes)).reshape(columns, lanes)
    modes = mix(modes, forward, inverse, spec_weight, 0, devices)
    modes = exchange(modes.reshape(devices, 2 * MX, lanes)).reshape(columns, lanes)
    grid, spectrum = layer(table, flipped, modes, grid, up, mlp_down, 0)
    listed = gather(rows, grid.reshape(-1, 128), lines * tiles, devices)
    modes = exchange(spectrum.reshape(devices, 2 * MX, lanes)).reshape(columns, lanes)
    modes = mix(modes, forward, inverse, spec_weight, 1, devices)
    modes = exchange(modes.reshape(devices, 2 * MX, lanes)).reshape(columns, lanes)
    result = last_layer(phases, modes, listed, up, mlp_down, 1, devices, lines)
    return decode(exchange(result), pair_kernel, channels)


def solution(mesh):
    in_specs = (
        P(None, ("groups", "pen")),
        P(("groups", "pen"), None, None),
        P(("groups", "pen"), None),
        P(("groups", "pen")),
        P(None, "pen", None, None, None),
        P(),
        P(),
    )
    out_specs = P(None, ("groups", "pen"))
    return jax.shard_map(
        per_device, mesh=mesh, in_specs=in_specs, out_specs=out_specs, check_vma=False
    )
```

```python
import functools
import math

import jax
import jax.numpy as jnp
import numpy as np
from jax import lax
from jax.experimental import pallas as pl
from jax.experimental.pallas import tpu as pltpu
from jax.sharding import PartitionSpec as P

NX = 128
NY = 64
NZ = 64
MX = 16
MY = 16
MZ = 16
LAYERS = 2
NBR = 4
GELU_K = math.sqrt(2.0 / math.pi)
SCALE = 1.66575
PAD = 8
PITCH = 2 * MX + PAD
PARTS = 4
LONG_PARTS = 2

F32 = jnp.float32
BF16 = jnp.bfloat16


def vmem_spec():
    return pl.BlockSpec(memory_space=pltpu.VMEM)


def in_vmem(values):
    return pltpu.with_memory_space_constraint(values, pltpu.VMEM)


def in_hbm(values):
    return pltpu.with_memory_space_constraint(values, pltpu.HBM)


def any_spec():
    return pl.BlockSpec(memory_space=pl.ANY)


def limit(mebibytes):
    return pltpu.CompilerParams(vmem_limit_bytes=mebibytes << 20)


def cost(flops, size, transcendentals=0):
    return pl.CostEstimate(
        flops=int(flops), bytes_accessed=int(size), transcendentals=int(transcendentals)
    )


def dot(left, right):
    return jnp.dot(left, right, preferred_element_type=F32)


def x_waves():
    wave = np.arange(MX) - MX // 2
    return np.concatenate([wave[wave % 2 == 0], wave[wave % 2 == 1]])


def y_waves(devices, modes_here):
    return (np.arange(devices) * modes_here) // MZ - MY // 2


def turn(wave, count):
    return 2.0 * np.pi / count * (np.arange(count)[:, None] * wave[None, :] % count)


def line_tables(devices, modes_here):
    size = 2 * MX * devices
    column = np.arange(size)
    half = MX // 2
    wave_x = x_waves()[column // (size // 2) * half + column % half]
    wave_y = y_waves(devices, modes_here)[column // MX % devices]
    part = column // half % 2
    x_angle = turn(wave_x, NX)[: NX // 2]
    y_angle = turn(wave_y, NY)
    x_cos, x_sin = SCALE * np.cos(x_angle), SCALE * np.sin(x_angle)
    first = np.where(part == 0, x_cos, -x_sin)
    second = np.where(part == 0, -x_sin, -x_cos)
    return [
        jnp.asarray(each.astype(np.float32))
        for each in (first, second, np.cos(y_angle), np.sin(y_angle))
    ]


def lookup_tables():
    result = []
    for wave, count, scale in ((x_waves(), NX, SCALE), (np.arange(MY) - MY // 2, NY, 1.0)):
        angle = turn(wave, count).T
        values = scale * np.concatenate([np.cos(angle), -np.sin(angle)])
        result.append(jnp.concatenate(split(jnp.asarray(values.astype(np.float32))), axis=0))
    return result


def split(values):
    high = values.astype(BF16)
    return high, (values - high.astype(F32)).astype(BF16)


def depth_tables(devices, modes_here):
    local = NZ // devices
    wave_z = np.arange(MZ).reshape(MZ // modes_here, modes_here)
    z_of = np.arange(devices)[None, :] + devices * np.arange(local)[:, None]
    angle = 2.0 * np.pi / NZ * (z_of[None, :, :, None] * wave_z[:, None, None, :] % NZ)
    cosine, sine = np.cos(angle), np.sin(angle)
    to_real = np.stack([cosine, sine], axis=-1)
    to_imag = np.stack([-sine, cosine], axis=-1)
    forward = np.stack([to_real, to_imag], axis=-2) / SCALE
    forward = forward.transpose(0, 1, 3, 4, 5, 2).reshape(
        -1, local * modes_here * 2, devices * 2
    )
    scale = np.where(wave_z == 0, 1.0, 2.0)[:, None, None, :] / (NX * NY * NZ * SCALE)
    cosine, sine = cosine * scale, sine * scale
    low = np.stack(
        [np.stack([cosine, -sine], axis=-1), np.stack([sine, cosine], axis=-1)], axis=2
    ).reshape(-1, local * devices * 2, modes_here * 2)
    high = np.stack(
        [np.stack([-sine, -cosine], axis=-1), np.stack([cosine, -sine], axis=-1)], axis=2
    ).reshape(-1, local * devices * 2, modes_here * 2)
    inverse = np.concatenate([low, high], axis=2)
    which = lax.axis_index("pen") * modes_here % MZ // modes_here
    chosen = []
    for table in (forward, inverse):
        table = jnp.asarray(table.astype(np.float32))
        chosen.append(table[0] if table.shape[0] == 1 else table[which])
    forward, inverse = chosen
    high, low = split(inverse)
    return (
        jnp.concatenate(split(forward), axis=1),
        jnp.concatenate([high, low, high], axis=1),
    )


def table_kernel(first_ref, second_ref, cos_ref, sin_ref, table_ref, flipped_ref):
    pieces = []
    for line in range(first_ref.shape[0]):
        piece = (
            first_ref[line : line + 1, :] * cos_ref[...]
            + second_ref[line : line + 1, :] * sin_ref[...]
        )
        pieces.append(piece.astype(BF16))
    whole = jnp.concatenate(pieces, axis=0)
    table_ref[...] = whole
    flipped_ref[...] = whole.T


def grid_tables(devices, modes_here):
    first, second, y_cos, y_sin = line_tables(devices, modes_here)
    columns = first.shape[1]
    lines = 8
    rows = lines * NY
    const = lambda i: (0, 0)
    return pl.pallas_call(
        table_kernel,
        out_shape=(
            pltpu.HBM((NX // 2 * NY, columns), BF16),
            pltpu.HBM((columns, NX // 2 * NY), BF16),
        ),
        grid=(NX // 2 // lines,),
        in_specs=[
            pl.BlockSpec((lines, columns), lambda i: (i, 0)),
            pl.BlockSpec((lines, columns), lambda i: (i, 0)),
            pl.BlockSpec((NY, columns), const),
            pl.BlockSpec((NY, columns), const),
        ],
        out_specs=(
            pl.BlockSpec((rows, columns), lambda i: (i, 0)),
            pl.BlockSpec((columns, rows), lambda i: (0, i)),
        ),
        cost_estimate=cost(4 * NX // 2 * NY * columns, 4 * NX // 2 * NY * columns),
        compiler_params=limit(8),
        name="tables",
    )(first, second, y_cos, y_sin)


def copies_of(from_ref, to_ref, sem_ref):
    step = from_ref.shape[0] // LONG_PARTS
    return [
        pltpu.make_async_copy(
            from_ref.at[pl.ds(part * step, step)],
            to_ref.at[pl.ds(part * step, step)],
            sem_ref.at[part],
        )
        for part in range(LONG_PARTS)
    ]


def encode_kernel(
    feature_hbm_ref, weight_hbm_ref, owner_hbm_ref, number_hbm_ref, out_hbm_ref, wide_ref,
    feature_ref, weight_ref, owner_ref, number_ref, out_ref, sem_ref, out_sem_ref
):
    devices = out_ref.shape[0]
    pairs, block = weight_ref.shape[0], weight_ref.shape[1]
    points = pairs // NBR
    lines = block // NZ
    tiles = NZ // devices // 2
    rows = tiles * pairs * lines
    copies = copies_of(weight_hbm_ref, weight_ref, sem_ref)
    small = [
        pltpu.make_async_copy(from_ref, to_ref, sem_ref.at[LONG_PARTS + place])
        for place, (from_ref, to_ref) in enumerate(
            (
                (owner_hbm_ref, owner_ref),
                (number_hbm_ref, number_ref),
                (feature_hbm_ref, feature_ref),
            )
        )
    ]
    for copy in small + copies:
        copy.start()
    for copy in small[0:2]:
        copy.wait()
    lane = lax.broadcasted_iota(jnp.int32, (devices, 128), 1)
    strip = NY // lines
    target = owner_ref[...] * (NX * strip // devices) + number_ref[...]
    y_at = (target % strip) * lines
    spots = jnp.concatenate(
        [
            jnp.concatenate([target // strip] * lines, axis=1),
            jnp.concatenate([y_at + line for line in range(lines)], axis=1),
            jnp.zeros((6, 128), jnp.int32),
        ],
        axis=0,
    )
    spots = spots.astype(F32).astype(BF16)
    for device in range(devices):
        out_ref[device, rows : rows + 8, :] = spots
    small[2].wait()

    def one(point, carry):
        features = feature_ref[:, pl.ds(pl.multiple_of(point * block, block), block)]
        features = jnp.concatenate([features, features], axis=0)
        for near in range(NBR):
            pair = point * NBR + near
            turned = lax.dot_general(
                weight_ref[pair], features, (((0,), (1,)), ((), ())), preferred_element_type=F32
            )
            for line in range(lines):
                for tile in range(tiles):
                    first = line * NZ + 2 * tile * devices
                    wide_ref[
                        pl.ds((tile * lines + line) * pairs + pair, devices, stride=rows + PAD), :
                    ] = jnp.where(
                        lane < 64,
                        turned[first : first + devices],
                        turned[first + devices : first + 2 * devices],
                    )
        return carry

    for part, copy in enumerate(copies):
        copy.wait()
        lax.fori_loop(
            part * points // LONG_PARTS, (part + 1) * points // LONG_PARTS, one, 0, unroll=points // LONG_PARTS
        )
    results = []
    for device in range(devices):
        base = device * (rows + PAD)
        out_ref[device, 0:rows, :] = wide_ref[base : base + rows, :].astype(BF16)
        results.append(
            pltpu.make_async_copy(
                out_ref.at[device], out_hbm_ref.at[device], out_sem_ref.at[device]
            )
        )
        results[-1].start()
    for result in results:
        result.wait()


def encode(features, weights, owners, numbers, devices):
    pairs, block = weights.shape[0], weights.shape[1]
    rows = NZ // devices // 2 * pairs * (block // NZ)
    return pl.pallas_call(
        encode_kernel,
        out_shape=pltpu.HBM((devices, rows + 8, 128), BF16),
        in_specs=[any_spec()] * 4,
        out_specs=any_spec(),
        scratch_shapes=[
            pltpu.VMEM((devices * (rows + PAD), 128), F32),
            pltpu.VMEM(features.shape, BF16),
            pltpu.VMEM(weights.shape, BF16),
            pltpu.VMEM(owners.shape, jnp.int32),
            pltpu.VMEM(numbers.shape, jnp.int32),
            pltpu.VMEM((devices, rows + 8, 128), BF16),
            pltpu.SemaphoreType.DMA((LONG_PARTS + 3,)),
            pltpu.SemaphoreType.DMA((devices,)),
        ],
        compiler_params=limit(10),
        cost_estimate=cost(4 * pairs * block * block * 64, pairs * block * block * 2),
        name="encode",
    )(in_hbm(features), in_hbm(weights), in_hbm(owners), in_hbm(numbers))


def decode_kernel(
    got_ref, weight_hbm_ref, out_hbm_ref, wide_ref, weight_ref, out_ref, sem_ref, out_sem_ref
):
    copies = copies_of(weight_hbm_ref, weight_ref, sem_ref)
    for copy in copies:
        copy.start()
    devices, rows, _ = got_ref.shape
    pairs, block = weight_ref.shape[0], weight_ref.shape[1]
    lines = block // NZ
    tiles = NZ // devices // 2
    lane = lax.broadcasted_iota(jnp.int32, (devices, 128), 1)
    for device in range(devices):
        base = device * (rows + PAD)
        wide_ref[base : base + rows, :] = got_ref[device].astype(F32)

    def one(point, carry):
        total = None
        for near in range(NBR):
            pair = point * NBR + near
            pieces = []
            for line in range(lines):
                for tile in range(tiles):
                    values = wide_ref[
                        pl.ds((tile * lines + line) * pairs + pair, devices, stride=rows + PAD), :
                    ]
                    pieces.append(jnp.where(lane < 64, values, 0.0))
                    pieces.append(jnp.where(lane < 64, 0.0, values))
            part = lax.dot_general(
                jnp.concatenate(pieces, axis=0).astype(BF16),
                weight_ref[pair],
                (((0,), (1,)), ((), ())),
                preferred_element_type=F32,
            )
            total = part if total is None else total + part
        out_ref[:, pl.ds(pl.multiple_of(point * block, block), block)] = (
            total[0:64, :] + total[64:128, :]
        )
        return carry

    points = pairs // NBR
    results = []
    for part, copy in enumerate(copies):
        copy.wait()
        lax.fori_loop(
            part * points // LONG_PARTS, (part + 1) * points // LONG_PARTS, one, 0, unroll=points // LONG_PARTS
        )
        place = pl.ds(part * points // LONG_PARTS * block, points // LONG_PARTS * block)
        results.append(
            pltpu.make_async_copy(
                out_ref.at[:, place], out_hbm_ref.at[:, place], out_sem_ref.at[part]
            )
        )
        results[-1].start()
    for result in results:
        result.wait()


def decode(got, weights, channels):
    devices, rows, _ = got.shape
    pairs, block = weights.shape[0], weights.shape[1]
    return pl.pallas_call(
        decode_kernel,
        out_shape=pltpu.HBM((channels, pairs // NBR * block), F32),
        in_specs=[vmem_spec(), any_spec()],
        out_specs=any_spec(),
        scratch_shapes=[
            pltpu.VMEM((devices * (rows + PAD), 128), F32),
            pltpu.VMEM(weights.shape, BF16),
            pltpu.VMEM((channels, pairs // NBR * block), F32),
            pltpu.SemaphoreType.DMA((LONG_PARTS,)),
            pltpu.SemaphoreType.DMA((LONG_PARTS,)),
        ],
        cost_estimate=cost(4 * pairs * block * block * 64, pairs * block * block * 2),
        compiler_params=limit(12),
        name="decode",
    )(got, in_hbm(weights))


def look_up(table_ref, count, spot):
    every = lax.broadcasted_iota(jnp.int32, (count, spot.shape[1]), 0)
    values = dot(table_ref[...], (every == spot).astype(F32).astype(BF16))
    half = values.shape[0] // 2
    return values[0:half] + values[half:]


def fill_phases(modes_here, devices, spots, x_ref, y_ref, phase_ref):
    half = MX // 2
    for source, spot in enumerate(spots):
        spot = spot.astype(F32)
        x_turn = look_up(x_ref, NX, spot[0:1, :].astype(jnp.int32))
        y_turn = look_up(y_ref, NY, spot[1:2, :].astype(jnp.int32))
        lanes = spot.shape[1]
        place = slice(source * lanes, (source + 1) * lanes)
        for device in range(devices):
            row = (device * modes_here) // MZ
            y_cos, y_less = y_turn[row : row + 1, :], y_turn[MY + row : MY + row + 1, :]
            for parity in range(2):
                first = parity * half
                x_cos, x_less = x_turn[first : first + half], x_turn[MX + first : MX + first + half]
                both = jnp.concatenate(
                    [x_cos * y_cos - x_less * y_less, x_less * y_cos + x_cos * y_less], axis=0
                )
                base = (2 * device + parity) * MX
                phase_ref[base : base + MX, place] = both.astype(BF16)


def pair_spectrum_kernel(
    modes_here, got_ref, x_ref, y_ref, out_ref, phase_ref
):
    devices = got_ref.shape[0]
    rows = got_ref.shape[1] - 8
    tiles = out_ref.shape[1] // 128
    lanes = rows // tiles
    spots = [got_ref[source, rows : rows + 8, :] for source in range(devices)]
    fill_phases(modes_here, devices, spots, x_ref, y_ref, phase_ref)
    values = jnp.concatenate(
        [
            jnp.concatenate(
                [
                    got_ref[source, tile * lanes : (tile + 1) * lanes, :]
                    for source in range(devices)
                ],
                axis=0,
            )
            for tile in range(tiles)
        ],
        axis=1,
    )
    out_ref[...] = dot(phase_ref[...], values).astype(BF16)


def pair_spectrum(got, tables, modes_here, lanes):
    devices, rows, _ = got.shape
    count = devices * (rows - 8) // (lanes // 128)
    columns = devices * 2 * MX
    return pl.pallas_call(
        functools.partial(pair_spectrum_kernel, modes_here),
        out_shape=jax.ShapeDtypeStruct((columns, lanes), BF16),
        in_specs=[vmem_spec()] * 3,
        out_specs=vmem_spec(),
        scratch_shapes=[pltpu.VMEM((columns, count), BF16)],
        compiler_params=limit(10),
        cost_estimate=cost(2 * columns * count * lanes, got.size * 2 + columns * count * 2),
        name="pair_spectrum",
    )(got, *tables)


def phase_kernel(modes_here, got_ref, x_ref, y_ref, out_hbm_ref, phase_ref, out_ref, sem_ref):
    devices = got_ref.shape[0]
    rows = got_ref.shape[1] - 8
    spots = [got_ref[source, rows : rows + 8, :] for source in range(devices)]
    fill_phases(modes_here, devices, spots, x_ref, y_ref, phase_ref)
    out_ref[...] = phase_ref[...].T
    copy = pltpu.make_async_copy(out_ref, out_hbm_ref, sem_ref)
    copy.start()
    copy.wait()


def pair_phases(got, tables, modes_here, lanes):
    devices, rows, _ = got.shape
    shape = (devices * 2 * MX, devices * (rows - 8) // (lanes // 128))
    return pl.pallas_call(
        functools.partial(phase_kernel, modes_here),
        out_shape=pltpu.HBM(shape[::-1], BF16),
        in_specs=[vmem_spec()] * 3,
        out_specs=any_spec(),
        scratch_shapes=[
            pltpu.VMEM(shape, BF16),
            pltpu.VMEM(shape[::-1], BF16),
            pltpu.SemaphoreType.DMA,
        ],
        compiler_params=limit((4 * shape[0] * shape[1] >> 20) + 6),
        cost_estimate=cost(1e6, got.size * 2 + shape[0] * shape[1] * 2),
        name="pair_phases",
    )(got, *tables)


def row_of(wave, part):
    half = MX // 2
    order = list(x_waves() + half).index(wave)
    return order // half * MX + part * half + order % half


def mix_kernel(
    devices, number, got_ref, forward_ref, inverse_ref, weight_hbm_ref, out_ref, wide_ref,
    back_ref, weight_ref, sem_ref
):
    modes_here, _, channels, _ = weight_ref.shape
    each = MX // PARTS
    copies = [
        pltpu.make_async_copy(
            weight_hbm_ref.at[number, :, pl.ds(part * each, each)],
            weight_ref.at[:, pl.ds(part * each, each)],
            sem_ref.at[part],
        )
        for part in range(PARTS)
    ]
    for copy in copies:
        copy.start()
    local = got_ref.shape[1] // channels
    tiles = got_ref.shape[1] // 128
    group = 8
    for tile in range(tiles):
        for device in range(devices):
            wide_ref[tile, device * PITCH : device * PITCH + 2 * MX, :] = got_ref[
                device * 2 * MX : (device + 1) * 2 * MX, tile * 128 : (tile + 1) * 128
            ].astype(F32)
    lane = lax.broadcasted_iota(jnp.int32, (2 * modes_here, 128), 1)
    row = lax.broadcasted_iota(jnp.int32, (2 * group, 128), 0)
    lane_small = lax.broadcasted_iota(jnp.int32, (2 * group, 128), 1)
    lane_back = lax.broadcasted_iota(jnp.int32, (2 * devices, 128), 1)
    forward = forward_ref[...]
    inverse = inverse_ref[...]
    spread = []
    for wave in range(MX):
        planes = jnp.concatenate(
            [
                jnp.concatenate(
                    [
                        wide_ref[tile, pl.ds(row_of(wave, part), devices, stride=PITCH), :]
                        for part in range(2)
                    ],
                    axis=0,
                )
                for tile in range(tiles)
            ],
            axis=1,
        ).astype(BF16)
        turned = dot(forward, jnp.concatenate([planes, planes], axis=0))
        total = None
        for tile in range(tiles):
            part = slice(tile * 128, (tile + 1) * 128)
            size = 2 * modes_here
            even = turned[2 * tile * size : (2 * tile + 1) * size, part]
            odd = turned[(2 * tile + 1) * size : (2 * tile + 2) * size, part]
            both = even + pltpu.roll(odd, 64, 1)
            total = both if total is None else total + both
        spread.append(jnp.where(lane < 64, total, pltpu.roll(total, 64, 1)))
    mixed = []
    for wave in range(MX):
        pieces = []
        if wave % each == 0:
            copies[wave // each].wait()
        for first in range(0, modes_here, group):
            now = spread[wave][2 * first : 2 * (first + group), :]
            left = jnp.concatenate(
                [
                    jnp.where(row // 2 == 2 * step + lane_small // 64, now, 0.0)
                    for step in range(group // 2)
                ],
                axis=1,
            )
            left = jnp.concatenate(split(left), axis=0)
            right = weight_ref[first : first + group, wave, :, :].reshape(
                group * channels, 2 * channels
            )
            both = dot(left, right)
            pieces.append(both[0 : 2 * group] + both[2 * group :])
        mixed.append(pieces[0] if len(pieces) == 1 else jnp.concatenate(pieces, axis=0))
    for wave in range(MX):
        stacked = jnp.concatenate([mixed[wave], pltpu.roll(mixed[wave], 64, 1)], axis=0)
        upper, lower = split(stacked)
        planes = dot(inverse, jnp.concatenate([upper, upper, lower], axis=0))
        size = 2 * devices
        for tile in range(tiles):
            even = planes[2 * tile * size : (2 * tile + 1) * size, :]
            odd = planes[(2 * tile + 1) * size : (2 * tile + 2) * size, :]
            both = jnp.where(lane_back < 64, even, pltpu.roll(odd, 64, 1))
            for part in range(2):
                back_ref[tile, pl.ds(row_of(wave, part), devices, stride=PITCH), :] = both[
                    part * devices : (part + 1) * devices
                ]
    for tile in range(tiles):
        for device in range(devices):
            out_ref[
                device * 2 * MX : (device + 1) * 2 * MX, tile * 128 : (tile + 1) * 128
            ] = back_ref[tile, device * PITCH : device * PITCH + 2 * MX, :].astype(BF16)


def mix(got, forward, inverse, weights, number, devices):
    rows, lanes = got.shape
    return pl.pallas_call(
        functools.partial(mix_kernel, devices, number),
        out_shape=jax.ShapeDtypeStruct((rows, lanes), BF16),
        in_specs=[vmem_spec()] * 3 + [any_spec()],
        out_specs=vmem_spec(),
        scratch_shapes=[pltpu.VMEM((lanes // 128, devices * PITCH, 128), F32)] * 2
        + [pltpu.VMEM(weights.shape[1:], BF16), pltpu.SemaphoreType.DMA((PARTS,))],
        compiler_params=limit(12),
        cost_estimate=cost(6e8, weights.size + rows * lanes * 4),
        name="mix",
    )(got, forward, inverse, in_hbm(weights))


def spread_weights(up_ref, down_ref, up_wide_ref, down_wide_ref):
    channels, hidden = up_ref.shape[1:]
    up = up_ref[0]
    down = (down_ref[0].astype(F32) * 0.5).astype(BF16).T
    up_wide_ref[...] = jnp.zeros_like(up_wide_ref)
    down_wide_ref[...] = jnp.zeros_like(down_wide_ref)
    for cell in range(2):
        here = slice(cell * channels, (cell + 1) * channels)
        there = slice(cell * hidden, (cell + 1) * hidden)
        up_wide_ref[here, there] = up
        down_wide_ref[there, here] = down


def gelu_twice(hidden):
    hidden = hidden.astype(BF16)
    first = jnp.asarray(GELU_K, BF16)
    third = jnp.asarray(GELU_K * 0.044715, BF16)
    return hidden * jnp.tanh(hidden * (first + third * (hidden * hidden))) + hidden


def mlp(summed, up_ref, down_ref):
    width = 256
    rounded = [each.astype(BF16) for each in summed]
    totals = list(summed)
    for first in range(0, up_ref.shape[1], width):
        hidden = [dot(each, up_ref[:, first : first + width]) for each in rounded]
        active = [gelu_twice(each) for each in hidden]
        for n, each in enumerate(active):
            totals[n] = totals[n] + dot(each, down_ref[first : first + width, :])
    return totals


def scatter_kernel(spot_ref, got_ref, out_hbm_ref, wide_ref, out_ref, sem_ref):
    devices, rows, _ = got_ref.shape
    rows = rows - 8
    pairs = spot_ref.shape[0] // devices
    size = rows // pairs
    tiles = TILES(out_ref)
    lines = size // tiles
    out_ref[...] = jnp.zeros_like(out_ref)
    for source in range(devices):
        for tile in range(tiles):
            for line in range(lines):
                first = (tile * lines + line) * pairs
                wide_ref[pl.ds(source * rows + line * tiles + tile, pairs, stride=size), :] = (
                    got_ref[source, first : first + pairs, :].astype(F32)
                )

    @pl.loop(0, devices)
    def _(source):
        for pair in range(pairs):
            base = pl.multiple_of(spot_ref[source * pairs + pair], size)
            here = pl.multiple_of(source * rows + pair * size, size)
            out_ref[pl.ds(base, size), :] = (
                out_ref[pl.ds(base, size), :] + wide_ref[pl.ds(here, size), :]
            )

    copy = pltpu.make_async_copy(out_ref, out_hbm_ref, sem_ref)
    copy.start()
    copy.wait()


def TILES(ref):
    return ref.shape[0] // (NX * NY)


def smem_spec():
    return pl.BlockSpec(memory_space=pltpu.SMEM)


def scatter(spots, got, tiles):
    devices, rows, _ = got.shape
    return pl.pallas_call(
        scatter_kernel,
        out_shape=pltpu.HBM((NX * NY * tiles, 128), F32),
        in_specs=[smem_spec(), vmem_spec()],
        out_specs=any_spec(),
        scratch_shapes=[
            pltpu.VMEM((devices * (rows - 8), 128), F32),
            pltpu.VMEM((NX * NY * tiles, 128), F32),
            pltpu.SemaphoreType.DMA,
        ],
        compiler_params=limit(14),
        cost_estimate=cost(1e6, NX * NY * tiles * 128 * 16),
        name="scatter",
    )(spots, got)


def gather_kernel(size, devices, spot_ref, grid_hbm_ref, out_ref, grid_ref, sem_ref):
    copy = pltpu.make_async_copy(grid_hbm_ref, grid_ref, sem_ref)
    copy.start()
    copy.wait()
    pairs = spot_ref.shape[0] // devices

    @pl.loop(0, devices)
    def _(source):
        for pair in range(pairs):
            base = pl.multiple_of(spot_ref[source * pairs + pair], size)
            here = pl.multiple_of(source * (pairs * size) + pair * size, size)
            out_ref[pl.ds(here, size), :] = grid_ref[pl.ds(base, size), :]


def gather(spots, grid, size, devices):
    count = spots.shape[0]
    return pl.pallas_call(
        functools.partial(gather_kernel, size, devices),
        out_shape=pltpu.VMEM((count * size, 128), F32),
        in_specs=[smem_spec(), any_spec()],
        out_specs=vmem_spec(),
        scratch_shapes=[pltpu.VMEM(grid.shape, F32), pltpu.SemaphoreType.DMA],
        compiler_params=limit(12),
        cost_estimate=cost(1e6, grid.size * 8),
        name="gather",
    )(spots, in_hbm(grid))


def layer_kernel(
    table_ref, flipped_ref, modes_ref, grid_ref, up_ref, down_ref, out_ref, spec_ref, total_ref,
    up_wide_ref, down_wide_ref, folded_ref
):
    step = pl.program_id(0)
    rows = table_ref.shape[0]
    tiles = modes_ref.shape[1] // 128
    count = table_ref.shape[1] // 2
    blocks = count // MX

    @pl.when(step == 0)
    def _():
        total_ref[...] = jnp.zeros_like(total_ref)
        spread_weights(up_ref, down_ref, up_wide_ref, down_wide_ref)
        for parity in range(2):
            for block in range(blocks):
                base = (2 * block + parity) * MX
                folded_ref[parity, block * MX : (block + 1) * MX, :] = modes_ref[base : base + MX]

    even = dot(table_ref[:, 0:count], folded_ref[0])
    odd = dot(table_ref[:, count:], folded_ref[1])
    halves = (even + odd, even - odd)
    places = [(side, tile) for side in range(2) for tile in range(tiles)]
    summed = [
        grid_ref[side, pl.ds(tile, rows, stride=tiles), :]
        + halves[side][:, tile * 128 : (tile + 1) * 128]
        for side, tile in places
    ]
    results = mlp(summed, up_wide_ref, down_wide_ref)
    for (side, tile), result in zip(places, results):
        out_ref[side, pl.ds(tile, rows, stride=tiles), :] = result
    low, high = results[0:tiles], results[tiles:]
    plus = jnp.concatenate([(a + b).astype(BF16) for a, b in zip(low, high)], axis=1)
    minus = jnp.concatenate([(a - b).astype(BF16) for a, b in zip(low, high)], axis=1)
    total_ref[0] += dot(flipped_ref[0:count, :], plus)
    total_ref[1] += dot(flipped_ref[count:, :], minus)

    @pl.when(step == pl.num_programs(0) - 1)
    def _():
        for parity in range(2):
            for block in range(blocks):
                base = (2 * block + parity) * MX
                spec_ref[base : base + MX, :] = total_ref[
                    parity, block * MX : (block + 1) * MX, :
                ].astype(BF16)


def weight_specs(up, down, number):
    return [
        pl.BlockSpec((1,) + up.shape[1:], lambda i: (number, 0, 0)),
        pl.BlockSpec((1,) + down.shape[1:], lambda i: (number, 0, 0)),
    ]


def wide_weights(up):
    channels, hidden = up.shape[1:]
    return [
        pltpu.VMEM((2 * channels, 2 * hidden), BF16),
        pltpu.VMEM((2 * hidden, 2 * channels), BF16),
    ]


def layer(table, flipped, modes, grid, up, down, number):
    cells, columns = table.shape
    lanes = modes.shape[1]
    tiles = lanes // 128
    rows = 512
    const = lambda i: (0, 0)
    return pl.pallas_call(
        layer_kernel,
        out_shape=(
            pltpu.HBM((2, cells * tiles, 128), F32),
            jax.ShapeDtypeStruct((columns, lanes), BF16),
        ),
        grid=(cells // rows,),
        in_specs=[
            pl.BlockSpec((rows, columns), lambda i: (i, 0)),
            pl.BlockSpec((columns, rows), lambda i: (0, i)),
            pl.BlockSpec((columns, lanes), const),
            pl.BlockSpec((2, rows * tiles, 128), lambda i: (0, i, 0)),
        ]
        + weight_specs(up, down, number),
        out_specs=(
            pl.BlockSpec((2, rows * tiles, 128), lambda i: (0, i, 0)),
            pl.BlockSpec((columns, lanes), const),
        ),
        scratch_shapes=[pltpu.VMEM((2, columns // 2, lanes), F32)]
        + wide_weights(up)
        + [pltpu.VMEM((2, columns // 2, lanes), BF16)],
        cost_estimate=cost(
            4 * cells * columns * lanes + 16 * cells * lanes * up.shape[2],
            cells * (columns * 4 + lanes * 8),
        ),
        compiler_params=limit(22),
        name="layer",
    )(
        in_hbm(table), in_hbm(flipped), modes, in_hbm(grid.reshape(2, cells * tiles, 128)),
        up, down,
    )


def last_kernel(lines, phase_ref, modes_ref, grid_ref, up_ref, down_ref, out_ref, up_wide_ref, down_wide_ref):
    group, rows, _ = out_ref.shape
    tiles = modes_ref.shape[1] // 128
    rows = rows // tiles

    @pl.when(pl.program_id(0) == 0)
    def _():
        spread_weights(up_ref, down_ref, up_wide_ref, down_wide_ref)

    spectral = dot(phase_ref[...], modes_ref[...])
    size = tiles * lines
    pairs = rows // lines
    summed = [
        jnp.concatenate(
            [
                grid_ref[
                    pl.ds(source * pairs * size + line * tiles + tile, pairs, stride=size), :
                ]
                for source in range(group)
                for line in range(lines)
            ],
            axis=0,
        )
        + spectral[:, tile * 128 : (tile + 1) * 128]
        for tile in range(tiles)
    ]
    results = mlp(summed, up_wide_ref, down_wide_ref)
    for tile, result in enumerate(results):
        result = result.astype(BF16)
        for source in range(group):
            out_ref[source, tile * rows : (tile + 1) * rows, :] = result[
                source * rows : (source + 1) * rows, :
            ]


def last_layer(phases, modes, grid, up, down, number, devices, lines):
    count, columns = phases.shape
    lanes = modes.shape[1]
    tiles = lanes // 128
    group = 8
    rows = count // devices
    return pl.pallas_call(
        functools.partial(last_kernel, lines),
        out_shape=jax.ShapeDtypeStruct((devices, rows * tiles, 128), BF16),
        grid=(devices // group,),
        in_specs=[
            pl.BlockSpec((group * rows, columns), lambda i: (i, 0)),
            pl.BlockSpec((columns, lanes), lambda i: (0, 0)),
            pl.BlockSpec((group * rows * tiles, 128), lambda i: (i, 0)),
        ]
        + weight_specs(up, down, number),
        out_specs=pl.BlockSpec((group, rows * tiles, 128), lambda i: (i, 0, 0)),
        scratch_shapes=wide_weights(up),
        cost_estimate=cost(
            2 * count * columns * lanes + 16 * count * lanes * up.shape[2],
            count * (columns * 2 + lanes * 6),
        ),
        compiler_params=limit(24),
        name="last_layer",
    )(in_hbm(phases), modes, in_vmem(grid), up, down)


def exchange(values):
    return lax.all_to_all(values, "pen", split_axis=0, concat_axis=0, tiled=True)


def per_device(point_feat, pair_kernel, pair_owner, pair_block, spec_weight, mlp_up, mlp_down):
    devices = lax.axis_size("pen")
    pairs, block = pair_kernel.shape[0], pair_kernel.shape[1]
    channels = point_feat.shape[0]
    modes_here = spec_weight.shape[1]
    lines = block // NZ
    lanes = NZ // devices * channels
    tiles = lanes // 128
    columns = devices * 2 * MX

    up = mlp_up.transpose(0, 2, 1)
    send = encode(
        point_feat, pair_kernel, pair_owner.reshape(1, pairs), pair_block.reshape(1, pairs), devices
    )
    got = exchange(send)

    table, flipped = grid_tables(devices, modes_here)
    got, table, flipped = lax.optimization_barrier((got, table, flipped))
    forward, inverse = depth_tables(devices, modes_here)
    lookups = lookup_tables()
    here = got[:, -8:-6, 0:pairs].astype(jnp.int32)
    rows = ((here[:, 0, :] * NY + here[:, 1, :]) * tiles).reshape(devices * pairs)

    spectrum = pair_spectrum(got, lookups, modes_here, lanes)
    phases = pair_phases(got, lookups, modes_here, lanes)
    grid = scatter(rows, got, tiles)
    modes = exchange(spectrum.reshape(devices, 2 * MX, lanes)).reshape(columns, lanes)
    modes = mix(modes, forward, inverse, spec_weight, 0, devices)
    modes = exchange(modes.reshape(devices, 2 * MX, lanes)).reshape(columns, lanes)
    grid, spectrum = layer(table, flipped, modes, grid, up, mlp_down, 0)
    listed = gather(rows, grid.reshape(-1, 128), lines * tiles, devices)
    modes = exchange(spectrum.reshape(devices, 2 * MX, lanes)).reshape(columns, lanes)
    modes = mix(modes, forward, inverse, spec_weight, 1, devices)
    modes = exchange(modes.reshape(devices, 2 * MX, lanes)).reshape(columns, lanes)
    result = last_layer(phases, modes, listed, up, mlp_down, 1, devices, lines)
    return decode(exchange(result), pair_kernel, channels)


def solution(mesh):
    in_specs = (
        P(None, ("groups", "pen")),
        P(("groups", "pen"), None, None),
        P(("groups", "pen"), None),
        P(("groups", "pen")),
        P(None, "pen", None, None, None),
        P(),
        P(),
    )
    out_specs = P(None, ("groups", "pen"))
    return jax.shard_map(
        per_device, mesh=mesh, in_specs=in_specs, out_specs=out_specs, check_vma=False
    )
```

```python
import functools
import math

import jax
import jax.numpy as jnp
import numpy as np
from jax import lax
from jax.experimental import pallas as pl
from jax.experimental.pallas import tpu as pltpu
from jax.sharding import PartitionSpec as P


NX = 128
NY = 64
NZ = 64
MX = 16
MY = 16
MZ = 16
NBR = 4
GELU_K = math.sqrt(2.0 / math.pi)
SCALE = 1.66575
PAD = 8
PITCH = 2 * MX + PAD
PARTS = 4
LONG_PARTS = 2

F32 = jnp.float32
BF16 = jnp.bfloat16


def vmem_spec():
    return pl.BlockSpec(memory_space=pltpu.VMEM)


def in_vmem(values):
    return pltpu.with_memory_space_constraint(values, pltpu.VMEM)


def in_hbm(values):
    return pltpu.with_memory_space_constraint(values, pltpu.HBM)


def any_spec():
    return pl.BlockSpec(memory_space=pl.ANY)


def limit(mebibytes):
    return pltpu.CompilerParams(vmem_limit_bytes=mebibytes << 20)


def cost(flops, size, transcendentals=0):
    return pl.CostEstimate(
        flops=int(flops), bytes_accessed=int(size), transcendentals=int(transcendentals)
    )


def dot(left, right):
    return jnp.dot(left, right, preferred_element_type=F32)


def x_waves():
    wave = np.arange(MX) - MX // 2
    return np.concatenate([wave[wave % 2 == 0], wave[wave % 2 == 1]])


def y_waves(devices, modes_here):
    return (np.arange(devices) * modes_here) // MZ - MY // 2


def turn(wave, count):
    return 2.0 * np.pi / count * (np.arange(count)[:, None] * wave[None, :] % count)


def line_tables(devices, modes_here):
    size = 2 * MX * devices
    column = np.arange(size)
    half = MX // 2
    wave_x = x_waves()[column // (size // 2) * half + column % half]
    wave_y = y_waves(devices, modes_here)[column // MX % devices]
    part = column // half % 2
    x_angle = turn(wave_x, NX)[: NX // 2]
    y_angle = turn(wave_y, NY)
    x_cos, x_sin = SCALE * np.cos(x_angle), SCALE * np.sin(x_angle)
    first = np.where(part == 0, x_cos, -x_sin)
    second = np.where(part == 0, -x_sin, -x_cos)
    return [
        jnp.asarray(each.astype(np.float32))
        for each in (first, second, np.cos(y_angle), np.sin(y_angle))
    ]


def lookup_tables():
    result = []
    for wave, count, scale in ((x_waves(), NX, SCALE), (np.arange(MY) - MY // 2, NY, 1.0)):
        angle = turn(wave, count).T
        values = scale * np.concatenate([np.cos(angle), -np.sin(angle)])
        result.append(jnp.concatenate(split(jnp.asarray(values.astype(np.float32))), axis=0))
    return result


def split(values):
    high = values.astype(BF16)
    return high, (values - high.astype(F32)).astype(BF16)


def depth_tables(devices, modes_here):
    local = NZ // devices
    wave_z = np.arange(MZ).reshape(MZ // modes_here, modes_here)
    z_of = np.arange(devices)[None, :] + devices * np.arange(local)[:, None]
    angle = 2.0 * np.pi / NZ * (z_of[None, :, :, None] * wave_z[:, None, None, :] % NZ)
    cosine, sine = np.cos(angle), np.sin(angle)
    to_real = np.stack([cosine, sine], axis=-1)
    to_imag = np.stack([-sine, cosine], axis=-1)
    forward = np.stack([to_real, to_imag], axis=-2) / SCALE
    forward = forward.transpose(0, 1, 3, 4, 5, 2).reshape(
        -1, local * modes_here * 2, devices * 2
    )
    scale = np.where(wave_z == 0, 1.0, 2.0)[:, None, None, :] / (NX * NY * NZ * SCALE)
    cosine, sine = cosine * scale, sine * scale
    low = np.stack(
        [np.stack([cosine, -sine], axis=-1), np.stack([sine, cosine], axis=-1)], axis=2
    ).reshape(-1, local * devices * 2, modes_here * 2)
    high = np.stack(
        [np.stack([-sine, -cosine], axis=-1), np.stack([cosine, -sine], axis=-1)], axis=2
    ).reshape(-1, local * devices * 2, modes_here * 2)
    inverse = np.concatenate([low, high], axis=2)
    which = lax.axis_index("pen") * modes_here % MZ // modes_here
    chosen = []
    for table in (forward, inverse):
        table = jnp.asarray(table.astype(np.float32))
        chosen.append(table[0] if table.shape[0] == 1 else table[which])
    forward, inverse = chosen
    high, low = split(inverse)
    return (
        jnp.concatenate(split(forward), axis=1),
        jnp.concatenate([high, low, high], axis=1),
    )


def table_kernel(first_ref, second_ref, cos_ref, sin_ref, table_ref, flipped_ref):
    pieces = []
    for line in range(first_ref.shape[0]):
        piece = (
            first_ref[line : line + 1, :] * cos_ref[...]
            + second_ref[line : line + 1, :] * sin_ref[...]
        )
        pieces.append(piece.astype(BF16))
    whole = jnp.concatenate(pieces, axis=0)
    table_ref[...] = whole
    flipped_ref[...] = whole.T


def grid_tables(devices, modes_here):
    first, second, y_cos, y_sin = line_tables(devices, modes_here)
    columns = first.shape[1]
    lines = 8
    rows = lines * NY
    const = lambda i: (0, 0)
    return pl.pallas_call(
        table_kernel,
        out_shape=(
            pltpu.HBM((NX // 2 * NY, columns), BF16),
            pltpu.HBM((columns, NX // 2 * NY), BF16),
        ),
        grid=(NX // 2 // lines,),
        in_specs=[
            pl.BlockSpec((lines, columns), lambda i: (i, 0)),
            pl.BlockSpec((lines, columns), lambda i: (i, 0)),
            pl.BlockSpec((NY, columns), const),
            pl.BlockSpec((NY, columns), const),
        ],
        out_specs=(
            pl.BlockSpec((rows, columns), lambda i: (i, 0)),
            pl.BlockSpec((columns, rows), lambda i: (0, i)),
        ),
        cost_estimate=cost(4 * NX // 2 * NY * columns, 4 * NX // 2 * NY * columns),
        compiler_params=limit(8),
        name="tables",
    )(first, second, y_cos, y_sin)


def copies_of(from_ref, to_ref, sem_ref):
    step = from_ref.shape[0] // LONG_PARTS
    return [
        pltpu.make_async_copy(
            from_ref.at[pl.ds(part * step, step)],
            to_ref.at[pl.ds(part * step, step)],
            sem_ref.at[part],
        )
        for part in range(LONG_PARTS)
    ]


def encode_kernel(
    feature_hbm_ref, weight_hbm_ref, owner_hbm_ref, number_hbm_ref, out_hbm_ref, wide_ref,
    feature_ref, weight_ref, owner_ref, number_ref, out_ref, sem_ref, out_sem_ref
):
    devices = out_ref.shape[0]
    pairs, block = weight_ref.shape[0], weight_ref.shape[1]
    points = pairs // NBR
    lines = block // NZ
    tiles = NZ // devices // 2
    rows = tiles * pairs * lines
    copies = copies_of(weight_hbm_ref, weight_ref, sem_ref)
    small = [
        pltpu.make_async_copy(from_ref, to_ref, sem_ref.at[LONG_PARTS + place])
        for place, (from_ref, to_ref) in enumerate(
            (
                (owner_hbm_ref, owner_ref),
                (number_hbm_ref, number_ref),
                (feature_hbm_ref, feature_ref),
            )
        )
    ]
    for copy in small + copies:
        copy.start()
    for copy in small[0:2]:
        copy.wait()
    lane = lax.broadcasted_iota(jnp.int32, (devices, 128), 1)
    strip = NY // lines
    target = owner_ref[...] * (NX * strip // devices) + number_ref[...]
    y_at = (target % strip) * lines
    spots = jnp.concatenate(
        [
            jnp.concatenate([target // strip] * lines, axis=1),
            jnp.concatenate([y_at + line for line in range(lines)], axis=1),
            jnp.zeros((6, 128), jnp.int32),
        ],
        axis=0,
    )
    spots = spots.astype(F32).astype(BF16)
    for device in range(devices):
        out_ref[device, rows : rows + 8, :] = spots
    small[2].wait()

    def one(point, carry):
        features = feature_ref[:, pl.ds(pl.multiple_of(point * block, block), block)]
        features = jnp.concatenate([features, features], axis=0)
        for near in range(NBR):
            pair = point * NBR + near
            turned = lax.dot_general(
                weight_ref[pair], features, (((0,), (1,)), ((), ())), preferred_element_type=F32
            )
            for line in range(lines):
                for tile in range(tiles):
                    first = line * NZ + 2 * tile * devices
                    wide_ref[
                        pl.ds((tile * lines + line) * pairs + pair, devices, stride=rows + PAD), :
                    ] = jnp.where(
                        lane < 64,
                        turned[first : first + devices],
                        turned[first + devices : first + 2 * devices],
                    )
        return carry

    for part, copy in enumerate(copies):
        copy.wait()
        lax.fori_loop(
            part * points // LONG_PARTS, (part + 1) * points // LONG_PARTS, one, 0, unroll=points // LONG_PARTS
        )
    results = []
    for device in range(devices):
        base = device * (rows + PAD)
        out_ref[device, 0:rows, :] = wide_ref[base : base + rows, :].astype(BF16)
        results.append(
            pltpu.make_async_copy(
                out_ref.at[device], out_hbm_ref.at[device], out_sem_ref.at[device]
            )
        )
        results[-1].start()
    for result in results:
        result.wait()


def encode(features, weights, owners, numbers, devices):
    pairs, block = weights.shape[0], weights.shape[1]
    rows = NZ // devices // 2 * pairs * (block // NZ)
    return pl.pallas_call(
        encode_kernel,
        out_shape=pltpu.HBM((devices, rows + 8, 128), BF16),
        in_specs=[any_spec()] * 4,
        out_specs=any_spec(),
        scratch_shapes=[
            pltpu.VMEM((devices * (rows + PAD), 128), F32),
            pltpu.VMEM(features.shape, BF16),
            pltpu.VMEM(weights.shape, BF16),
            pltpu.VMEM(owners.shape, jnp.int32),
            pltpu.VMEM(numbers.shape, jnp.int32),
            pltpu.VMEM((devices, rows + 8, 128), BF16),
            pltpu.SemaphoreType.DMA((LONG_PARTS + 3,)),
            pltpu.SemaphoreType.DMA((devices,)),
        ],
        compiler_params=limit(10),
        cost_estimate=cost(4 * pairs * block * block * 64, pairs * block * block * 2),
        name="encode",
    )(in_hbm(features), in_hbm(weights), in_hbm(owners), in_hbm(numbers))


def decode_kernel(
    got_ref, weight_hbm_ref, out_hbm_ref, wide_ref, weight_ref, out_ref, sem_ref, out_sem_ref
):
    copies = copies_of(weight_hbm_ref, weight_ref, sem_ref)
    for copy in copies:
        copy.start()
    devices, rows, _ = got_ref.shape
    pairs, block = weight_ref.shape[0], weight_ref.shape[1]
    lines = block // NZ
    tiles = NZ // devices // 2
    lane = lax.broadcasted_iota(jnp.int32, (devices, 128), 1)
    for device in range(devices):
        base = device * (rows + PAD)
        wide_ref[base : base + rows, :] = got_ref[device].astype(F32)

    def one(point, carry):
        pieces = []
        for near in range(NBR):
            pair = point * NBR + near
            for line in range(lines):
                for tile in range(tiles):
                    values = wide_ref[
                        pl.ds((tile * lines + line) * pairs + pair, devices, stride=rows + PAD), :
                    ]
                    pieces.append(jnp.where(lane < 64, values, 0.0))
                    pieces.append(jnp.where(lane < 64, 0.0, values))
        total = dot(
            jnp.concatenate([weight_ref[point * NBR + near] for near in range(NBR)], axis=1),
            jnp.concatenate(pieces, axis=0).astype(BF16),
        )
        total = (total + pltpu.roll(total, 64, 1)).T
        out_ref[:, pl.ds(pl.multiple_of(point * block, block), block)] = total[0:64, :]
        return carry

    points = pairs // NBR
    results = []
    for part, copy in enumerate(copies):
        copy.wait()
        lax.fori_loop(
            part * points // LONG_PARTS, (part + 1) * points // LONG_PARTS, one, 0, unroll=points // LONG_PARTS
        )
        place = pl.ds(part * points // LONG_PARTS * block, points // LONG_PARTS * block)
        results.append(
            pltpu.make_async_copy(
                out_ref.at[:, place], out_hbm_ref.at[:, place], out_sem_ref.at[part]
            )
        )
        results[-1].start()
    for result in results:
        result.wait()


def decode(got, weights, channels):
    devices, rows, _ = got.shape
    pairs, block = weights.shape[0], weights.shape[1]
    return pl.pallas_call(
        decode_kernel,
        out_shape=pltpu.HBM((channels, pairs // NBR * block), F32),
        in_specs=[vmem_spec(), any_spec()],
        out_specs=any_spec(),
        scratch_shapes=[
            pltpu.VMEM((devices * (rows + PAD), 128), F32),
            pltpu.VMEM(weights.shape, BF16),
            pltpu.VMEM((channels, pairs // NBR * block), F32),
            pltpu.SemaphoreType.DMA((LONG_PARTS,)),
            pltpu.SemaphoreType.DMA((LONG_PARTS,)),
        ],
        cost_estimate=cost(4 * pairs * block * block * 64, pairs * block * block * 2),
        compiler_params=limit(12),
        name="decode",
    )(got, in_hbm(weights))


def look_up(table_ref, count, spot):
    every = lax.broadcasted_iota(jnp.int32, (count, spot.shape[1]), 0)
    values = dot(table_ref[...], (every == spot).astype(F32).astype(BF16))
    half = values.shape[0] // 2
    return values[0:half] + values[half:]


def fill_phases(modes_here, devices, spots, x_ref, y_ref, phase_ref):
    half = MX // 2
    for source, spot in enumerate(spots):
        spot = spot.astype(F32)
        x_turn = look_up(x_ref, NX, spot[0:1, :].astype(jnp.int32))
        y_turn = look_up(y_ref, NY, spot[1:2, :].astype(jnp.int32))
        lanes = spot.shape[1]
        place = slice(source * lanes, (source + 1) * lanes)
        for device in range(devices):
            row = (device * modes_here) // MZ
            y_cos, y_less = y_turn[row : row + 1, :], y_turn[MY + row : MY + row + 1, :]
            for parity in range(2):
                first = parity * half
                x_cos, x_less = x_turn[first : first + half], x_turn[MX + first : MX + first + half]
                both = jnp.concatenate(
                    [x_cos * y_cos - x_less * y_less, x_less * y_cos + x_cos * y_less], axis=0
                )
                base = (2 * device + parity) * MX
                phase_ref[base : base + MX, place] = both.astype(BF16)


def pair_spectrum_kernel(
    modes_here, got_ref, x_ref, y_ref, out_ref, phase_ref
):
    devices = got_ref.shape[0]
    rows = got_ref.shape[1] - 8
    tiles = out_ref.shape[1] // 128
    lanes = rows // tiles
    spots = [got_ref[source, rows : rows + 8, :] for source in range(devices)]
    fill_phases(modes_here, devices, spots, x_ref, y_ref, phase_ref)
    values = jnp.concatenate(
        [
            jnp.concatenate(
                [
                    got_ref[source, tile * lanes : (tile + 1) * lanes, :]
                    for source in range(devices)
                ],
                axis=0,
            )
            for tile in range(tiles)
        ],
        axis=1,
    )
    out_ref[...] = dot(phase_ref[...], values).astype(BF16)


def pair_spectrum(got, tables, modes_here, lanes):
    devices, rows, _ = got.shape
    count = devices * (rows - 8) // (lanes // 128)
    columns = devices * 2 * MX
    return pl.pallas_call(
        functools.partial(pair_spectrum_kernel, modes_here),
        out_shape=jax.ShapeDtypeStruct((columns, lanes), BF16),
        in_specs=[vmem_spec()] * 3,
        out_specs=vmem_spec(),
        scratch_shapes=[pltpu.VMEM((columns, count), BF16)],
        compiler_params=limit(10),
        cost_estimate=cost(2 * columns * count * lanes, got.size * 2 + columns * count * 2),
        name="pair_spectrum",
    )(got, *tables)


def phase_kernel(modes_here, got_ref, x_ref, y_ref, out_hbm_ref, phase_ref, out_ref, sem_ref):
    devices = got_ref.shape[0]
    rows = got_ref.shape[1] - 8
    spots = [got_ref[source, rows : rows + 8, :] for source in range(devices)]
    fill_phases(modes_here, devices, spots, x_ref, y_ref, phase_ref)
    out_ref[...] = phase_ref[...].T
    copy = pltpu.make_async_copy(out_ref, out_hbm_ref, sem_ref)
    copy.start()
    copy.wait()


def pair_phases(got, tables, modes_here, lanes):
    devices, rows, _ = got.shape
    shape = (devices * 2 * MX, devices * (rows - 8) // (lanes // 128))
    return pl.pallas_call(
        functools.partial(phase_kernel, modes_here),
        out_shape=pltpu.HBM(shape[::-1], BF16),
        in_specs=[vmem_spec()] * 3,
        out_specs=any_spec(),
        scratch_shapes=[
            pltpu.VMEM(shape, BF16),
            pltpu.VMEM(shape[::-1], BF16),
            pltpu.SemaphoreType.DMA,
        ],
        compiler_params=limit((4 * shape[0] * shape[1] >> 20) + 6),
        cost_estimate=cost(1e6, got.size * 2 + shape[0] * shape[1] * 2),
        name="pair_phases",
    )(got, *tables)


def row_of(wave, part):
    half = MX // 2
    order = list(x_waves() + half).index(wave)
    return order // half * MX + part * half + order % half


def mix_kernel(
    devices, number, got_ref, forward_ref, inverse_ref, weight_hbm_ref, out_ref, wide_ref,
    back_ref, weight_ref, sem_ref
):
    modes_here, _, channels, _ = weight_ref.shape
    each = MX // PARTS
    copies = [
        pltpu.make_async_copy(
            weight_hbm_ref.at[number, :, pl.ds(part * each, each)],
            weight_ref.at[:, pl.ds(part * each, each)],
            sem_ref.at[part],
        )
        for part in range(PARTS)
    ]
    for copy in copies:
        copy.start()
    tiles = got_ref.shape[1] // 128
    group = 8
    for tile in range(tiles):
        for device in range(devices):
            wide_ref[tile, device * PITCH : device * PITCH + 2 * MX, :] = got_ref[
                device * 2 * MX : (device + 1) * 2 * MX, tile * 128 : (tile + 1) * 128
            ].astype(F32)
    lane = lax.broadcasted_iota(jnp.int32, (2 * modes_here, 128), 1)
    row = lax.broadcasted_iota(jnp.int32, (2 * group, 128), 0)
    lane_small = lax.broadcasted_iota(jnp.int32, (2 * group, 128), 1)
    lane_back = lax.broadcasted_iota(jnp.int32, (2 * devices, 128), 1)
    forward = forward_ref[...]
    inverse = inverse_ref[...]
    spread = []
    for wave in range(MX):
        planes = jnp.concatenate(
            [
                jnp.concatenate(
                    [
                        wide_ref[tile, pl.ds(row_of(wave, part), devices, stride=PITCH), :]
                        for part in range(2)
                    ],
                    axis=0,
                )
                for tile in range(tiles)
            ],
            axis=1,
        ).astype(BF16)
        turned = dot(forward, jnp.concatenate([planes, planes], axis=0))
        total = None
        for tile in range(tiles):
            part = slice(tile * 128, (tile + 1) * 128)
            size = 2 * modes_here
            even = turned[2 * tile * size : (2 * tile + 1) * size, part]
            odd = turned[(2 * tile + 1) * size : (2 * tile + 2) * size, part]
            both = even + pltpu.roll(odd, 64, 1)
            total = both if total is None else total + both
        spread.append(jnp.where(lane < 64, total, pltpu.roll(total, 64, 1)))
    mixed = []
    for wave in range(MX):
        pieces = []
        if wave % each == 0:
            copies[wave // each].wait()
        for first in range(0, modes_here, group):
            now = spread[wave][2 * first : 2 * (first + group), :]
            left = jnp.concatenate(
                [
                    jnp.where(row // 2 == 2 * step + lane_small // 64, now, 0.0)
                    for step in range(group // 2)
                ],
                axis=1,
            )
            left = jnp.concatenate(split(left), axis=0)
            right = weight_ref[first : first + group, wave, :, :].reshape(
                group * channels, 2 * channels
            )
            both = dot(left, right)
            pieces.append(both[0 : 2 * group] + both[2 * group :])
        mixed.append(pieces[0] if len(pieces) == 1 else jnp.concatenate(pieces, axis=0))
    for wave in range(MX):
        stacked = jnp.concatenate([mixed[wave], pltpu.roll(mixed[wave], 64, 1)], axis=0)
        upper, lower = split(stacked)
        planes = dot(inverse, jnp.concatenate([upper, upper, lower], axis=0))
        size = 2 * devices
        for tile in range(tiles):
            even = planes[2 * tile * size : (2 * tile + 1) * size, :]
            odd = planes[(2 * tile + 1) * size : (2 * tile + 2) * size, :]
            both = jnp.where(lane_back < 64, even, pltpu.roll(odd, 64, 1))
            for part in range(2):
                back_ref[tile, pl.ds(row_of(wave, part), devices, stride=PITCH), :] = both[
                    part * devices : (part + 1) * devices
                ]
    for tile in range(tiles):
        for device in range(devices):
            out_ref[
                device * 2 * MX : (device + 1) * 2 * MX, tile * 128 : (tile + 1) * 128
            ] = back_ref[tile, device * PITCH : device * PITCH + 2 * MX, :].astype(BF16)


def mix(got, forward, inverse, weights, number, devices):
    rows, lanes = got.shape
    return pl.pallas_call(
        functools.partial(mix_kernel, devices, number),
        out_shape=jax.ShapeDtypeStruct((rows, lanes), BF16),
        in_specs=[vmem_spec()] * 3 + [any_spec()],
        out_specs=vmem_spec(),
        scratch_shapes=[pltpu.VMEM((lanes // 128, devices * PITCH, 128), F32)] * 2
        + [pltpu.VMEM(weights.shape[1:], BF16), pltpu.SemaphoreType.DMA((PARTS,))],
        compiler_params=limit(12),
        cost_estimate=cost(6e8, weights.size + rows * lanes * 4),
        name="mix",
    )(got, forward, inverse, in_hbm(weights))


def spread_weights(up_ref, down_ref, up_wide_ref, down_wide_ref):
    channels, hidden = up_ref.shape[1:]
    up = up_ref[0]
    down = (down_ref[0].astype(F32) * 0.5).astype(BF16).T
    up_wide_ref[...] = jnp.zeros_like(up_wide_ref)
    down_wide_ref[...] = jnp.zeros_like(down_wide_ref)
    for cell in range(2):
        here = slice(cell * channels, (cell + 1) * channels)
        there = slice(cell * hidden, (cell + 1) * hidden)
        up_wide_ref[here, there] = up
        down_wide_ref[there, here] = down


def gelu_twice(hidden):
    hidden = hidden.astype(BF16)
    first = jnp.asarray(GELU_K, BF16)
    third = jnp.asarray(GELU_K * 0.044715, BF16)
    return hidden * jnp.tanh(hidden * (first + third * (hidden * hidden))) + hidden


def mlp(summed, up_ref, down_ref):
    width = 256
    rounded = [each.astype(BF16) for each in summed]
    totals = list(summed)
    for first in range(0, up_ref.shape[1], width):
        hidden = [dot(each, up_ref[:, first : first + width]) for each in rounded]
        active = [gelu_twice(each) for each in hidden]
        for n, each in enumerate(active):
            totals[n] = totals[n] + dot(each, down_ref[first : first + width, :])
    return totals


def scatter_kernel(spot_ref, got_ref, out_hbm_ref, wide_ref, out_ref, sem_ref):
    devices, rows, _ = got_ref.shape
    rows = rows - 8
    pairs = spot_ref.shape[0] // devices
    size = rows // pairs
    tiles = TILES(out_ref)
    lines = size // tiles
    out_ref[...] = jnp.zeros_like(out_ref)
    for source in range(devices):
        for tile in range(tiles):
            for line in range(lines):
                first = (tile * lines + line) * pairs
                wide_ref[pl.ds(source * rows + line * tiles + tile, pairs, stride=size), :] = (
                    got_ref[source, first : first + pairs, :].astype(F32)
                )

    @pl.loop(0, devices)
    def _(source):
        for pair in range(pairs):
            base = pl.multiple_of(spot_ref[source * pairs + pair], size)
            here = pl.multiple_of(source * rows + pair * size, size)
            out_ref[pl.ds(base, size), :] = (
                out_ref[pl.ds(base, size), :] + wide_ref[pl.ds(here, size), :]
            )

    copy = pltpu.make_async_copy(out_ref, out_hbm_ref, sem_ref)
    copy.start()
    copy.wait()


def TILES(ref):
    return ref.shape[0] // (NX * NY)


def smem_spec():
    return pl.BlockSpec(memory_space=pltpu.SMEM)


def scatter(spots, got, tiles):
    devices, rows, _ = got.shape
    return pl.pallas_call(
        scatter_kernel,
        out_shape=pltpu.HBM((NX * NY * tiles, 128), F32),
        in_specs=[smem_spec(), vmem_spec()],
        out_specs=any_spec(),
        scratch_shapes=[
            pltpu.VMEM((devices * (rows - 8), 128), F32),
            pltpu.VMEM((NX * NY * tiles, 128), F32),
            pltpu.SemaphoreType.DMA,
        ],
        compiler_params=limit(14),
        cost_estimate=cost(1e6, NX * NY * tiles * 128 * 16),
        name="scatter",
    )(spots, got)


def gather_kernel(size, devices, spot_ref, grid_hbm_ref, out_ref, grid_ref, sem_ref):
    copy = pltpu.make_async_copy(grid_hbm_ref, grid_ref, sem_ref)
    copy.start()
    copy.wait()
    pairs = spot_ref.shape[0] // devices

    @pl.loop(0, devices)
    def _(source):
        for pair in range(pairs):
            base = pl.multiple_of(spot_ref[source * pairs + pair], size)
            here = pl.multiple_of(source * (pairs * size) + pair * size, size)
            out_ref[pl.ds(here, size), :] = grid_ref[pl.ds(base, size), :]


def gather(spots, grid, size, devices):
    count = spots.shape[0]
    return pl.pallas_call(
        functools.partial(gather_kernel, size, devices),
        out_shape=pltpu.VMEM((count * size, 128), F32),
        in_specs=[smem_spec(), any_spec()],
        out_specs=vmem_spec(),
        scratch_shapes=[pltpu.VMEM(grid.shape, F32), pltpu.SemaphoreType.DMA],
        compiler_params=limit(12),
        cost_estimate=cost(1e6, grid.size * 8),
        name="gather",
    )(spots, in_hbm(grid))


def layer_kernel(
    table_ref, flipped_ref, modes_ref, grid_ref, up_ref, down_ref, out_ref, spec_ref, total_ref,
    up_wide_ref, down_wide_ref, folded_ref
):
    step = pl.program_id(0)
    rows = table_ref.shape[0]
    tiles = modes_ref.shape[1] // 128
    count = table_ref.shape[1] // 2
    blocks = count // MX

    @pl.when(step == 0)
    def _():
        total_ref[...] = jnp.zeros_like(total_ref)
        spread_weights(up_ref, down_ref, up_wide_ref, down_wide_ref)
        for parity in range(2):
            for block in range(blocks):
                base = (2 * block + parity) * MX
                folded_ref[parity, block * MX : (block + 1) * MX, :] = modes_ref[base : base + MX]

    even = dot(table_ref[:, 0:count], folded_ref[0])
    odd = dot(table_ref[:, count:], folded_ref[1])
    halves = (even + odd, even - odd)
    places = [(side, tile) for side in range(2) for tile in range(tiles)]
    summed = [
        grid_ref[side, pl.ds(tile, rows, stride=tiles), :]
        + halves[side][:, tile * 128 : (tile + 1) * 128]
        for side, tile in places
    ]
    results = mlp(summed, up_wide_ref, down_wide_ref)
    for (side, tile), result in zip(places, results):
        out_ref[side, pl.ds(tile, rows, stride=tiles), :] = result
    low, high = results[0:tiles], results[tiles:]
    plus = jnp.concatenate([(a + b).astype(BF16) for a, b in zip(low, high)], axis=1)
    minus = jnp.concatenate([(a - b).astype(BF16) for a, b in zip(low, high)], axis=1)
    total_ref[0] += dot(flipped_ref[0:count, :], plus)
    total_ref[1] += dot(flipped_ref[count:, :], minus)

    @pl.when(step == pl.num_programs(0) - 1)
    def _():
        for parity in range(2):
            for block in range(blocks):
                base = (2 * block + parity) * MX
                spec_ref[base : base + MX, :] = total_ref[
                    parity, block * MX : (block + 1) * MX, :
                ].astype(BF16)


def weight_specs(up, down, number):
    return [
        pl.BlockSpec((1,) + up.shape[1:], lambda i: (number, 0, 0)),
        pl.BlockSpec((1,) + down.shape[1:], lambda i: (number, 0, 0)),
    ]


def wide_weights(up):
    channels, hidden = up.shape[1:]
    return [
        pltpu.VMEM((2 * channels, 2 * hidden), BF16),
        pltpu.VMEM((2 * hidden, 2 * channels), BF16),
    ]


def layer(table, flipped, modes, grid, up, down, number):
    cells, columns = table.shape
    lanes = modes.shape[1]
    tiles = lanes // 128
    rows = 512
    const = lambda i: (0, 0)
    return pl.pallas_call(
        layer_kernel,
        out_shape=(
            pltpu.HBM((2, cells * tiles, 128), F32),
            jax.ShapeDtypeStruct((columns, lanes), BF16),
        ),
        grid=(cells // rows,),
        in_specs=[
            pl.BlockSpec((rows, columns), lambda i: (i, 0)),
            pl.BlockSpec((columns, rows), lambda i: (0, i)),
            pl.BlockSpec((columns, lanes), const),
            pl.BlockSpec((2, rows * tiles, 128), lambda i: (0, i, 0)),
        ]
        + weight_specs(up, down, number),
        out_specs=(
            pl.BlockSpec((2, rows * tiles, 128), lambda i: (0, i, 0)),
            pl.BlockSpec((columns, lanes), const),
        ),
        scratch_shapes=[pltpu.VMEM((2, columns // 2, lanes), F32)]
        + wide_weights(up)
        + [pltpu.VMEM((2, columns // 2, lanes), BF16)],
        cost_estimate=cost(
            4 * cells * columns * lanes + 16 * cells * lanes * up.shape[2],
            cells * (columns * 4 + lanes * 8),
        ),
        compiler_params=limit(22),
        name="layer",
    )(
        in_hbm(table), in_hbm(flipped), modes, in_hbm(grid.reshape(2, cells * tiles, 128)),
        up, down,
    )


def last_kernel(lines, phase_ref, modes_ref, grid_ref, up_ref, down_ref, out_ref, up_wide_ref, down_wide_ref):
    group, rows, _ = out_ref.shape
    tiles = modes_ref.shape[1] // 128
    rows = rows // tiles

    @pl.when(pl.program_id(0) == 0)
    def _():
        spread_weights(up_ref, down_ref, up_wide_ref, down_wide_ref)

    spectral = dot(phase_ref[...], modes_ref[...])
    size = tiles * lines
    pairs = rows // lines
    summed = [
        jnp.concatenate(
            [
                grid_ref[
                    pl.ds(source * pairs * size + line * tiles + tile, pairs, stride=size), :
                ]
                for source in range(group)
                for line in range(lines)
            ],
            axis=0,
        )
        + spectral[:, tile * 128 : (tile + 1) * 128]
        for tile in range(tiles)
    ]
    results = mlp(summed, up_wide_ref, down_wide_ref)
    for tile, result in enumerate(results):
        result = result.astype(BF16)
        for source in range(group):
            out_ref[source, tile * rows : (tile + 1) * rows, :] = result[
                source * rows : (source + 1) * rows, :
            ]


def last_layer(phases, modes, grid, up, down, number, devices, lines):
    count, columns = phases.shape
    lanes = modes.shape[1]
    tiles = lanes // 128
    group = 8
    rows = count // devices
    return pl.pallas_call(
        functools.partial(last_kernel, lines),
        out_shape=jax.ShapeDtypeStruct((devices, rows * tiles, 128), BF16),
        grid=(devices // group,),
        in_specs=[
            pl.BlockSpec((group * rows, columns), lambda i: (i, 0)),
            pl.BlockSpec((columns, lanes), lambda i: (0, 0)),
            pl.BlockSpec((group * rows * tiles, 128), lambda i: (i, 0)),
        ]
        + weight_specs(up, down, number),
        out_specs=pl.BlockSpec((group, rows * tiles, 128), lambda i: (i, 0, 0)),
        scratch_shapes=wide_weights(up),
        cost_estimate=cost(
            2 * count * columns * lanes + 16 * count * lanes * up.shape[2],
            count * (columns * 2 + lanes * 6),
        ),
        compiler_params=limit(24),
        name="last_layer",
    )(in_hbm(phases), modes, in_vmem(grid), up, down)


def exchange(values):
    return lax.all_to_all(values, "pen", split_axis=0, concat_axis=0, tiled=True)


def forward_pass(point_feat, pair_kernel, pair_owner, pair_block, spec_weight, mlp_up, mlp_down):
    devices = lax.axis_size("pen")
    pairs, block = pair_kernel.shape[0], pair_kernel.shape[1]
    channels = point_feat.shape[0]
    modes_here = spec_weight.shape[1]
    lines = block // NZ
    lanes = NZ // devices * channels
    tiles = lanes // 128
    columns = devices * 2 * MX

    up = mlp_up.transpose(0, 2, 1)
    send = encode(
        point_feat, pair_kernel, pair_owner.reshape(1, pairs), pair_block.reshape(1, pairs), devices
    )
    got = exchange(send)

    table, flipped = grid_tables(devices, modes_here)
    got, table, flipped = lax.optimization_barrier((got, table, flipped))
    forward, inverse = depth_tables(devices, modes_here)
    lookups = lookup_tables()
    here = got[:, -8:-6, 0:pairs].astype(jnp.int32)
    rows = ((here[:, 0, :] * NY + here[:, 1, :]) * tiles).reshape(devices * pairs)

    spectrum = pair_spectrum(got, lookups, modes_here, lanes)
    phases = pair_phases(got, lookups, modes_here, lanes)
    grid = scatter(rows, got, tiles)
    modes = exchange(spectrum.reshape(devices, 2 * MX, lanes)).reshape(columns, lanes)
    modes = mix(modes, forward, inverse, spec_weight, 0, devices)
    modes = exchange(modes.reshape(devices, 2 * MX, lanes)).reshape(columns, lanes)
    grid, spectrum = layer(table, flipped, modes, grid, up, mlp_down, 0)
    listed = gather(rows, grid.reshape(-1, 128), lines * tiles, devices)
    modes = exchange(spectrum.reshape(devices, 2 * MX, lanes)).reshape(columns, lanes)
    modes = mix(modes, forward, inverse, spec_weight, 1, devices)
    modes = exchange(modes.reshape(devices, 2 * MX, lanes)).reshape(columns, lanes)
    result = last_layer(phases, modes, listed, up, mlp_down, 1, devices, lines)
    return decode(exchange(result), pair_kernel, channels)


def solution(mesh):
    in_specs = (
        P(None, ("groups", "pen")),
        P(("groups", "pen"), None, None),
        P(("groups", "pen"), None),
        P(("groups", "pen")),
        P(None, "pen", None, None, None),
        P(),
        P(),
    )
    out_specs = P(None, ("groups", "pen"))
    return jax.shard_map(
        forward_pass, mesh=mesh, in_specs=in_specs, out_specs=out_specs, check_vma=False
    )
```

```python
import functools
import math

import jax
import jax.numpy as jnp
import numpy as np
from jax import lax
from jax.experimental import pallas as pl
from jax.experimental.pallas import tpu as pltpu
from jax.sharding import PartitionSpec as P


NX = 128
NY = 64
NZ = 64
MX = 16
MY = 16
MZ = 16
NBR = 4
GELU_K = math.sqrt(2.0 / math.pi)
SCALE = 1.66575
PAD = 8
PITCH = 2 * MX + PAD
PARTS = 2
LONG_PARTS = 2

F32 = jnp.float32
BF16 = jnp.bfloat16


def vmem_spec():
    return pl.BlockSpec(memory_space=pltpu.VMEM)


def in_vmem(values):
    return pltpu.with_memory_space_constraint(values, pltpu.VMEM)


def in_hbm(values):
    return pltpu.with_memory_space_constraint(values, pltpu.HBM)


def any_spec():
    return pl.BlockSpec(memory_space=pl.ANY)


def limit(mebibytes):
    return pltpu.CompilerParams(vmem_limit_bytes=mebibytes << 20)


def cost(flops, size, transcendentals=0):
    return pl.CostEstimate(
        flops=int(flops), bytes_accessed=int(size), transcendentals=int(transcendentals)
    )


def dot(left, right):
    return jnp.dot(left, right, preferred_element_type=F32)


def x_waves():
    wave = np.arange(MX) - MX // 2
    return np.concatenate([wave[wave % 2 == 0], wave[wave % 2 == 1]])


def y_waves(devices, modes_here):
    return (np.arange(devices) * modes_here) // MZ - MY // 2


def turn(wave, count):
    return 2.0 * np.pi / count * (np.arange(count)[:, None] * wave[None, :] % count)


def line_tables(devices, modes_here):
    size = 2 * MX * devices
    column = np.arange(size)
    half = MX // 2
    wave_x = x_waves()[column // (size // 2) * half + column % half]
    wave_y = y_waves(devices, modes_here)[column // MX % devices]
    part = column // half % 2
    x_angle = turn(wave_x, NX)[: NX // 2]
    y_angle = turn(wave_y, NY)
    x_cos, x_sin = SCALE * np.cos(x_angle), SCALE * np.sin(x_angle)
    first = np.where(part == 0, x_cos, -x_sin)
    second = np.where(part == 0, -x_sin, -x_cos)
    return [
        jnp.asarray(each.astype(np.float32))
        for each in (first, second, np.cos(y_angle), np.sin(y_angle))
    ]


def lookup_tables():
    result = []
    for wave, count, scale in ((x_waves(), NX, SCALE), (np.arange(MY) - MY // 2, NY, 1.0)):
        angle = turn(wave, count).T
        values = scale * np.concatenate([np.cos(angle), -np.sin(angle)])
        result.append(jnp.concatenate(split(jnp.asarray(values.astype(np.float32))), axis=0))
    return result


def split(values):
    high = values.astype(BF16)
    return high, (values - high.astype(F32)).astype(BF16)


def depth_tables(devices, modes_here):
    local = NZ // devices
    wave_z = np.arange(MZ).reshape(MZ // modes_here, modes_here)
    z_of = np.arange(devices)[None, :] + devices * np.arange(local)[:, None]
    angle = 2.0 * np.pi / NZ * (z_of[None, :, :, None] * wave_z[:, None, None, :] % NZ)
    cosine, sine = np.cos(angle), np.sin(angle)
    to_real = np.stack([cosine, sine], axis=-1)
    to_imag = np.stack([-sine, cosine], axis=-1)
    forward = np.stack([to_real, to_imag], axis=-2) / SCALE
    forward = forward.transpose(0, 1, 3, 4, 5, 2).reshape(
        -1, local * modes_here * 2, devices * 2
    )
    scale = np.where(wave_z == 0, 1.0, 2.0)[:, None, None, :] / (NX * NY * NZ * SCALE)
    cosine, sine = cosine * scale, sine * scale
    low = np.stack(
        [np.stack([cosine, -sine], axis=-1), np.stack([sine, cosine], axis=-1)], axis=2
    ).reshape(-1, local * devices * 2, modes_here * 2)
    high = np.stack(
        [np.stack([-sine, -cosine], axis=-1), np.stack([cosine, -sine], axis=-1)], axis=2
    ).reshape(-1, local * devices * 2, modes_here * 2)
    inverse = np.concatenate([low, high], axis=2)
    which = lax.axis_index("pen") * modes_here % MZ // modes_here
    chosen = []
    for table in (forward, inverse):
        table = jnp.asarray(table.astype(np.float32))
        chosen.append(table[0] if table.shape[0] == 1 else table[which])
    forward, inverse = chosen
    high, low = split(inverse)
    return (
        jnp.concatenate(split(forward), axis=1),
        jnp.concatenate([high, low, high], axis=1),
    )


def table_kernel(first_ref, second_ref, cos_ref, sin_ref, table_ref, flipped_ref):
    pieces = []
    for line in range(first_ref.shape[0]):
        piece = (
            first_ref[line : line + 1, :] * cos_ref[...]
            + second_ref[line : line + 1, :] * sin_ref[...]
        )
        pieces.append(piece.astype(BF16))
    whole = jnp.concatenate(pieces, axis=0)
    table_ref[...] = whole
    flipped_ref[...] = whole.T


def grid_tables(devices, modes_here):
    first, second, y_cos, y_sin = line_tables(devices, modes_here)
    columns = first.shape[1]
    lines = 8
    rows = lines * NY
    const = lambda i: (0, 0)
    return pl.pallas_call(
        table_kernel,
        out_shape=(
            pltpu.HBM((NX // 2 * NY, columns), BF16),
            pltpu.HBM((columns, NX // 2 * NY), BF16),
        ),
        grid=(NX // 2 // lines,),
        in_specs=[
            pl.BlockSpec((lines, columns), lambda i: (i, 0)),
            pl.BlockSpec((lines, columns), lambda i: (i, 0)),
            pl.BlockSpec((NY, columns), const),
            pl.BlockSpec((NY, columns), const),
        ],
        out_specs=(
            pl.BlockSpec((rows, columns), lambda i: (i, 0)),
            pl.BlockSpec((columns, rows), lambda i: (0, i)),
        ),
        cost_estimate=cost(4 * NX // 2 * NY * columns, 4 * NX // 2 * NY * columns),
        compiler_params=limit(8),
        name="tables",
    )(first, second, y_cos, y_sin)


def copies_of(from_ref, to_ref, sem_ref):
    step = from_ref.shape[0] // LONG_PARTS
    return [
        pltpu.make_async_copy(
            from_ref.at[pl.ds(part * step, step)],
            to_ref.at[pl.ds(part * step, step)],
            sem_ref.at[part],
        )
        for part in range(LONG_PARTS)
    ]


def encode_kernel(
    feature_hbm_ref, weight_hbm_ref, owner_hbm_ref, number_hbm_ref, out_hbm_ref, wide_ref,
    feature_ref, weight_ref, owner_ref, number_ref, out_ref, sem_ref, out_sem_ref
):
    devices = out_ref.shape[0]
    pairs, block = weight_ref.shape[0], weight_ref.shape[1]
    points = pairs // NBR
    lines = block // NZ
    tiles = NZ // devices // 2
    rows = tiles * pairs * lines
    copies = copies_of(weight_hbm_ref, weight_ref, sem_ref)
    small = [
        pltpu.make_async_copy(from_ref, to_ref, sem_ref.at[LONG_PARTS + place])
        for place, (from_ref, to_ref) in enumerate(
            (
                (owner_hbm_ref, owner_ref),
                (number_hbm_ref, number_ref),
                (feature_hbm_ref, feature_ref),
            )
        )
    ]
    for copy in small + copies:
        copy.start()
    for copy in small[0:2]:
        copy.wait()
    lane = lax.broadcasted_iota(jnp.int32, (devices, 128), 1)
    strip = NY // lines
    target = owner_ref[...] * (NX * strip // devices) + number_ref[...]
    y_at = (target % strip) * lines
    spots = jnp.concatenate(
        [
            jnp.concatenate([target // strip] * lines, axis=1),
            jnp.concatenate([y_at + line for line in range(lines)], axis=1),
            jnp.zeros((6, 128), jnp.int32),
        ],
        axis=0,
    )
    spots = spots.astype(F32).astype(BF16)
    for device in range(devices):
        out_ref[device, rows : rows + 8, :] = spots
    small[2].wait()

    def one(point, carry):
        features = feature_ref[:, pl.ds(pl.multiple_of(point * block, block), block)]
        features = jnp.concatenate([features, features], axis=0)
        for near in range(NBR):
            pair = point * NBR + near
            turned = lax.dot_general(
                weight_ref[pair], features, (((0,), (1,)), ((), ())), preferred_element_type=F32
            )
            for line in range(lines):
                for tile in range(tiles):
                    first = line * NZ + 2 * tile * devices
                    wide_ref[
                        pl.ds((tile * lines + line) * pairs + pair, devices, stride=rows + PAD), :
                    ] = jnp.where(
                        lane < 64,
                        turned[first : first + devices],
                        turned[first + devices : first + 2 * devices],
                    )
        return carry

    for part, copy in enumerate(copies):
        copy.wait()
        lax.fori_loop(
            part * points // LONG_PARTS, (part + 1) * points // LONG_PARTS, one, 0, unroll=points // LONG_PARTS
        )
    results = []
    for device in range(devices):
        base = device * (rows + PAD)
        out_ref[device, 0:rows, :] = wide_ref[base : base + rows, :].astype(BF16)
        results.append(
            pltpu.make_async_copy(
                out_ref.at[device], out_hbm_ref.at[device], out_sem_ref.at[device]
            )
        )
        results[-1].start()
    for result in results:
        result.wait()


def encode(features, weights, owners, numbers, devices):
    pairs, block = weights.shape[0], weights.shape[1]
    rows = NZ // devices // 2 * pairs * (block // NZ)
    return pl.pallas_call(
        encode_kernel,
        out_shape=pltpu.HBM((devices, rows + 8, 128), BF16),
        in_specs=[any_spec()] * 4,
        out_specs=any_spec(),
        scratch_shapes=[
            pltpu.VMEM((devices * (rows + PAD), 128), F32),
            pltpu.VMEM(features.shape, BF16),
            pltpu.VMEM(weights.shape, BF16),
            pltpu.VMEM(owners.shape, jnp.int32),
            pltpu.VMEM(numbers.shape, jnp.int32),
            pltpu.VMEM((devices, rows + 8, 128), BF16),
            pltpu.SemaphoreType.DMA((LONG_PARTS + 3,)),
            pltpu.SemaphoreType.DMA((devices,)),
        ],
        compiler_params=limit(10),
        cost_estimate=cost(4 * pairs * block * block * 64, pairs * block * block * 2),
        name="encode",
    )(in_hbm(features), in_hbm(weights), in_hbm(owners), in_hbm(numbers))


def decode_kernel(
    got_ref, weight_hbm_ref, out_hbm_ref, wide_ref, weight_ref, out_ref, sem_ref, out_sem_ref
):
    copies = copies_of(weight_hbm_ref, weight_ref, sem_ref)
    for copy in copies:
        copy.start()
    devices, rows, _ = got_ref.shape
    pairs, block = weight_ref.shape[0], weight_ref.shape[1]
    lines = block // NZ
    tiles = NZ // devices // 2
    lane = lax.broadcasted_iota(jnp.int32, (devices, 128), 1)
    for device in range(devices):
        base = device * (rows + PAD)
        wide_ref[base : base + rows, :] = got_ref[device].astype(F32)

    def one(point, carry):
        pieces = []
        for near in range(NBR):
            pair = point * NBR + near
            for line in range(lines):
                for tile in range(tiles):
                    values = wide_ref[
                        pl.ds((tile * lines + line) * pairs + pair, devices, stride=rows + PAD), :
                    ]
                    pieces.append(jnp.where(lane < 64, values, 0.0))
                    pieces.append(jnp.where(lane < 64, 0.0, values))
        total = dot(
            jnp.concatenate([weight_ref[point * NBR + near] for near in range(NBR)], axis=1),
            jnp.concatenate(pieces, axis=0).astype(BF16),
        )
        total = (total + pltpu.roll(total, 64, 1)).T
        out_ref[:, pl.ds(pl.multiple_of(point * block, block), block)] = total[0:64, :]
        return carry

    points = pairs // NBR
    results = []
    for part, copy in enumerate(copies):
        copy.wait()
        lax.fori_loop(
            part * points // LONG_PARTS, (part + 1) * points // LONG_PARTS, one, 0, unroll=points // LONG_PARTS
        )
        place = pl.ds(part * points // LONG_PARTS * block, points // LONG_PARTS * block)
        results.append(
            pltpu.make_async_copy(
                out_ref.at[:, place], out_hbm_ref.at[:, place], out_sem_ref.at[part]
            )
        )
        results[-1].start()
    for result in results:
        result.wait()


def decode(got, weights, channels):
    devices, rows, _ = got.shape
    pairs, block = weights.shape[0], weights.shape[1]
    return pl.pallas_call(
        decode_kernel,
        out_shape=pltpu.HBM((channels, pairs // NBR * block), F32),
        in_specs=[vmem_spec(), any_spec()],
        out_specs=any_spec(),
        scratch_shapes=[
            pltpu.VMEM((devices * (rows + PAD), 128), F32),
            pltpu.VMEM(weights.shape, BF16),
            pltpu.VMEM((channels, pairs // NBR * block), F32),
            pltpu.SemaphoreType.DMA((LONG_PARTS,)),
            pltpu.SemaphoreType.DMA((LONG_PARTS,)),
        ],
        cost_estimate=cost(4 * pairs * block * block * 64, pairs * block * block * 2),
        compiler_params=limit(12),
        name="decode",
    )(got, in_hbm(weights))


def look_up(table_ref, count, spot):
    every = lax.broadcasted_iota(jnp.int32, (count, spot.shape[1]), 0)
    values = dot(table_ref[...], (every == spot).astype(F32).astype(BF16))
    half = values.shape[0] // 2
    return values[0:half] + values[half:]


def fill_phases(modes_here, devices, spots, x_ref, y_ref, phase_ref):
    half = MX // 2
    for source, spot in enumerate(spots):
        spot = spot.astype(F32)
        x_turn = look_up(x_ref, NX, spot[0:1, :].astype(jnp.int32))
        y_turn = look_up(y_ref, NY, spot[1:2, :].astype(jnp.int32))
        lanes = spot.shape[1]
        place = slice(source * lanes, (source + 1) * lanes)
        for device in range(devices):
            row = (device * modes_here) // MZ
            y_cos, y_less = y_turn[row : row + 1, :], y_turn[MY + row : MY + row + 1, :]
            for parity in range(2):
                first = parity * half
                x_cos, x_less = x_turn[first : first + half], x_turn[MX + first : MX + first + half]
                both = jnp.concatenate(
                    [x_cos * y_cos - x_less * y_less, x_less * y_cos + x_cos * y_less], axis=0
                )
                base = (2 * device + parity) * MX
                phase_ref[base : base + MX, place] = both.astype(BF16)


def pair_spectrum_kernel(
    modes_here, got_ref, x_ref, y_ref, out_ref, phase_ref
):
    devices = got_ref.shape[0]
    rows = got_ref.shape[1] - 8
    tiles = out_ref.shape[1] // 128
    lanes = rows // tiles
    spots = [got_ref[source, rows : rows + 8, :] for source in range(devices)]
    fill_phases(modes_here, devices, spots, x_ref, y_ref, phase_ref)
    values = jnp.concatenate(
        [
            jnp.concatenate(
                [
                    got_ref[source, tile * lanes : (tile + 1) * lanes, :]
                    for source in range(devices)
                ],
                axis=0,
            )
            for tile in range(tiles)
        ],
        axis=1,
    )
    out_ref[...] = dot(phase_ref[...], values).astype(BF16)


def pair_spectrum(got, tables, modes_here, lanes):
    devices, rows, _ = got.shape
    count = devices * (rows - 8) // (lanes // 128)
    columns = devices * 2 * MX
    return pl.pallas_call(
        functools.partial(pair_spectrum_kernel, modes_here),
        out_shape=jax.ShapeDtypeStruct((columns, lanes), BF16),
        in_specs=[vmem_spec()] * 3,
        out_specs=vmem_spec(),
        scratch_shapes=[pltpu.VMEM((columns, count), BF16)],
        compiler_params=limit(10),
        cost_estimate=cost(2 * columns * count * lanes, got.size * 2 + columns * count * 2),
        name="pair_spectrum",
    )(got, *tables)


def phase_kernel(modes_here, got_ref, x_ref, y_ref, out_hbm_ref, phase_ref, out_ref, sem_ref):
    devices = got_ref.shape[0]
    rows = got_ref.shape[1] - 8
    spots = [got_ref[source, rows : rows + 8, :] for source in range(devices)]
    fill_phases(modes_here, devices, spots, x_ref, y_ref, phase_ref)
    out_ref[...] = phase_ref[...].T
    copy = pltpu.make_async_copy(out_ref, out_hbm_ref, sem_ref)
    copy.start()
    copy.wait()


def pair_phases(got, tables, modes_here, lanes):
    devices, rows, _ = got.shape
    shape = (devices * 2 * MX, devices * (rows - 8) // (lanes // 128))
    return pl.pallas_call(
        functools.partial(phase_kernel, modes_here),
        out_shape=pltpu.HBM(shape[::-1], BF16),
        in_specs=[vmem_spec()] * 3,
        out_specs=any_spec(),
        scratch_shapes=[
            pltpu.VMEM(shape, BF16),
            pltpu.VMEM(shape[::-1], BF16),
            pltpu.SemaphoreType.DMA,
        ],
        compiler_params=limit((4 * shape[0] * shape[1] >> 20) + 6),
        cost_estimate=cost(1e6, got.size * 2 + shape[0] * shape[1] * 2),
        name="pair_phases",
    )(got, *tables)


def row_of(wave, part):
    half = MX // 2
    order = list(x_waves() + half).index(wave)
    return order // half * MX + part * half + order % half


def mix_kernel(
    devices, number, got_ref, forward_ref, inverse_ref, weight_hbm_ref, out_ref, wide_ref,
    back_ref, weight_ref, sem_ref
):
    modes_here, _, channels, _ = weight_ref.shape
    each = MX // PARTS
    copies = [
        pltpu.make_async_copy(
            weight_hbm_ref.at[number, :, pl.ds(part * each, each)],
            weight_ref.at[:, pl.ds(part * each, each)],
            sem_ref.at[part],
        )
        for part in range(PARTS)
    ]
    for copy in copies:
        copy.start()
    tiles = got_ref.shape[1] // 128
    group = 8
    for tile in range(tiles):
        for device in range(devices):
            wide_ref[tile, device * PITCH : device * PITCH + 2 * MX, :] = got_ref[
                device * 2 * MX : (device + 1) * 2 * MX, tile * 128 : (tile + 1) * 128
            ].astype(F32)
    lane = lax.broadcasted_iota(jnp.int32, (2 * modes_here, 128), 1)
    row = lax.broadcasted_iota(jnp.int32, (2 * group, 128), 0)
    lane_small = lax.broadcasted_iota(jnp.int32, (2 * group, 128), 1)
    lane_back = lax.broadcasted_iota(jnp.int32, (2 * devices, 128), 1)
    forward = forward_ref[...]
    inverse = inverse_ref[...]
    spread = []
    for wave in range(MX):
        planes = jnp.concatenate(
            [
                jnp.concatenate(
                    [
                        wide_ref[tile, pl.ds(row_of(wave, part), devices, stride=PITCH), :]
                        for part in range(2)
                    ],
                    axis=0,
                )
                for tile in range(tiles)
            ],
            axis=1,
        ).astype(BF16)
        turned = dot(forward, jnp.concatenate([planes, planes], axis=0))
        total = None
        for tile in range(tiles):
            part = slice(tile * 128, (tile + 1) * 128)
            size = 2 * modes_here
            even = turned[2 * tile * size : (2 * tile + 1) * size, part]
            odd = turned[(2 * tile + 1) * size : (2 * tile + 2) * size, part]
            both = even + pltpu.roll(odd, 64, 1)
            total = both if total is None else total + both
        spread.append(jnp.where(lane < 64, total, pltpu.roll(total, 64, 1)))
    mixed = []
    for wave in range(MX):
        pieces = []
        if wave % each == 0:
            copies[wave // each].wait()
        for first in range(0, modes_here, group):
            now = spread[wave][2 * first : 2 * (first + group), :]
            left = jnp.concatenate(
                [
                    jnp.where(row // 2 == 2 * step + lane_small // 64, now, 0.0)
                    for step in range(group // 2)
                ],
                axis=1,
            )
            left = jnp.concatenate(split(left), axis=0)
            right = weight_ref[first : first + group, wave, :, :].reshape(
                group * channels, 2 * channels
            )
            both = dot(left, right)
            pieces.append(both[0 : 2 * group] + both[2 * group :])
        mixed.append(pieces[0] if len(pieces) == 1 else jnp.concatenate(pieces, axis=0))
    for wave in range(MX):
        stacked = jnp.concatenate([mixed[wave], pltpu.roll(mixed[wave], 64, 1)], axis=0)
        upper, lower = split(stacked)
        planes = dot(inverse, jnp.concatenate([upper, upper, lower], axis=0))
        size = 2 * devices
        for tile in range(tiles):
            even = planes[2 * tile * size : (2 * tile + 1) * size, :]
            odd = planes[(2 * tile + 1) * size : (2 * tile + 2) * size, :]
            both = jnp.where(lane_back < 64, even, pltpu.roll(odd, 64, 1))
            for part in range(2):
                back_ref[tile, pl.ds(row_of(wave, part), devices, stride=PITCH), :] = both[
                    part * devices : (part + 1) * devices
                ]
    for tile in range(tiles):
        for device in range(devices):
            out_ref[
                device * 2 * MX : (device + 1) * 2 * MX, tile * 128 : (tile + 1) * 128
            ] = back_ref[tile, device * PITCH : device * PITCH + 2 * MX, :].astype(BF16)


def mix(got, forward, inverse, weights, number, devices):
    rows, lanes = got.shape
    return pl.pallas_call(
        functools.partial(mix_kernel, devices, number),
        out_shape=jax.ShapeDtypeStruct((rows, lanes), BF16),
        in_specs=[vmem_spec()] * 3 + [any_spec()],
        out_specs=vmem_spec(),
        scratch_shapes=[pltpu.VMEM((lanes // 128, devices * PITCH, 128), F32)] * 2
        + [pltpu.VMEM(weights.shape[1:], BF16), pltpu.SemaphoreType.DMA((PARTS,))],
        compiler_params=limit(12),
        cost_estimate=cost(6e8, weights.size + rows * lanes * 4),
        name="mix",
    )(got, forward, inverse, in_hbm(weights))


def spread_weights(up_ref, down_ref, up_wide_ref, down_wide_ref):
    channels, hidden = up_ref.shape[1:]
    up = up_ref[0]
    down = (down_ref[0].astype(F32) * 0.5).astype(BF16).T
    up_wide_ref[...] = jnp.zeros_like(up_wide_ref)
    down_wide_ref[...] = jnp.zeros_like(down_wide_ref)
    for cell in range(2):
        here = slice(cell * channels, (cell + 1) * channels)
        there = slice(cell * hidden, (cell + 1) * hidden)
        up_wide_ref[here, there] = up
        down_wide_ref[there, here] = down


def gelu_twice(hidden):
    hidden = hidden.astype(BF16)
    first = jnp.asarray(GELU_K, BF16)
    third = jnp.asarray(GELU_K * 0.044715, BF16)
    return hidden * jnp.tanh(hidden * (first + third * (hidden * hidden))) + hidden


def mlp(summed, up_ref, down_ref):
    width = 256
    rounded = [each.astype(BF16) for each in summed]
    totals = list(summed)
    for first in range(0, up_ref.shape[1], width):
        hidden = [dot(each, up_ref[:, first : first + width]) for each in rounded]
        active = [gelu_twice(each) for each in hidden]
        for n, each in enumerate(active):
            totals[n] = totals[n] + dot(each, down_ref[first : first + width, :])
    return totals


def scatter_kernel(spot_ref, got_ref, out_hbm_ref, wide_ref, out_ref, sem_ref):
    devices, rows, _ = got_ref.shape
    rows = rows - 8
    pairs = spot_ref.shape[0] // devices
    size = rows // pairs
    tiles = TILES(out_ref)
    lines = size // tiles
    out_ref[...] = jnp.zeros_like(out_ref)
    for source in range(devices):
        for tile in range(tiles):
            for line in range(lines):
                first = (tile * lines + line) * pairs
                wide_ref[pl.ds(source * rows + line * tiles + tile, pairs, stride=size), :] = (
                    got_ref[source, first : first + pairs, :].astype(F32)
                )

    @pl.loop(0, devices)
    def _(source):
        for pair in range(pairs):
            base = pl.multiple_of(spot_ref[source * pairs + pair], size)
            here = pl.multiple_of(source * rows + pair * size, size)
            out_ref[pl.ds(base, size), :] = (
                out_ref[pl.ds(base, size), :] + wide_ref[pl.ds(here, size), :]
            )

    copy = pltpu.make_async_copy(out_ref, out_hbm_ref, sem_ref)
    copy.start()
    copy.wait()


def TILES(ref):
    return ref.shape[0] // (NX * NY)


def smem_spec():
    return pl.BlockSpec(memory_space=pltpu.SMEM)


def scatter(spots, got, tiles):
    devices, rows, _ = got.shape
    return pl.pallas_call(
        scatter_kernel,
        out_shape=pltpu.HBM((NX * NY * tiles, 128), F32),
        in_specs=[smem_spec(), vmem_spec()],
        out_specs=any_spec(),
        scratch_shapes=[
            pltpu.VMEM((devices * (rows - 8), 128), F32),
            pltpu.VMEM((NX * NY * tiles, 128), F32),
            pltpu.SemaphoreType.DMA,
        ],
        compiler_params=limit(14),
        cost_estimate=cost(1e6, NX * NY * tiles * 128 * 16),
        name="scatter",
    )(spots, got)


def gather_kernel(size, devices, spot_ref, grid_hbm_ref, out_ref, grid_ref, sem_ref):
    copy = pltpu.make_async_copy(grid_hbm_ref, grid_ref, sem_ref)
    copy.start()
    copy.wait()
    pairs = spot_ref.shape[0] // devices

    @pl.loop(0, devices)
    def _(source):
        for pair in range(pairs):
            base = pl.multiple_of(spot_ref[source * pairs + pair], size)
            here = pl.multiple_of(source * (pairs * size) + pair * size, size)
            out_ref[pl.ds(here, size), :] = grid_ref[pl.ds(base, size), :]


def gather(spots, grid, size, devices):
    count = spots.shape[0]
    return pl.pallas_call(
        functools.partial(gather_kernel, size, devices),
        out_shape=pltpu.VMEM((count * size, 128), F32),
        in_specs=[smem_spec(), any_spec()],
        out_specs=vmem_spec(),
        scratch_shapes=[pltpu.VMEM(grid.shape, F32), pltpu.SemaphoreType.DMA],
        compiler_params=limit(12),
        cost_estimate=cost(1e6, grid.size * 8),
        name="gather",
    )(spots, in_hbm(grid))


def layer_kernel(
    table_ref, flipped_ref, modes_ref, grid_ref, up_ref, down_ref, out_ref, spec_ref, total_ref,
    up_wide_ref, down_wide_ref, folded_ref
):
    step = pl.program_id(0)
    rows = table_ref.shape[0]
    tiles = modes_ref.shape[1] // 128
    count = table_ref.shape[1] // 2
    blocks = count // MX

    @pl.when(step == 0)
    def _():
        total_ref[...] = jnp.zeros_like(total_ref)
        spread_weights(up_ref, down_ref, up_wide_ref, down_wide_ref)
        for parity in range(2):
            for block in range(blocks):
                base = (2 * block + parity) * MX
                folded_ref[parity, block * MX : (block + 1) * MX, :] = modes_ref[base : base + MX]

    even = dot(table_ref[:, 0:count], folded_ref[0])
    odd = dot(table_ref[:, count:], folded_ref[1])
    halves = (even + odd, even - odd)
    places = [(side, tile) for side in range(2) for tile in range(tiles)]
    summed = [
        grid_ref[side, pl.ds(tile, rows, stride=tiles), :]
        + halves[side][:, tile * 128 : (tile + 1) * 128]
        for side, tile in places
    ]
    results = mlp(summed, up_wide_ref, down_wide_ref)
    for (side, tile), result in zip(places, results):
        out_ref[side, pl.ds(tile, rows, stride=tiles), :] = result
    low, high = results[0:tiles], results[tiles:]
    plus = jnp.concatenate([(a + b).astype(BF16) for a, b in zip(low, high)], axis=1)
    minus = jnp.concatenate([(a - b).astype(BF16) for a, b in zip(low, high)], axis=1)
    total_ref[0] += dot(flipped_ref[0:count, :], plus)
    total_ref[1] += dot(flipped_ref[count:, :], minus)

    @pl.when(step == pl.num_programs(0) - 1)
    def _():
        for parity in range(2):
            for block in range(blocks):
                base = (2 * block + parity) * MX
                spec_ref[base : base + MX, :] = total_ref[
                    parity, block * MX : (block + 1) * MX, :
                ].astype(BF16)


def weight_specs(up, down, number):
    return [
        pl.BlockSpec((1,) + up.shape[1:], lambda i: (number, 0, 0)),
        pl.BlockSpec((1,) + down.shape[1:], lambda i: (number, 0, 0)),
    ]


def wide_weights(up):
    channels, hidden = up.shape[1:]
    return [
        pltpu.VMEM((2 * channels, 2 * hidden), BF16),
        pltpu.VMEM((2 * hidden, 2 * channels), BF16),
    ]


def layer(table, flipped, modes, grid, up, down, number):
    cells, columns = table.shape
    lanes = modes.shape[1]
    tiles = lanes // 128
    rows = 1024
    const = lambda i: (0, 0)
    return pl.pallas_call(
        layer_kernel,
        out_shape=(
            pltpu.HBM((2, cells * tiles, 128), F32),
            jax.ShapeDtypeStruct((columns, lanes), BF16),
        ),
        grid=(cells // rows,),
        in_specs=[
            pl.BlockSpec((rows, columns), lambda i: (i, 0)),
            pl.BlockSpec((columns, rows), lambda i: (0, i)),
            pl.BlockSpec((columns, lanes), const),
            pl.BlockSpec((2, rows * tiles, 128), lambda i: (0, i, 0)),
        ]
        + weight_specs(up, down, number),
        out_specs=(
            pl.BlockSpec((2, rows * tiles, 128), lambda i: (0, i, 0)),
            pl.BlockSpec((columns, lanes), const),
        ),
        scratch_shapes=[pltpu.VMEM((2, columns // 2, lanes), F32)]
        + wide_weights(up)
        + [pltpu.VMEM((2, columns // 2, lanes), BF16)],
        cost_estimate=cost(
            4 * cells * columns * lanes + 16 * cells * lanes * up.shape[2],
            cells * (columns * 4 + lanes * 8),
        ),
        compiler_params=limit(42),
        name="layer",
    )(
        in_hbm(table), in_hbm(flipped), modes, in_hbm(grid.reshape(2, cells * tiles, 128)),
        up, down,
    )


def last_kernel(lines, phase_ref, modes_ref, grid_ref, up_ref, down_ref, out_ref, up_wide_ref, down_wide_ref):
    group, rows, _ = out_ref.shape
    tiles = modes_ref.shape[1] // 128
    rows = rows // tiles

    @pl.when(pl.program_id(0) == 0)
    def _():
        spread_weights(up_ref, down_ref, up_wide_ref, down_wide_ref)

    spectral = dot(phase_ref[...], modes_ref[...])
    size = tiles * lines
    pairs = rows // lines
    summed = [
        jnp.concatenate(
            [
                grid_ref[
                    pl.ds(source * pairs * size + line * tiles + tile, pairs, stride=size), :
                ]
                for source in range(group)
                for line in range(lines)
            ],
            axis=0,
        )
        + spectral[:, tile * 128 : (tile + 1) * 128]
        for tile in range(tiles)
    ]
    results = mlp(summed, up_wide_ref, down_wide_ref)
    for tile, result in enumerate(results):
        result = result.astype(BF16)
        for source in range(group):
            out_ref[source, tile * rows : (tile + 1) * rows, :] = result[
                source * rows : (source + 1) * rows, :
            ]


def last_layer(phases, modes, grid, up, down, number, devices, lines):
    count, columns = phases.shape
    lanes = modes.shape[1]
    tiles = lanes // 128
    group = 8
    rows = count // devices
    return pl.pallas_call(
        functools.partial(last_kernel, lines),
        out_shape=jax.ShapeDtypeStruct((devices, rows * tiles, 128), BF16),
        grid=(devices // group,),
        in_specs=[
            pl.BlockSpec((group * rows, columns), lambda i: (i, 0)),
            pl.BlockSpec((columns, lanes), lambda i: (0, 0)),
            pl.BlockSpec((group * rows * tiles, 128), lambda i: (i, 0)),
        ]
        + weight_specs(up, down, number),
        out_specs=pl.BlockSpec((group, rows * tiles, 128), lambda i: (i, 0, 0)),
        scratch_shapes=wide_weights(up),
        cost_estimate=cost(
            2 * count * columns * lanes + 16 * count * lanes * up.shape[2],
            count * (columns * 2 + lanes * 6),
        ),
        compiler_params=limit(24),
        name="last_layer",
    )(in_hbm(phases), modes, in_vmem(grid), up, down)


def exchange(values):
    return lax.all_to_all(values, "pen", split_axis=0, concat_axis=0, tiled=True)


def forward_pass(point_feat, pair_kernel, pair_owner, pair_block, spec_weight, mlp_up, mlp_down):
    devices = lax.axis_size("pen")
    pairs, block = pair_kernel.shape[0], pair_kernel.shape[1]
    channels = point_feat.shape[0]
    modes_here = spec_weight.shape[1]
    lines = block // NZ
    lanes = NZ // devices * channels
    tiles = lanes // 128
    columns = devices * 2 * MX

    up = mlp_up.transpose(0, 2, 1)
    send = encode(
        point_feat, pair_kernel, pair_owner.reshape(1, pairs), pair_block.reshape(1, pairs), devices
    )
    got = exchange(send)

    table, flipped = grid_tables(devices, modes_here)
    got, table, flipped = lax.optimization_barrier((got, table, flipped))
    forward, inverse = depth_tables(devices, modes_here)
    lookups = lookup_tables()
    here = got[:, -8:-6, 0:pairs].astype(jnp.int32)
    rows = ((here[:, 0, :] * NY + here[:, 1, :]) * tiles).reshape(devices * pairs)

    spectrum = pair_spectrum(got, lookups, modes_here, lanes)
    phases = pair_phases(got, lookups, modes_here, lanes)
    grid = scatter(rows, got, tiles)
    modes = exchange(spectrum.reshape(devices, 2 * MX, lanes)).reshape(columns, lanes)
    modes = mix(modes, forward, inverse, spec_weight, 0, devices)
    modes = exchange(modes.reshape(devices, 2 * MX, lanes)).reshape(columns, lanes)
    grid, spectrum = layer(table, flipped, modes, grid, up, mlp_down, 0)
    listed = gather(rows, grid.reshape(-1, 128), lines * tiles, devices)
    modes = exchange(spectrum.reshape(devices, 2 * MX, lanes)).reshape(columns, lanes)
    modes = mix(modes, forward, inverse, spec_weight, 1, devices)
    modes = exchange(modes.reshape(devices, 2 * MX, lanes)).reshape(columns, lanes)
    result = last_layer(phases, modes, listed, up, mlp_down, 1, devices, lines)
    return decode(exchange(result), pair_kernel, channels)


def solution(mesh):
    in_specs = (
        P(None, ("groups", "pen")),
        P(("groups", "pen"), None, None),
        P(("groups", "pen"), None),
        P(("groups", "pen")),
        P(None, "pen", None, None, None),
        P(),
        P(),
    )
    out_specs = P(None, ("groups", "pen"))
    return jax.shard_map(
        forward_pass, mesh=mesh, in_specs=in_specs, out_specs=out_specs, check_vma=False
    )
```
